32 devices in a mesh: grp: 2 (over y), row: 4 (over z), col: 2 (over x), rep: 2 (over core).
Axes of the slice: x: 2, y: 2, z: 4, core: 2. Of those that a mesh axis runs over, the one named last changes fastest.
Arguments:
- emb_row: bfloat16 [2048, 1280], P(('grp', 'row', 'rep'), 'col'), parts along dimension 0, may hold values from -6 to 6
- emb_col: bfloat16 [512, 1280], P(('grp', 'col'), 'row'), parts along dimension 0, may hold values from -6 to 6
- proj_row: bfloat16 [1280, 64], replicated, may hold values from -0.15625 to 0.15625
- proj_col: bfloat16 [1280, 64], replicated, may hold values from -0.15625 to 0.15625
- pair_out: bfloat16 [64, 64], replicated, may hold values from -0.75 to 0.75
- pair_bias: float32 [64], replicated, may hold values from -3 to 3
- conv_weight: bfloat16 [3, 3, 64, 64], replicated, may hold values from -0.25 to 0.25
- conv_bias: float32 [64], replicated, may hold values from -3 to 3
- target: bfloat16 [64, 2048, 256], P(None, ('grp', 'row', 'rep'), 'col'), parts along dimension 1, may hold values from -6 to 6
- kept_tiles: int32 [16, 2], P(('grp', 'row', 'rep'), 'col'), parts along dimension 0, may hold values 0 or 1
Outputs:
- cell_loss: float32 [2048, 256], P(('grp', 'row', 'rep'), 'col'), parts along dimension 0
- grad_conv: float32 [6, 3, 64, 64], P('grp'), parts along dimension 0
- grad_bias: float32 [128], P('grp'), parts along dimension 0
The draws below stay inside these ranges and needn't reach their ends.
There are 2 independent parts, one for each index of `grp`. The reference program is written for one: setup_inputs(seed, part) draws one part's arguments, and reference() takes and returns one part's arrays. A program takes and returns all parts, laid end to end along the dimension named above; an argument that names none is the same for every part. Nothing has to cross between parts.
All inputs are finite; a program needn't handle non-finite values. No bound on the sum of `kept_tiles` on one device may be relied on, other than what follows from the above.
Results may differ from the reference program's by a relative error of at most 0.0025.
Values may be sent and summed in bfloat16 or wider, within the bound.
A program may use at most 128 MiB of HBM per device.

```python
import jax
import jax.numpy as jnp
from jax import lax

EMBED = 1280
RANK = 64
CHANNELS = 64
TILE_EDGE = 128
ROWS_ALL = 1024
COLS_ALL = 256
TILE_ROWS = 8
TILE_COLS = 2


def touch_ends(result, rng, least, high):
    index_at = [jax.random.randint(jax.random.fold_in(rng, axis), (), 0, length) for axis, length in enumerate(result.shape)]
    widest = result.shape.index(max(result.shape))
    next_to = index_at[:widest] + [(index_at[widest] + 1) % result.shape[widest]] + index_at[widest + 1:]
    return result.at[tuple(index_at)].set(least).at[tuple(next_to)].set(high)


def block_scale(own_key, shape, pieces, least, largest):
    def one(dim, shards_of):
        draws = jax.random.uniform(jax.random.fold_in(jax.random.fold_in(own_key, 6), dim), (shards_of,), jnp.float32, least / len(pieces), largest / len(pieces))
        return jnp.repeat(jnp.exp(draws), shape[dim] // shards_of).reshape((-1,) + (1,) * (len(shape) - dim - 1))

    gain = one(*pieces[0])
    for cut in pieces[1:]:
        gain = gain * one(*cut)
    return gain


def centred(key, extent, scale, bound, cuts=(), held_as=jnp.bfloat16):
    values = jax.random.normal(key, extent, jnp.float32) * scale
    if len(cuts) > 0:
        values = block_scale(key, extent, cuts, -0.22, 0.18) * values
    return jnp.clip(values, min=-bound, max=bound).astype(held_as)


def setup_inputs(seed: int = 0, part: int = 0) -> dict:
    key_list = jax.random.split(jax.random.key(seed), 11)
    own_keys = jax.random.split(jax.random.fold_in(key_list[10], part), 11)
    return {
        "emb_row": centred(own_keys[0], (ROWS_ALL, EMBED), 1.0, 6.0, ((0, 8), (1, 2))),
        "emb_col": centred(own_keys[1], (COLS_ALL, EMBED), 1.0, 6.0, ((0, 2), (1, 4))),
        "proj_row": centred(key_list[2], (EMBED, RANK), EMBED ** -0.5, 0.15625),
        "proj_col": centred(key_list[3], (EMBED, RANK), EMBED ** -0.5, 0.15625),
        "pair_out": centred(key_list[4], (RANK, CHANNELS), RANK ** -0.5, 0.75),
        "pair_bias": centred(key_list[5], (CHANNELS,), 0.5, 3.0, (), jnp.float32),
        "conv_weight": centred(key_list[6], (3, 3, CHANNELS, CHANNELS), (9 * CHANNELS) ** -0.5, 0.25),
        "conv_bias": centred(key_list[7], (CHANNELS,), 0.5, 3.0, (), jnp.float32),
        "target": centred(own_keys[8], (CHANNELS, ROWS_ALL, COLS_ALL), 1.0, 6.0, ((1, 8), (2, 2))),
        "kept_tiles": touch_ends((jax.random.randint(own_keys[9], (TILE_ROWS, TILE_COLS), 0, 4) < 3).astype(jnp.int32), jax.random.fold_in(own_keys[9], 1), 0, 1),
    }


def expand_tiles(tiles, edge):
    count_r, count_c = tiles.shape
    wide = jnp.broadcast_to(tiles.astype(jnp.float32)[:, None, :, None], (count_r, edge, count_c, edge))
    return wide.reshape(count_r * edge, count_c * edge)


def block_terms(padded, pair_feat, target_part, mask, conv_weight, conv_bias):
    rows = pair_feat.shape[1]
    width = pair_feat.shape[2]
    conv_out = jnp.broadcast_to(conv_bias[:, None, None], pair_feat.shape)
    for row_tap in range(3):
        for col_tap in range(3):
            window = padded[:, 2 * row_tap:2 * row_tap + rows, 2 * col_tap:2 * col_tap + width].astype(jnp.float32)
            conv_out = conv_out + jnp.einsum("co,cij->oij", conv_weight[row_tap, col_tap].astype(jnp.float32), window)
    differ = mask[None] * (pair_feat + conv_out - target_part.astype(jnp.float32))
    loss_part = 0.5 * jnp.sum(differ * differ, axis=0)
    grad_in = differ.astype(jnp.bfloat16).astype(jnp.float32)
    taps = []
    for row_tap in range(3):
        for col_tap in range(3):
            window = padded[:, 2 * row_tap:2 * row_tap + rows, 2 * col_tap:2 * col_tap + width].astype(jnp.float32)
            taps.append(jnp.einsum("cij,oij->co", window, grad_in))
    grads = jnp.stack(taps).reshape(3, 3, pair_feat.shape[0], pair_feat.shape[0])
    return loss_part, grads, jnp.sum(differ, axis=(1, 2))


def reference(emb_row, emb_col, proj_row, proj_col, pair_out, pair_bias, conv_weight, conv_bias, target, kept_tiles):
    row_feat = jnp.dot(emb_row, proj_row, preferred_element_type=jnp.float32).astype(jnp.bfloat16)
    col_feat = jnp.dot(emb_col, proj_col, preferred_element_type=jnp.float32).astype(jnp.bfloat16)
    mask = expand_tiles(kept_tiles, TILE_EDGE)
    row_pad = jnp.pad(row_feat, ((2, 2), (0, 0)))
    mask_pad = jnp.pad(mask, ((2, 2), (0, 0)))
    col_wide = col_feat.astype(jnp.float32)
    out_wide = pair_out.astype(jnp.float32)

    def one_block(index):
        start = (index * TILE_EDGE).astype(jnp.int32)
        feats = lax.dynamic_slice_in_dim(row_pad, start, TILE_EDGE + 4, 0)
        mask_rows = lax.dynamic_slice_in_dim(mask_pad, start, TILE_EDGE + 4, 0)
        scaled = (out_wide.T[:, :, None] * feats.astype(jnp.float32).T[None, :, :]).astype(jnp.bfloat16)
        feat_ext = jnp.einsum("cki,jk->cij", scaled.astype(jnp.float32), col_wide) + pair_bias[:, None, None]
        hidden = (jnp.maximum(feat_ext, 0.0) * mask_rows[None]).astype(jnp.bfloat16)
        padded = jnp.pad(hidden, ((0, 0), (0, 0), (2, 2)))
        pair_feat = feat_ext[:, 2:TILE_EDGE + 2]
        mask_here = mask_rows[2:TILE_EDGE + 2]
        target_part = lax.dynamic_slice_in_dim(target, start, TILE_EDGE, 1)
        return block_terms(padded, pair_feat, target_part, mask_here, conv_weight, conv_bias)

    losses, grads, biases = lax.map(one_block, jnp.arange(ROWS_ALL // TILE_EDGE).astype(jnp.int32))
    norm = 1.0 / (TILE_EDGE * TILE_EDGE)
    cell_loss = losses.reshape(ROWS_ALL, COLS_ALL)
    return cell_loss, jnp.sum(grads, axis=0) * norm, jnp.sum(biases, axis=0) * norm
```

```python
import functools

import jax
import jax.numpy as jnp
from jax import lax
from jax.experimental import pallas as pl
from jax.experimental.pallas import tpu as pltpu
from jax.sharding import PartitionSpec as P

MESH = pl.DeviceIdType.MESH
F32 = jnp.float32
BF16 = jnp.bfloat16
NT = (((1,), (1,)), ((), ()))


def loop(low, high, body):
    if high - low <= 16:
        for d in range(low, high):
            body(d)
    else:
        lax.fori_loop(low, high, lambda d, _: (body(d), 0)[1], 0)


def columns(ref, width, index, count):
    everything = ref.shape[1]
    if width % 128 == 0:
        return ref[:, pl.ds(pl.multiple_of(index * width, 128), width)]
    offset = max(i * width % 128 for i in range(count))
    window = min(-(-(offset + width) // 128) * 128, everything)
    tile = index * width // 128
    if any(i * width // 128 * 128 + window > everything for i in range(count)):
        tile = jnp.minimum(tile, (everything - window) // 128)
    value = ref[:, pl.ds(pl.multiple_of(tile * 128, 128), window)].astype(F32)
    shift = window - (index * width - tile * 128)
    return pltpu.roll(value, shift % window, 1)[:, 0:width].astype(BF16)


def kernel(
    sizes,
    emb_row_hbm,
    emb_col_hbm,
    proj_row_hbm,
    proj_col_hbm,
    pair_out_hbm,
    pair_bias_hbm,
    conv_weight_hbm,
    conv_bias_hbm,
    target,
    kept,
    loss_out,
    full,
    emb_row,
    emb_col,
    proj_row,
    proj_col,
    conv_weight,
    pair_out,
    pair_bias,
    conv_bias,
    in_sem,
    rowtail,
    coltail,
    rowbuf,
    rowedge,
    colbuf,
    coledge,
    row_feat,
    col_wide,
    wide_t,
    target_in,
    target32,
    hid,
    base,
    grad_in,
    weight_f,
    total,
    bias_acc,
    part,
    reduced,
    whole,
    target_sem,
    row_send,
    row_recv,
    redge_send,
    redge_recv,
    col_send,
    col_recv,
    cedge_send,
    cedge_recv,
    rs_send,
    rs_recv,
    ag_send,
    ag_recv,
):
    n_row, n_col, n_rep, edge, chan, n_own, first_own, chunk = sizes
    n_all = n_row * n_col * n_rep
    pairs = edge // 2
    row, col, rep = lax.axis_index("row"), lax.axis_index("col"), lax.axis_index("rep")
    line = row * n_rep + rep
    n_line = n_row * n_rep
    me = line * n_col + col

    def device(index):
        across = lax.rem(index, n_col)
        along = lax.div(index, n_col)
        return {"row": lax.div(along, n_rep), "rep": lax.rem(along, n_rep), "col": across}

    def await_bytes(ref, sem):
        pltpu.make_async_copy(ref, ref, sem).wait()

    barrier = pltpu.get_barrier_semaphore()
    loop(
        1,
        n_all,
        lambda d: pl.semaphore_signal(
            barrier, inc=1, device_id=device(lax.rem(me + d, n_all)), device_id_type=MESH
        ),
    )

    inputs = [
        pltpu.make_async_copy(src, dst, in_sem.at[i])
        for i, (src, dst) in enumerate(
            (
                (emb_row_hbm, emb_row),
                (proj_row_hbm, proj_row),
                (emb_col_hbm, emb_col),
                (proj_col_hbm, proj_col),
                (conv_weight_hbm, conv_weight),
                (pair_out_hbm, pair_out),
                (pair_bias_hbm, pair_bias),
                (conv_bias_hbm, conv_bias),
            )
        )
    ]
    for copy in inputs:
        copy.start()
    fetch = pltpu.make_async_copy(target, target_in, target_sem)
    fetch.start()

    def rounded(x):
        return x.astype(BF16).astype(F32)

    for copy in inputs[2:4]:
        copy.wait()
    part_col = jnp.dot(
        columns(proj_col, emb_col.shape[0], row, n_row),
        emb_col[...],
        preferred_element_type=F32,
    )
    for copy in inputs[0:2]:
        copy.wait()
    keep = kept[0, 0].astype(F32)
    part_row = lax.dot_general(
        columns(proj_row, emb_row.shape[1], col, n_col),
        emb_row[...],
        NT,
        preferred_element_type=F32,
    )
    rank = part_row.shape[0]
    colbuf[row] = part_col.astype(BF16)
    rowbuf[col, 0:rank, :] = part_row.astype(BF16)
    rowbuf[col, rank:, :] = jnp.full((16, edge), keep, F32).astype(BF16)
    turned = rounded(part_col).T
    coltail[0] = turned[edge - 8 :]
    coltail[1] = turned[0:8]
    turned = rounded(part_row).T
    rowtail[0, 0:8] = turned[edge - 8 :]
    rowtail[1, 0:8] = turned[0:8]
    for side in range(2):
        rowtail[side, 8:16] = jnp.full((8, rank), keep, F32)

    pl.semaphore_wait(barrier, n_all - 1)

    def row_copy(d, src):
        return pltpu.make_async_remote_copy(
            src_ref=rowbuf.at[src],
            dst_ref=rowbuf.at[src],
            send_sem=row_send,
            recv_sem=row_recv,
            device_id={"col": lax.rem(col + d, n_col)},
            device_id_type=MESH,
        )

    def redge_copy(side, d, src):
        to = lax.rem(line + (1 if side == 0 else n_line - 1), n_line)
        return pltpu.make_async_remote_copy(
            src_ref=rowtail.at[side],
            dst_ref=rowedge.at[side, src],
            send_sem=redge_send,
            recv_sem=redge_recv,
            device_id={
                "row": lax.div(to, n_rep),
                "rep": lax.rem(to, n_rep),
                "col": lax.rem(col + d, n_col),
            },
            device_id_type=MESH,
        )

    def col_copy(d, src):
        return pltpu.make_async_remote_copy(
            src_ref=colbuf.at[src],
            dst_ref=colbuf.at[src],
            send_sem=col_send,
            recv_sem=col_recv,
            device_id={"row": lax.rem(row + d, n_row)},
            device_id_type=MESH,
        )

    def cedge_copy(side, d, src):
        to = lax.rem(col + (1 if side == 0 else n_col - 1), n_col)
        return pltpu.make_async_remote_copy(
            src_ref=coltail.at[side],
            dst_ref=coledge.at[side, src],
            send_sem=cedge_send,
            recv_sem=cedge_recv,
            device_id={"row": lax.rem(row + d, n_row), "col": to},
            device_id_type=MESH,
        )

    for side in range(2):
        loop(0, n_row, lambda d: cedge_copy(side, d, row).start())
    loop(1, n_row, lambda d: col_copy(d, row).start())
    for side in range(2):
        loop(0, n_col, lambda d: redge_copy(side, d, col).start())
    loop(1, n_col, lambda d: row_copy(d, col).start())

    def await_features(col_sem, row_sem, cedge_sem, redge_sem):
        await_bytes(coledge, cedge_sem)
        if n_row > 1:
            await_bytes(colbuf.at[0 : n_row - 1], col_sem)
        await_bytes(rowedge, redge_sem)
        if n_col > 1:
            await_bytes(rowbuf.at[0 : n_col - 1], row_sem)

    fetch.wait()
    for copy in inputs[4:]:
        copy.wait()

    def widen(c, _):
        start = pl.multiple_of(c * edge, edge)
        target32[pl.ds(start, edge), :] = target_in[c].astype(F32)
        return 0

    lax.fori_loop(0, chan, widen, 0, unroll=4)
    for a in range(3):
        for b in range(3):
            weight_f[b * chan : (b + 1) * chan, a * chan : (a + 1) * chan] = conv_weight[
                a, b
            ].astype(F32)
    weight_t = weight_f[...].T.astype(BF16)
    out_t = pair_out[...].astype(F32).T
    pair_b = jnp.broadcast_to(pair_bias[...], (128, chan)).T
    conv_b = jnp.broadcast_to(conv_bias[...], (128, chan)).T
    zeros = jnp.zeros((2 * chan, 2 * edge), BF16)
    grad_in[0 : 2 * chan, :] = zeros
    grad_in[(pairs + 2) * chan : (pairs + 4) * chan, :] = zeros
    base[0 : 2 * chan, :] = zeros.astype(F32)
    base[(pairs + 2) * chan : (pairs + 4) * chan, :] = zeros.astype(F32)
    bias_acc[...] = jnp.zeros_like(bias_acc)
    total[...] = jnp.zeros_like(total)

    await_features(col_recv, row_recv, cedge_recv, redge_recv)

    def summed(terms):
        return sum(x.astype(F32) for x in terms)

    row_feat[0:8, :] = rounded(summed(rowedge[0, c, 0:8, :] for c in range(n_col)))
    row_feat[8 : edge + 8, :] = rounded(summed(rowbuf[c, 0:rank, :] for c in range(n_col))).T
    row_feat[edge + 8 :, :] = rounded(summed(rowedge[1, c, 0:8, :] for c in range(n_col)))
    col_wide[0:8, :] = summed(coledge[0, r] for r in range(n_row))
    col_wide[8 : edge + 8, :] = summed(colbuf[r] for r in range(n_row)).T
    col_wide[edge + 8 :, :] = summed(coledge[1, r] for r in range(n_row))
    for b in range(3):
        wide_t[b * edge : (b + 1) * edge, :] = col_wide[
            6 + 2 * b : 6 + 2 * b + edge, :
        ].astype(BF16)

    lane = lax.broadcasted_iota(jnp.int32, (1, edge), 1)
    before, after = (col + n_col - 1) % n_col, (col + 1) % n_col
    has_before = (col > 0).astype(F32)
    has_after = (col < n_col - 1).astype(F32)

    def masks(get, valid):
        here, left, right = (
            jnp.broadcast_to(get(c), (1, edge)) * scale
            for c, scale in ((col, valid), (before, valid * has_before), (after, valid * has_after))
        )
        return (jnp.where(lane < 2, left, here), here, jnp.where(lane >= edge - 2, right, here))

    top = masks(lambda c: rowedge[0, c, 8:9, 0:1], (line > 0).astype(F32))
    middle = masks(lambda c: rowbuf[c, rank:, 0:1].astype(F32)[0:1], jnp.float32(1))
    bottom = masks(lambda c: rowedge[1, c, 8:9, 0:1], (line < n_line - 1).astype(F32))

    def features(pair, count, mask, inner):
        scaled = []
        for r in range(2 * count):
            feat = row_feat[pl.ds(2 * pair + 8 + r, 1), :]
            scaled.append((out_t * feat).astype(BF16))
        product = lax.dot_general(
            jnp.concatenate(scaled, axis=0), wide_t[...], NT, preferred_element_type=F32
        )
        for r in range(2 * count):
            p = pair + r // 2
            lanes = slice((r % 2) * edge, (r % 2 + 1) * edge)
            for b in range(3):
                value = product[r * chan : (r + 1) * chan, b * edge : (b + 1) * edge] + pair_b
                start = pl.multiple_of((p + 1) * 3 * chan + b * chan, chan)
                hid[pl.ds(start, chan), lanes] = (jnp.maximum(value, 0.0) * mask[b]).astype(BF16)
                if inner and b == 1:
                    aim = target32[pl.ds(2 * pair + r, chan, stride=edge), :]
                    start = pl.multiple_of((p + 2) * chan, chan)
                    base[pl.ds(start, chan), lanes] = (value + conv_b) - aim

    features(-1, 1, top, False)
    features(pairs, 1, bottom, False)
    group = 4

    def conv_of(p):
        start = pl.multiple_of((p + 1) * 3 * chan, 3 * chan)
        return jnp.dot(weight_t, hid[pl.ds(start, 3 * chan), :], preferred_element_type=F32)

    def slot(p):
        return pl.ds(pl.multiple_of((p + 2) * chan, chan), chan)

    def spread(p, done):
        y = conv_of(p)
        base[slot(p + 1), :] += y[0:chan]
        base[slot(p), :] += y[chan : 2 * chan]
        if done:
            differ = (base[slot(p - 1), :] + y[2 * chan :]) * keep
            grad_in[slot(p - 1), :] = differ.astype(BF16)
            bias_acc[...] += differ
            loss = 0.5 * jnp.sum(differ * differ, axis=0, keepdims=True)
            loss_out[pl.ds(2 * (p - 1), 1), :] = loss[:, 0:edge]
            loss_out[pl.ds(2 * (p - 1) + 1, 1), :] = loss[:, edge : 2 * edge]

    def grads(first, count):
        value = total[...]
        for r in range(count):
            p = first + r
            start = pl.multiple_of((p + 1) * 3 * chan, 3 * chan)
            near = pl.multiple_of((p + 1) * chan, chan)
            value = value + lax.dot_general(
                hid[pl.ds(start, 3 * chan), :],
                grad_in[pl.ds(near, 3 * chan), :],
                NT,
                preferred_element_type=F32,
            )
        total[...] = value

    for g in range(3):
        features(g * group, group, middle, True)
    spread(-1, False)
    spread(0, False)
    for r in range(group):
        spread(1 + r, True)
    lag = 2 * group - 1

    def step(g, _):
        grads(g * group - 3 * group - 1, group)
        for r in range(group):
            spread(g * group - lag + r, True)
        features(g * group, group, middle, True)
        return 0

    lax.fori_loop(3, pairs // group, step, 0)

    def conv_step(g, _):
        for r in range(group):
            spread(pairs - lag + g * group + r, True)
        return 0

    lax.fori_loop(0, 2, conv_step, 0)

    def grad_step(g, _):
        grads(pairs - 3 * group - 1 + g * 7, 7)
        return 0

    lax.fori_loop(0, 2, grad_step, 0)

    norm = 1.0 / (edge * edge)
    half = 3 * chan // 2
    rows = 3 * chan + half
    sums = total[...] * norm
    flat = jnp.concatenate(
        [
            sums[:, 0 : 2 * chan],
            jnp.concatenate([sums[0:half, 2 * chan :], sums[half:, 2 * chan :]], axis=1),
        ],
        axis=0,
    )
    bias_sum = lax.dot_general(
        jnp.ones((8, 2 * edge), F32),
        bias_acc[...] * norm,
        NT,
        precision=lax.Precision.HIGHEST,
        preferred_element_type=F32,
    )
    part[0:rows, :] = flat
    for term in range(3):
        low = rows + 8 * term
        part[low : low + 8, :] = jnp.concatenate([bias_sum, bias_sum], axis=1)
    rest = n_own * chunk - rows - 24
    if rest > 0:
        part[rows + 24 :, :] = jnp.zeros((rest, 128), F32)

    mine = me - first_own
    owner = (mine >= 0) & (mine < n_own)

    def piece(index):
        return pl.ds(pl.multiple_of(index * chunk, 8), chunk)

    def scatter(d):
        index = lax.rem(me + d, n_own)

        @pl.when(first_own + index != me)
        def _():
            pltpu.make_async_remote_copy(
                src_ref=part.at[piece(index)],
                dst_ref=reduced.at[me],
                send_sem=rs_send,
                recv_sem=rs_recv,
                device_id=device(first_own + index),
                device_id_type=MESH,
            ).start()

    def gather(d):
        pltpu.make_async_remote_copy(
            src_ref=full.at[mine],
            dst_ref=full.at[mine],
            send_sem=ag_send,
            recv_sem=ag_recv,
            device_id=device(lax.rem(me + d, n_all)),
            device_id_type=MESH,
        ).start()

    loop(0, n_own, scatter)

    @pl.when(owner)
    def _():
        reduced[me] = part[piece(mine), :]
        await_bytes(reduced.at[0 : n_all - 1], rs_recv)
        if n_all <= 16:
            own = sum(reduced[r] for r in range(n_all))
        else:
            own = lax.fori_loop(
                0, n_all, lambda r, x: x + reduced[r], jnp.zeros((chunk, 128), F32)
            )
        at = mine * chunk + lax.broadcasted_iota(jnp.int32, (chunk, 128), 0)
        second = own - rounded(own)
        third = second - rounded(second)
        own = jnp.where(at >= rows + 8, jnp.where(at >= rows + 16, third, second), own)
        full[mine] = own.astype(BF16)
        loop(1, n_all, gather)
        if n_own > 1:
            await_bytes(full.at[0 : n_own - 1], ag_recv)
            await_bytes(part.at[0 : (n_own - 1) * chunk], rs_send)

    @pl.when(jnp.logical_not(owner))
    def _():
        await_bytes(full, ag_recv)
        await_bytes(part, rs_send)

    await_features(col_send, row_send, cedge_send, redge_send)

    @pl.when(owner)
    def _():
        await_bytes(whole, ag_send)


def finish(loss, gathered, loss_hbm, conv_grad_hbm, bias_hbm, full, conv_grad_out, bias_out, sem):
    n_all, chunk = gathered.shape[0:2]
    loss_copy = pltpu.make_async_copy(loss, loss_hbm, sem.at[0])
    loss_copy.start()

    def place(r):
        full[pl.ds(r * chunk, chunk), :] = gathered[r].astype(F32)

    loop(0, n_all, place)
    chan = bias_out.shape[1]
    half = 3 * chan // 2
    rows = 3 * chan + half
    for b in range(3):
        low = b * chan
        conv_grad_out[2, b] = full[low : low + chan, 0:chan]
        conv_grad_out[1, b] = full[low : low + chan, chan : 2 * chan]
    low = 3 * chan
    conv_grad_out[0, 0] = full[low : low + chan, 0:chan]
    conv_grad_out[0, 1, 0 : half - chan] = full[low + chan : low + half, 0:chan]
    conv_grad_out[0, 1, half - chan :] = full[low : low + 2 * chan - half, chan : 2 * chan]
    conv_grad_out[0, 2] = full[low + 2 * chan - half : low + half, chan : 2 * chan]
    bias_out[...] = sum(full[rows + 8 * t : rows + 8 * t + 1, 0:chan] for t in range(3))
    grad_copy = pltpu.make_async_copy(conv_grad_out, conv_grad_hbm, sem.at[1])
    bias_copy = pltpu.make_async_copy(bias_out, bias_hbm, sem.at[2])
    grad_copy.start()
    bias_copy.start()
    loss_copy.wait()
    grad_copy.wait()
    bias_copy.wait()


def solution(mesh):
    n_row, n_col, n_rep = (mesh.shape[axis] for axis in ("row", "col", "rep"))
    n_all = n_row * n_col * n_rep

    def per_device(
        emb_row,
        emb_col,
        proj_row,
        proj_col,
        pair_out,
        pair_bias,
        conv_weight,
        conv_bias,
        target,
        kept_tiles,
    ):
        chan, edge = target.shape[0], target.shape[1]
        rank = pair_out.shape[0]
        pairs = edge // 2
        used = 3 * chan + 3 * chan // 2 + 24
        inner = n_row // 2 if n_row >= 4 else n_row
        n_own = inner * n_col * n_rep
        first_own = (n_row - inner) // 2 * n_col * n_rep
        chunk = 8 * pl.cdiv(used, 8 * n_own)

        dma = pltpu.SemaphoreType.DMA
        vmem = pl.BlockSpec(memory_space=pltpu.VMEM)
        hbm = pl.BlockSpec(memory_space=pltpu.HBM)
        loss, sums = pl.pallas_call(
            functools.partial(
                kernel, (n_row, n_col, n_rep, edge, chan, n_own, first_own, chunk)
            ),
            out_shape=(
                pltpu.VMEM((edge, edge), F32),
                pltpu.VMEM((n_own, chunk, 128), BF16),
            ),
            in_specs=[hbm] * 9 + [pl.BlockSpec(memory_space=pltpu.SMEM)],
            out_specs=(vmem,) * 2,
            scratch_shapes=[
                pltpu.VMEM(emb_row.shape, BF16),
                pltpu.VMEM(emb_col.shape[::-1], BF16),
                pltpu.VMEM(proj_row.shape[::-1], BF16),
                pltpu.VMEM(proj_col.shape[::-1], BF16),
                pltpu.VMEM(conv_weight.shape, BF16),
                pltpu.VMEM(pair_out.shape, BF16),
                pltpu.VMEM((1, chan), F32),
                pltpu.VMEM((1, chan), F32),
                dma((8,)),
                pltpu.VMEM((2, 16, rank), F32),
                pltpu.VMEM((2, 8, rank), F32),
                pltpu.VMEM((n_col, rank + 16, edge), BF16),
                pltpu.VMEM((2, n_col, 16, rank), F32),
                pltpu.VMEM((n_row, rank, edge), BF16),
                pltpu.VMEM((2, n_row, 8, rank), F32),
                pltpu.VMEM((edge + 16, rank), F32),
                pltpu.VMEM((edge + 16, rank), F32),
                pltpu.VMEM((3 * edge, rank), BF16),
                pltpu.VMEM((chan, edge, edge), BF16),
                pltpu.VMEM((chan * edge, edge), F32),
                pltpu.VMEM(((pairs + 2) * 3 * chan, 2 * edge), BF16),
                pltpu.VMEM(((pairs + 4) * chan, 2 * edge), F32),
                pltpu.VMEM(((pairs + 4) * chan, 2 * edge), BF16),
                pltpu.VMEM((3 * chan, 3 * chan), F32),
                pltpu.VMEM((3 * chan, 3 * chan), F32),
                pltpu.VMEM((chan, 2 * edge), F32),
                pltpu.VMEM((n_own * chunk, 128), F32),
                pltpu.VMEM((n_all, chunk, 128), F32),
                pltpu.VMEM((n_all - 1, chunk, 128), BF16),
                *[pltpu.SemaphoreType.DMA] * 13,
            ],
            compiler_params=pltpu.CompilerParams(collective_id=0, has_side_effects=True),
            name="pair_step",
        )(
            emb_row,
            emb_col.T,
            proj_row.T,
            proj_col.T,
            pair_out,
            pair_bias.reshape(1, chan),
            conv_weight,
            conv_bias.reshape(1, chan),
            target,
            kept_tiles,
        )
        loss, grads, bias = pl.pallas_call(
            finish,
            out_shape=(
                jax.ShapeDtypeStruct((edge, edge), F32),
                jax.ShapeDtypeStruct((3, 3, chan, chan), F32),
                jax.ShapeDtypeStruct((1, chan), F32),
            ),
            in_specs=[vmem] * 2,
            out_specs=(hbm,) * 3,
            scratch_shapes=[
                pltpu.VMEM((n_own * chunk, 128), F32),
                pltpu.VMEM((3, 3, chan, chan), F32),
                pltpu.VMEM((1, chan), F32),
                dma((3,)),
            ],
            name="finish",
        )(
            *(pltpu.with_memory_space_constraint(x, pltpu.VMEM) for x in (loss, sums))
        )
        return loss, grads, bias.reshape(chan)

    in_specs = (
        P(("grp", "row", "rep"), "col"),
        P(("grp", "col"), "row"),
        P(),
        P(),
        P(),
        P(),
        P(),
        P(),
        P(None, ("grp", "row", "rep"), "col"),
        P(("grp", "row", "rep"), "col"),
    )
    out_specs = (P(("grp", "row", "rep"), "col"), P("grp", None, None, None), P("grp"))
    return jax.shard_map(
        per_device, mesh=mesh, in_specs=in_specs, out_specs=out_specs, check_vma=False
    )
```

```python
import functools

import jax
import jax.numpy as jnp
from jax import lax
from jax.experimental import pallas as pl
from jax.experimental.pallas import tpu as pltpu
from jax.sharding import PartitionSpec as P

MESH = pl.DeviceIdType.MESH
F32 = jnp.float32
BF16 = jnp.bfloat16
NT = (((1,), (1,)), ((), ()))


def loop(low, high, body):
    if high - low <= 16:
        for d in range(low, high):
            body(d)
    else:
        lax.fori_loop(low, high, lambda d, _: (body(d), 0)[1], 0)


def columns(ref, width, index, count):
    everything = ref.shape[1]
    if width % 128 == 0:
        return ref[:, pl.ds(pl.multiple_of(index * width, 128), width)]
    offset = max(i * width % 128 for i in range(count))
    window = min(-(-(offset + width) // 128) * 128, everything)
    tile = index * width // 128
    if any(i * width // 128 * 128 + window > everything for i in range(count)):
        tile = jnp.minimum(tile, (everything - window) // 128)
    value = ref[:, pl.ds(pl.multiple_of(tile * 128, 128), window)].astype(F32)
    shift = window - (index * width - tile * 128)
    value = pltpu.roll(value, lax.rem(shift, window), 1)
    lane = lax.broadcasted_iota(jnp.int32, value.shape, 1)
    return jnp.where(lane < width, value, 0.0).astype(BF16)


def padded(value, square):
    if all(have == 256 or have % 128 == 0 for have in value.shape):
        for axis in range(2):
            if value.shape[axis] < 256:
                blank = list(value.shape)
                blank[axis] = 256 - blank[axis]
                value = jnp.concatenate([value, jnp.zeros(blank, BF16)], axis=axis)
        return value
    square[...] = jnp.zeros_like(square)
    square[0 : value.shape[0], 0 : value.shape[1]] = value
    return square[...]


def wide_tile(value, low):
    value = value[:, low : low + 256]
    if value.shape[1] < 256:
        blank = jnp.zeros((value.shape[0], 256 - value.shape[1]), BF16)
        value = jnp.concatenate([value, blank], axis=1)
    return value


def kernel(
    sizes,
    emb_row_hbm,
    emb_col_hbm,
    proj_row_hbm,
    proj_col_hbm,
    pair_out_hbm,
    pair_bias_hbm,
    conv_weight_hbm,
    conv_bias_hbm,
    target,
    kept,
    loss_out,
    full,
    emb_row,
    emb_col,
    proj_row,
    proj_col,
    conv_weight,
    pair_out,
    pair_bias,
    conv_bias,
    in_sem,
    rowtail,
    coltail,
    rowbuf,
    rowedge,
    colbuf,
    coledge,
    row_feat,
    col_wide,
    feat_pairs,
    square,
    wide,
    weight_t,
    target_in,
    target32,
    aims,
    hid,
    base,
    grad_in,
    weight_f,
    total,
    bias_acc,
    part,
    reduced,
    whole,
    target_sem,
    row_send,
    row_recv,
    redge_send,
    redge_recv,
    col_send,
    col_recv,
    cedge_send,
    cedge_recv,
    rs_send,
    rs_recv,
    ag_send,
    ag_recv,
):
    n_row, n_col, n_rep, edge, chan, n_own, first_own, chunk = sizes
    n_all = n_row * n_col * n_rep
    pairs = edge // 2
    row, col, rep = lax.axis_index("row"), lax.axis_index("col"), lax.axis_index("rep")
    line = row * n_rep + rep
    n_line = n_row * n_rep
    me = line * n_col + col

    def device(index):
        across = lax.rem(index, n_col)
        along = lax.div(index, n_col)
        return {"row": lax.div(along, n_rep), "rep": lax.rem(along, n_rep), "col": across}

    def await_bytes(ref, sem):
        pltpu.make_async_copy(ref, ref, sem).wait()

    barrier = pltpu.get_barrier_semaphore()
    loop(
        1,
        n_all,
        lambda d: pl.semaphore_signal(
            barrier, inc=1, device_id=device(lax.rem(me + d, n_all)), device_id_type=MESH
        ),
    )

    inputs = [
        pltpu.make_async_copy(src, dst, in_sem.at[i])
        for i, (src, dst) in enumerate(
            (
                (emb_row_hbm, emb_row),
                (proj_row_hbm, proj_row),
                (emb_col_hbm, emb_col),
                (proj_col_hbm, proj_col),
                (conv_weight_hbm, conv_weight),
                (pair_out_hbm, pair_out),
                (pair_bias_hbm, pair_bias),
                (conv_bias_hbm, conv_bias),
            )
        )
    ]
    for copy in inputs:
        copy.start()
    fetch = pltpu.make_async_copy(target, target_in, target_sem)
    fetch.start()

    def rounded(x):
        return x.astype(BF16).astype(F32)

    for copy in inputs[2:4]:
        copy.wait()
    rank = proj_row.shape[0]

    def project(col_sum, row_sum):
        width = emb_col.shape[0]
        left = columns(proj_col, width, row, n_row)
        for low in range(0, width, 256):
            right = padded(emb_col[low : min(low + 256, width), :], square)
            pltpu.matmul_push_rhs(right, 0, 0)
            pltpu.matmul_acc_lhs(col_sum, wide_tile(left, low), load_staged_rhs=0)
        for copy in inputs[0:2]:
            copy.wait()
        width = emb_row.shape[1]
        left = columns(proj_row, width, col, n_col)
        for low in range(0, width, 256):
            right = padded(emb_row[:, low : min(low + 256, width)], square)
            pltpu.matmul_push_rhs(right, 0, 1, transpose=True)
            pltpu.matmul_acc_lhs(row_sum, wide_tile(left, low), load_staged_rhs=0)
        return pltpu.matmul_pop(col_sum)[:, 0:edge], pltpu.matmul_pop(row_sum)[:, 0:edge]

    part_col, part_row = pl.run_scoped(
        project, *[pltpu.ACC(unit)((rank, 256), F32) for unit in range(2)]
    )
    keep = kept[0, 0].astype(F32)
    colbuf[row] = part_col.astype(BF16)
    rowbuf[col, 0:rank, :] = part_row.astype(BF16)
    rowbuf[col, rank:, :] = jnp.full((16, edge), keep, F32).astype(BF16)
    turned = rounded(part_col).T
    coltail[0] = turned[edge - 8 :]
    coltail[1] = turned[0:8]
    turned = rounded(part_row).T
    rowtail[0, 0:8] = turned[edge - 8 :]
    rowtail[1, 0:8] = turned[0:8]
    for side in range(2):
        rowtail[side, 8:16] = jnp.full((8, rank), keep, F32)

    pl.semaphore_wait(barrier, n_all - 1)

    def row_copy(d, src):
        return pltpu.make_async_remote_copy(
            src_ref=rowbuf.at[src],
            dst_ref=rowbuf.at[src],
            send_sem=row_send,
            recv_sem=row_recv,
            device_id={"col": lax.rem(col + d, n_col)},
            device_id_type=MESH,
        )

    def redge_copy(side, d, src):
        to = lax.rem(line + (1 if side == 0 else n_line - 1), n_line)
        return pltpu.make_async_remote_copy(
            src_ref=rowtail.at[side],
            dst_ref=rowedge.at[side, src],
            send_sem=redge_send,
            recv_sem=redge_recv,
            device_id={
                "row": lax.div(to, n_rep),
                "rep": lax.rem(to, n_rep),
                "col": lax.rem(col + d, n_col),
            },
            device_id_type=MESH,
        )

    def col_copy(d, src):
        return pltpu.make_async_remote_copy(
            src_ref=colbuf.at[src],
            dst_ref=colbuf.at[src],
            send_sem=col_send,
            recv_sem=col_recv,
            device_id={"row": lax.rem(row + d, n_row)},
            device_id_type=MESH,
        )

    def cedge_copy(side, d, src):
        to = lax.rem(col + (1 if side == 0 else n_col - 1), n_col)
        return pltpu.make_async_remote_copy(
            src_ref=coltail.at[side],
            dst_ref=coledge.at[side, src],
            send_sem=cedge_send,
            recv_sem=cedge_recv,
            device_id={"row": lax.rem(row + d, n_row), "col": to},
            device_id_type=MESH,
        )

    for side in range(2):
        loop(0, n_row, lambda d: cedge_copy(side, d, row).start())
    loop(1, n_row, lambda d: col_copy(d, row).start())
    for side in range(2):
        loop(0, n_col, lambda d: redge_copy(side, d, col).start())
    loop(1, n_col, lambda d: row_copy(d, col).start())

    def await_features(col_sem, row_sem, cedge_sem, redge_sem):
        await_bytes(coledge, cedge_sem)
        if n_row > 1:
            await_bytes(colbuf.at[0 : n_row - 1], col_sem)
        await_bytes(rowedge, redge_sem)
        if n_col > 1:
            await_bytes(rowbuf.at[0 : n_col - 1], row_sem)

    fetch.wait()
    for copy in inputs[4:]:
        copy.wait()

    def widen(c, _):
        start = pl.multiple_of(c * edge, edge)
        target32[pl.ds(start, edge), :] = target_in[c].astype(F32)
        return 0

    lax.fori_loop(0, chan, widen, 0, unroll=4)
    def lay(p, _):
        for r in range(2):
            aim = target32[pl.ds(2 * p + r, chan, stride=edge), :].astype(BF16)
            start = pl.multiple_of(p * chan, chan)
            aims[pl.ds(start, chan), r * edge : (r + 1) * edge] = aim
        return 0

    lax.fori_loop(0, pairs, lay, 0, unroll=2)
    for a in range(3):
        for b in range(3):
            weight_f[b * chan : (b + 1) * chan, a * chan : (a + 1) * chan] = conv_weight[
                a, b
            ].astype(F32)
    turned = weight_f[...].T
    eye = lax.broadcasted_iota(jnp.int32, (chan, chan), 0) == lax.broadcasted_iota(
        jnp.int32, (chan, chan), 1
    )
    none = jnp.zeros((chan, chan), F32)
    minus = jnp.concatenate([none, jnp.where(eye, -1.0, 0.0), none], axis=0)
    weight_t[...] = jnp.concatenate([turned, minus], axis=1).astype(BF16)
    out_t = pair_out[...].astype(F32).T
    out_t = jnp.concatenate([out_t, out_t], axis=1)
    pair_b = jnp.broadcast_to(pair_bias[...], (128, chan)).T
    conv_b = jnp.broadcast_to(conv_bias[...], (128, chan)).T
    term = lax.broadcasted_iota(jnp.int32, (chan, 128), 1)
    second = pair_b - rounded(pair_b)
    third = second - rounded(second)
    bias_terms = jnp.where(
        term == 0,
        pair_b,
        jnp.where(term == 1, second, jnp.where(term == 2, third, 0.0)),
    ).astype(BF16)
    bias_acc[...] = jnp.zeros_like(bias_acc)

    await_features(col_recv, row_recv, cedge_recv, redge_recv)

    def summed(terms):
        return sum(x.astype(F32) for x in terms)

    row_feat[0:8, :] = rounded(summed(rowedge[0, c, 0:8, :] for c in range(n_col)))
    row_feat[8 : edge + 8, :] = rounded(summed(rowbuf[c, 0:rank, :] for c in range(n_col))).T
    row_feat[edge + 8 :, :] = rounded(summed(rowedge[1, c, 0:8, :] for c in range(n_col)))
    col_wide[0:8, :] = summed(coledge[0, r] for r in range(n_row))
    col_wide[8 : edge + 8, :] = summed(colbuf[r] for r in range(n_row)).T
    col_wide[edge + 8 :, :] = summed(coledge[1, r] for r in range(n_row))
    feat_pairs[0 : pairs + 2, :] = jnp.concatenate(
        [row_feat[pl.ds(6 + r, pairs + 2, stride=2), :] for r in range(2)], axis=1
    )

    lane = lax.broadcasted_iota(jnp.int32, (1, edge), 1)
    before, after = lax.rem(col + n_col - 1, n_col), lax.rem(col + 1, n_col)
    has_before = (col > 0).astype(F32)
    has_after = (col < n_col - 1).astype(F32)

    def masks(get, valid):
        here, left, right = (
            jnp.broadcast_to(get(c), (1, edge)) * scale
            for c, scale in ((col, valid), (before, valid * has_before), (after, valid * has_after))
        )
        return (jnp.where(lane < 2, left, here), here, jnp.where(lane >= edge - 2, right, here))

    top = masks(lambda c: rowedge[0, c, 8:9, 0:1], (line > 0).astype(F32))
    middle = masks(lambda c: rowbuf[c, rank:, 0:1].astype(F32)[0:1], jnp.float32(1))
    bottom = masks(lambda c: rowedge[1, c, 8:9, 0:1], (line < n_line - 1).astype(F32))

    shifted = [col_wide[6 + 2 * b : 6 + 2 * b + edge, :].T for b in range(3)]
    first_rows = lax.broadcasted_iota(jnp.int32, (2 * edge - 2 * rank, 2 * edge), 0) < 3

    def operand(b, mask):
        value = shifted[b] * mask
        blank = jnp.zeros_like(value)
        ones = jnp.where(first_rows, jnp.concatenate([mask, mask], axis=1), 0.0)
        return jnp.concatenate(
            [
                jnp.concatenate([value, blank], axis=1),
                jnp.concatenate([blank, value], axis=1),
                ones,
            ],
            axis=0,
        ).astype(BF16)

    for b in range(3):
        wide[b] = operand(b, middle[b])

    def scaled(p, count):
        low = (out_t * feat_pairs[pl.ds(p + 1 + r, 1), :] for r in range(count))
        low = jnp.concatenate([x.astype(BF16) for x in low], axis=0)
        return jnp.concatenate([low, jnp.concatenate([bias_terms] * count, axis=0)], axis=1)

    conv_b = jnp.concatenate([conv_b, conv_b], axis=1)
    blank = jnp.zeros((chan, 2 * edge), BF16)

    def slot(offset, first=0, count=1, of=1):
        low = (offset % 16 * of + first) * chan
        return slice(low, low + count * chan)

    def inside(p, offset):
        return not isinstance(p, int) or 0 <= p + offset < pairs

    def finish_pair(p, offset, conv):
        differ = (base[slot(offset), :] + conv) * keep
        grad_in[slot(offset), :] = differ.astype(BF16)
        bias_acc[...] += differ
        loss = 0.5 * jnp.sum(differ * differ, axis=0, keepdims=True)
        at = 2 * (p + offset)
        loss_out[pl.ds(at, 1), :] = loss[:, 0:edge]
        loss_out[pl.ds(at + 1, 1), :] = loss[:, edge : 2 * edge]

    def main(sum0, sum1, sum2, sum3, left0, left1, mid0, mid1, spare0, grad0, right0, right1, spare1, halo, grad1):
        sums, lefts, mids, rights = (
            (sum0, sum1, sum2, sum3),
            (left0, left1),
            (mid0, mid1),
            (right0, right1),
        )
        spares, grads = (spare0, spare1), (grad0, grad1)
        stage = [0, 0]

        def push_wide(unit, b):
            return lambda at: pltpu.matmul_push_rhs(wide[b], at, unit)

        def halo_item(p, offset, b, mask):
            def push(at):
                pltpu.matmul_push_rhs(operand(b, mask[b]), at, 1)

            def go(at):
                pltpu.matmul_acc_lhs(halo, scaled(p + offset, 1), load_staged_rhs=at)
                value = jnp.maximum(pltpu.matmul_pop(halo), 0.0)
                hid[slot(offset, b, 1, 3), :] = value.astype(BF16)

            return push, go, None, 4

        def feature_item(unit, b, p, offset, acc, memo):
            def go(at):
                if offset not in memo:
                    memo[offset] = scaled(p + offset, 2)
                pltpu.matmul_acc_lhs(acc, memo[offset], load_staged_rhs=at)

            def after():
                value = pltpu.matmul_pop(acc)
                for r in range(2):
                    own = value[r * chan : (r + 1) * chan]
                    hid[slot(offset + r, b, 1, 3), :] = jnp.maximum(own, 0.0).astype(BF16)
                    if b == 1:
                        base[slot(offset + r), :] = own + conv_b

            return push_wide(unit, b), go, after, 8

        def conv_item(p, offset):
            taps = [a for a in range(3) if inside(p, offset + 1 - a)]

            def push(at):
                aim = blank
                if inside(p, offset):
                    aim = aims[pl.ds(pl.multiple_of((p + offset) * chan, chan), chan), :]
                right = jnp.concatenate([hid[slot(offset, 0, 3, 3), :], aim], axis=0)
                pltpu.matmul_push_rhs(right, at, 0)

            def go(at):
                for a in taps:
                    pltpu.matmul_acc_lhs(
                        sums[(offset + 1 - a) % 4],
                        weight_t[a * chan : (a + 1) * chan, :],
                        load_staged_rhs=at,
                    )
                    at = None

            def after():
                if 2 in taps:
                    finish_pair(p, offset - 1, pltpu.matmul_pop(sums[(offset - 1) % 4]))

            return push, go, after, 4 * len(taps)

        def grad_item(unit, p, offset):
            def push(at):
                right = [
                    grad_in[slot(offset + k), :] if inside(p, offset + k) else blank
                    for k in range(-2, 2)
                ]
                right = jnp.concatenate(right, axis=0)
                pltpu.matmul_push_rhs(right, at, unit, transpose=True)

            def go(at):
                left = hid[slot(offset, 0, 3, 3), :]
                pltpu.matmul_acc_lhs(grads[unit], left, load_staged_rhs=at)

            return push, go, None, 12

        def spare_item(unit, b):
            def go(at):
                left = jnp.zeros((16, 2 * edge), BF16)
                pltpu.matmul_acc_lhs(spares[unit], left, load_staged_rhs=at)

            def after():
                part[0:16, :] = pltpu.matmul_pop(spares[unit])[:, 0:128]

            return push_wide(unit, b), go, after, 1

        def run(queues, tails=(None, None), primed=True):
            spent, at, waiting = [0, 0], [0, 0], []
            for unit in range(2):
                if queues[unit] and not primed:
                    queues[unit][0][0](stage[unit])
            while any(at[u] < len(queues[u]) for u in range(2)):
                unit = min(
                    (u for u in range(2) if at[u] < len(queues[u])), key=lambda u: spent[u]
                )
                queue, index = queues[unit], at[unit]
                _, go, after, cost = queue[index]
                later = queue[index + 1][0] if index + 1 < len(queue) else tails[unit]
                while len(waiting) > 1:
                    waiting.pop(0)()
                go(stage[unit])
                stage[unit] = 1 - stage[unit]
                if later is not None:
                    later(stage[unit])
                at[unit] += 1
                spent[unit] += cost
                if after is not None:
                    waiting.append(after)
            for after in waiting:
                after()

        tails = (push_wide(0, 0), push_wide(1, 2))

        def features(p, low):
            memo = {}
            first, second = [], []
            for half in range(2):
                offset = low + 2 * half
                first.append(feature_item(0, 0, p, offset, lefts[half], memo))
                first.append(feature_item(0, 1, p, offset, mids[half], memo))
                second.append(feature_item(1, 2, p, offset, rights[half], memo))
            return first, second

        def merged(own, other):
            return own[0:2] + other[0:2] + own[2:4] + other[2:]

        def group(p, low):
            f0, f1 = features(p, low)
            convs = [conv_item(p, low - 4 + r) for r in range(4)]
            turns = [grad_item(1, p, low - 12 + r) for r in range(4)]
            run((merged(f0, convs), [f1[0], *turns[0:2], f1[1], *turns[2:4]]), tails)

        halos = [halo_item(0, -1, b, top) for b in range(3)]
        f0, f1 = features(0, 0)
        run((f0, halos + f1), tails, primed=False)
        f0, f1 = features(0, 4)
        convs = [conv_item(0, r) for r in range(-1, 4)]
        run((merged(f0, convs) + [spare_item(0, 0)], f1), tails)
        f0, f1 = features(0, 8)
        convs = [conv_item(0, r) for r in range(4, 8)]
        turns = [grad_item(1, 0, r) for r in (-1, 0, 1)]
        run((merged(f0, convs), [f1[0], *turns[0:2], f1[1], turns[2], spare_item(1, 2)]), tails)
        f0, f1 = features(0, 12)
        convs = [conv_item(0, r) for r in range(8, 12)]
        turns = [grad_item(1, 0, r) for r in (2, 3)]
        run((merged(f0, convs), [f1[0], turns[0], f1[1], turns[1]]), tails)

        def step(t, _):
            p = pl.multiple_of(t * 16, 16)
            for k in range(4):
                group(p, 4 * k)
            return 0

        lax.fori_loop(1, pairs // 16, step, 0)
        halos = [halo_item(pairs, 0, b, bottom) for b in range(3)]
        turns = [grad_item(1, pairs, r) for r in range(-12, -6)]
        convs = [conv_item(pairs, r) for r in range(-4, 1)]
        run(
            (
                [spare_item(0, 0)] + convs,
                [spare_item(1, 2)] + halos + turns,
            )
        )
        turns = [[grad_item(u, pairs, r) for r in range(-6 + u, 1, 2)] for u in range(2)]
        run(turns, primed=False)
        total[...] = pltpu.matmul_pop(grad0) + pltpu.matmul_pop(grad1)

    def accumulator(unit, rows_of):
        return pltpu.ACC(unit)((rows_of, 2 * edge), F32)

    pl.run_scoped(
        main,
        *[accumulator(0, chan)] * 4,
        *[accumulator(0, 2 * chan)] * 4,
        accumulator(0, 16),
        accumulator(0, 3 * chan),
        *[accumulator(1, 2 * chan)] * 2,
        accumulator(1, 16),
        accumulator(1, chan),
        accumulator(1, 3 * chan),
    )

    norm = 1.0 / (edge * edge)
    half = 3 * chan // 2
    rows = 3 * chan + half
    sums = total[...] * norm
    flat = jnp.concatenate(
        [
            sums[:, 2 * chan :],
            jnp.concatenate(
                [sums[0:half, chan : 2 * chan], sums[half:, chan : 2 * chan]], axis=1
            ),
        ],
        axis=0,
    )
    bias_sum = (bias_acc[:, 0:edge] + bias_acc[:, edge:]).T
    bias_sum = jnp.sum(bias_sum, axis=0, keepdims=True) * norm
    bias_sum = jnp.broadcast_to(bias_sum, (8, chan))
    part[0:rows, :] = flat
    for term in range(3):
        low = rows + 8 * term
        part[low : low + 8, :] = jnp.concatenate([bias_sum, bias_sum], axis=1)
    rest = n_own * chunk - rows - 24
    if rest > 0:
        part[rows + 24 :, :] = jnp.zeros((rest, 128), F32)

    mine = me - first_own
    owner = (mine >= 0) & (mine < n_own)

    def piece(index):
        return pl.ds(pl.multiple_of(index * chunk, 8), chunk)

    def scatter(d):
        index = lax.rem(me + d, n_own)

        @pl.when(first_own + index != me)
        def _():
            pltpu.make_async_remote_copy(
                src_ref=part.at[piece(index)],
                dst_ref=reduced.at[me],
                send_sem=rs_send,
                recv_sem=rs_recv,
                device_id=device(first_own + index),
                device_id_type=MESH,
            ).start()

    def gather(d):
        pltpu.make_async_remote_copy(
            src_ref=full.at[mine],
            dst_ref=full.at[mine],
            send_sem=ag_send,
            recv_sem=ag_recv,
            device_id=device(lax.rem(me + d, n_all)),
            device_id_type=MESH,
        ).start()

    loop(0, n_own, scatter)

    @pl.when(owner)
    def _():
        reduced[me] = part[piece(mine), :]
        await_bytes(reduced.at[0 : n_all - 1], rs_recv)
        if n_all <= 16:
            own = sum(reduced[r] for r in range(n_all))
        else:
            own = lax.fori_loop(
                0, n_all, lambda r, x: x + reduced[r], jnp.zeros((chunk, 128), F32)
            )
        at = mine * chunk + lax.broadcasted_iota(jnp.int32, (chunk, 128), 0)
        second = own - rounded(own)
        third = second - rounded(second)
        own = jnp.where(at >= rows + 8, jnp.where(at >= rows + 16, third, second), own)
        full[mine] = own.astype(BF16)
        loop(1, n_all, gather)
        if n_own > 1:
            await_bytes(full.at[0 : n_own - 1], ag_recv)
            await_bytes(part.at[0 : (n_own - 1) * chunk], rs_send)

    @pl.when(jnp.logical_not(owner))
    def _():
        await_bytes(full, ag_recv)
        await_bytes(part, rs_send)

    await_features(col_send, row_send, cedge_send, redge_send)

    @pl.when(owner)
    def _():
        await_bytes(whole, ag_send)


def finish(loss, gathered, loss_hbm, conv_grad_hbm, bias_hbm, full, conv_grad_out, bias_out, sem):
    n_all, chunk = gathered.shape[0:2]
    loss_copy = pltpu.make_async_copy(loss, loss_hbm, sem.at[0])
    loss_copy.start()

    def place(r):
        full[pl.ds(r * chunk, chunk), :] = gathered[r].astype(F32)

    loop(0, n_all, place)
    chan = bias_out.shape[1]
    half = 3 * chan // 2
    rows = 3 * chan + half
    for b in range(3):
        low = b * chan
        conv_grad_out[1, b] = full[low : low + chan, 0:chan]
        conv_grad_out[0, b] = full[low : low + chan, chan : 2 * chan]
    low = 3 * chan
    conv_grad_out[2, 0] = full[low : low + chan, 0:chan]
    conv_grad_out[2, 1, 0 : half - chan] = full[low + chan : low + half, 0:chan]
    conv_grad_out[2, 1, half - chan :] = full[low : low + 2 * chan - half, chan : 2 * chan]
    conv_grad_out[2, 2] = full[low + 2 * chan - half : low + half, chan : 2 * chan]
    bias_out[...] = sum(full[rows + 8 * t : rows + 8 * t + 1, 0:chan] for t in range(3))
    grad_copy = pltpu.make_async_copy(conv_grad_out, conv_grad_hbm, sem.at[1])
    bias_copy = pltpu.make_async_copy(bias_out, bias_hbm, sem.at[2])
    grad_copy.start()
    bias_copy.start()
    loss_copy.wait()
    grad_copy.wait()
    bias_copy.wait()


def solution(mesh):
    n_row, n_col, n_rep = (mesh.shape[axis] for axis in ("row", "col", "rep"))
    n_all = n_row * n_col * n_rep

    def per_device(
        emb_row,
        emb_col,
        proj_row,
        proj_col,
        pair_out,
        pair_bias,
        conv_weight,
        conv_bias,
        target,
        kept_tiles,
    ):
        chan, edge = target.shape[0], target.shape[1]
        rank = pair_out.shape[0]
        pairs = edge // 2
        used = 3 * chan + 3 * chan // 2 + 24
        inner = n_row // 2 if n_row >= 4 else n_row
        n_own = inner * n_col * n_rep
        first_own = (n_row - inner) // 2 * n_col * n_rep
        chunk = 8 * pl.cdiv(used, 8 * n_own)

        dma = pltpu.SemaphoreType.DMA
        vmem = pl.BlockSpec(memory_space=pltpu.VMEM)
        hbm = pl.BlockSpec(memory_space=pltpu.HBM)
        loss, sums = pl.pallas_call(
            functools.partial(
                kernel, (n_row, n_col, n_rep, edge, chan, n_own, first_own, chunk)
            ),
            out_shape=(
                pltpu.VMEM((edge, edge), F32),
                pltpu.VMEM((n_own, chunk, 128), BF16),
            ),
            in_specs=[hbm] * 9 + [pl.BlockSpec(memory_space=pltpu.SMEM)],
            out_specs=(vmem,) * 2,
            scratch_shapes=[
                pltpu.VMEM(emb_row.shape, BF16),
                pltpu.VMEM(emb_col.shape[::-1], BF16),
                pltpu.VMEM(proj_row.shape[::-1], BF16),
                pltpu.VMEM(proj_col.shape[::-1], BF16),
                pltpu.VMEM(conv_weight.shape, BF16),
                pltpu.VMEM(pair_out.shape, BF16),
                pltpu.VMEM((1, chan), F32),
                pltpu.VMEM((1, chan), F32),
                dma((8,)),
                pltpu.VMEM((2, 16, rank), F32),
                pltpu.VMEM((2, 8, rank), F32),
                pltpu.VMEM((n_col, rank + 16, edge), BF16),
                pltpu.VMEM((2, n_col, 16, rank), F32),
                pltpu.VMEM((n_row, rank, edge), BF16),
                pltpu.VMEM((2, n_row, 8, rank), F32),
                pltpu.VMEM((edge + 16, rank), F32),
                pltpu.VMEM((edge + 16, rank), F32),
                pltpu.VMEM((pairs + 8, 2 * rank), F32),
                pltpu.VMEM((256, 256), BF16),
                pltpu.VMEM((3, 2 * edge, 2 * edge), BF16),
                pltpu.VMEM((3 * chan, 4 * chan), BF16),
                pltpu.VMEM((chan, edge, edge), BF16),
                pltpu.VMEM((chan * edge, edge), F32),
                pltpu.VMEM((pairs * chan, 2 * edge), BF16),
                pltpu.VMEM((16 * 3 * chan, 2 * edge), BF16),
                pltpu.VMEM((16 * chan, 2 * edge), F32),
                pltpu.VMEM((16 * chan, 2 * edge), BF16),
                pltpu.VMEM((3 * chan, 3 * chan), F32),
                pltpu.VMEM((3 * chan, 4 * chan), F32),
                pltpu.VMEM((chan, 2 * edge), F32),
                pltpu.VMEM((n_own * chunk, 128), F32),
                pltpu.VMEM((n_all, chunk, 128), F32),
                pltpu.VMEM((n_all - 1, chunk, 128), BF16),
                *[pltpu.SemaphoreType.DMA] * 13,
            ],
            compiler_params=pltpu.CompilerParams(collective_id=0, has_side_effects=True),
            name="pair_step",
        )(
            emb_row,
            emb_col.T,
            proj_row.T,
            proj_col.T,
            pair_out,
            pair_bias.reshape(1, chan),
            conv_weight,
            conv_bias.reshape(1, chan),
            target,
            kept_tiles,
        )
        loss, grads, bias = pl.pallas_call(
            finish,
            out_shape=(
                jax.ShapeDtypeStruct((edge, edge), F32),
                jax.ShapeDtypeStruct((3, 3, chan, chan), F32),
                jax.ShapeDtypeStruct((1, chan), F32),
            ),
            in_specs=[vmem] * 2,
            out_specs=(hbm,) * 3,
            scratch_shapes=[
                pltpu.VMEM((n_own * chunk, 128), F32),
                pltpu.VMEM((3, 3, chan, chan), F32),
                pltpu.VMEM((1, chan), F32),
                dma((3,)),
            ],
            name="finish",
        )(
            *(pltpu.with_memory_space_constraint(x, pltpu.VMEM) for x in (loss, sums))
        )
        return loss, grads, bias.reshape(chan)

    in_specs = (
        P(("grp", "row", "rep"), "col"),
        P(("grp", "col"), "row"),
        P(),
        P(),
        P(),
        P(),
        P(),
        P(),
        P(None, ("grp", "row", "rep"), "col"),
        P(("grp", "row", "rep"), "col"),
    )
    out_specs = (P(("grp", "row", "rep"), "col"), P("grp", None, None, None), P("grp"))
    return jax.shard_map(
        per_device, mesh=mesh, in_specs=in_specs, out_specs=out_specs, check_vma=False
    )
```

```python
import functools

import jax
import jax.numpy as jnp
from jax import lax
from jax.experimental import pallas as pl
from jax.experimental.pallas import tpu as pltpu
from jax.sharding import PartitionSpec as P

MESH = pl.DeviceIdType.MESH
F32 = jnp.float32
BF16 = jnp.bfloat16
NT = (((1,), (1,)), ((), ()))


def loop(low, high, body):
    if high - low <= 16:
        for d in range(low, high):
            body(d)
    else:
        lax.fori_loop(low, high, lambda d, _: (body(d), 0)[1], 0)


def columns(ref, width, index, count):
    everything = ref.shape[1]
    if width % 128 == 0:
        return ref[:, pl.ds(pl.multiple_of(index * width, 128), width)]
    offset = max(i * width % 128 for i in range(count))
    window = min(-(-(offset + width) // 128) * 128, everything)
    tile = index * width // 128
    if any(i * width // 128 * 128 + window > everything for i in range(count)):
        tile = jnp.minimum(tile, (everything - window) // 128)
    value = ref[:, pl.ds(pl.multiple_of(tile * 128, 128), window)].astype(F32)
    shift = window - (index * width - tile * 128)
    value = pltpu.roll(value, lax.rem(shift, window), 1)
    lane = lax.broadcasted_iota(jnp.int32, value.shape, 1)
    return jnp.where(lane < width, value, 0.0).astype(BF16)


def padded(value, square):
    if all(have == 256 or have % 128 == 0 for have in value.shape):
        for axis in range(2):
            if value.shape[axis] < 256:
                blank = list(value.shape)
                blank[axis] = 256 - blank[axis]
                value = jnp.concatenate([value, jnp.zeros(blank, BF16)], axis=axis)
        return value
    square[...] = jnp.zeros_like(square)
    square[0 : value.shape[0], 0 : value.shape[1]] = value
    return square[...]


def wide_tile(value, low):
    value = value[:, low : low + 256]
    if value.shape[1] < 256:
        blank = jnp.zeros((value.shape[0], 256 - value.shape[1]), BF16)
        value = jnp.concatenate([value, blank], axis=1)
    return value


def kernel(
    sizes,
    emb_row_hbm,
    emb_col_hbm,
    proj_row_hbm,
    proj_col_hbm,
    pair_out_hbm,
    pair_bias_hbm,
    conv_weight_hbm,
    conv_bias_hbm,
    target,
    kept,
    loss_out,
    full,
    full_side,
    emb_row,
    emb_col,
    proj_row,
    proj_col,
    conv_weight,
    pair_out,
    pair_bias,
    conv_bias,
    in_sem,
    rowtail,
    coltail,
    rowbuf,
    rowedge,
    colbuf,
    coledge,
    row_feat,
    col_wide,
    feat_pairs,
    square,
    wide,
    weight_t,
    target_in,
    aims,
    hid,
    base,
    grad_in,
    weight_f,
    total,
    bias_acc,
    spill,
    part,
    reduced,
    own_side,
    sides,
    target_sem,
    row_send,
    row_recv,
    redge_send,
    redge_recv,
    col_send,
    col_recv,
    cedge_send,
    cedge_recv,
    rs_send,
    rs_recv,
    ag_send,
    ag_recv,
    side_send,
    side_recv,
    full_send,
    full_recv,
):
    n_row, n_col, n_rep, edge, chan, n_own, first_own, chunk = sizes
    n_all = n_row * n_col * n_rep
    pairs = edge // 2
    row, col, rep = lax.axis_index("row"), lax.axis_index("col"), lax.axis_index("rep")
    line = row * n_rep + rep
    n_line = n_row * n_rep
    me = line * n_col + col

    def device(index):
        across = lax.rem(index, n_col)
        along = lax.div(index, n_col)
        return {"row": lax.div(along, n_rep), "rep": lax.rem(along, n_rep), "col": across}

    def await_bytes(ref, sem):
        pltpu.make_async_copy(ref, ref, sem).wait()

    barrier = pltpu.get_barrier_semaphore()
    loop(
        1,
        n_all,
        lambda d: pl.semaphore_signal(
            barrier, inc=1, device_id=device(lax.rem(me + d, n_all)), device_id_type=MESH
        ),
    )

    inputs = [
        pltpu.make_async_copy(src, dst, in_sem.at[i])
        for i, (src, dst) in enumerate(
            (
                (emb_row_hbm, emb_row),
                (proj_row_hbm, proj_row),
                (emb_col_hbm, emb_col),
                (proj_col_hbm, proj_col),
                (conv_weight_hbm, conv_weight),
                (pair_out_hbm, pair_out),
                (pair_bias_hbm, pair_bias),
                (conv_bias_hbm, conv_bias),
            )
        )
    ]
    for copy in inputs:
        copy.start()
    fetch = pltpu.make_async_copy(target, target_in, target_sem)
    fetch.start()

    def rounded(x):
        return x.astype(BF16).astype(F32)

    for copy in inputs[2:4]:
        copy.wait()
    rank = proj_row.shape[0]

    def project(col_sum, row_sum):
        width = emb_col.shape[0]
        left = columns(proj_col, width, row, n_row)
        for low in range(0, width, 256):
            right = padded(emb_col[low : min(low + 256, width), :], square)
            pltpu.matmul_push_rhs(right, 0, 0)
            pltpu.matmul_acc_lhs(col_sum, wide_tile(left, low), load_staged_rhs=0)
        for copy in inputs[0:2]:
            copy.wait()
        width = emb_row.shape[1]
        left = columns(proj_row, width, col, n_col)
        for low in range(0, width, 256):
            right = padded(emb_row[:, low : min(low + 256, width)], square)
            pltpu.matmul_push_rhs(right, 0, 1, transpose=True)
            pltpu.matmul_acc_lhs(row_sum, wide_tile(left, low), load_staged_rhs=0)
        return pltpu.matmul_pop(col_sum)[:, 0:edge], pltpu.matmul_pop(row_sum)[:, 0:edge]

    part_col, part_row = pl.run_scoped(
        project, *[pltpu.ACC(unit)((rank, 256), F32) for unit in range(2)]
    )
    keep = kept[0, 0].astype(F32)
    colbuf[row] = part_col.astype(BF16)
    rowbuf[col, 0:rank, :] = part_row.astype(BF16)
    rowbuf[col, rank:, :] = jnp.full((16, edge), keep, F32).astype(BF16)
    ends = ((edge - 2, edge - 1), (0, 1))

    def pair_row(values, at):
        return jnp.concatenate([values[r : r + 1] for r in at], axis=1)

    turned = rounded(part_col).T
    for side in range(2):
        coltail[side] = pair_row(turned, ends[side])
    turned = rounded(part_row).T
    for side in range(2):
        rowtail[side, 0:1] = pair_row(turned, ends[side])
        rowtail[side, 1:2] = jnp.full((1, 2 * rank), keep, F32)

    pl.semaphore_wait(barrier, n_all - 1)

    def row_copy(d, src):
        return pltpu.make_async_remote_copy(
            src_ref=rowbuf.at[src],
            dst_ref=rowbuf.at[src],
            send_sem=row_send,
            recv_sem=row_recv,
            device_id={"col": lax.rem(col + d, n_col)},
            device_id_type=MESH,
        )

    def redge_copy(side, d, src):
        to = lax.rem(line + (1 if side == 0 else n_line - 1), n_line)
        return pltpu.make_async_remote_copy(
            src_ref=rowtail.at[side],
            dst_ref=rowedge.at[side, src],
            send_sem=redge_send,
            recv_sem=redge_recv,
            device_id={
                "row": lax.div(to, n_rep),
                "rep": lax.rem(to, n_rep),
                "col": lax.rem(col + d, n_col),
            },
            device_id_type=MESH,
        )

    def col_copy(k, src):
        down, up = n_row - 1 - k, k
        down = down - (down <= row).astype(jnp.int32)
        up = up + (up >= row).astype(jnp.int32)
        return pltpu.make_async_remote_copy(
            src_ref=colbuf.at[src],
            dst_ref=colbuf.at[src],
            send_sem=col_send,
            recv_sem=col_recv,
            device_id={"row": jnp.where(2 * row < n_row, down, up)},
            device_id_type=MESH,
        )

    def cedge_copy(side, d, src):
        to = lax.rem(col + (1 if side == 0 else n_col - 1), n_col)
        return pltpu.make_async_remote_copy(
            src_ref=coltail.at[side],
            dst_ref=coledge.at[side, src],
            send_sem=cedge_send,
            recv_sem=cedge_recv,
            device_id={"row": lax.rem(row + d, n_row), "col": to},
            device_id_type=MESH,
        )

    for side in range(2):
        loop(0, n_row, lambda d: cedge_copy(side, d, row).start())
    loop(0, n_row - 1, lambda k: col_copy(k, row).start())
    for side in range(2):
        loop(0, n_col, lambda d: redge_copy(side, d, col).start())
    loop(1, n_col, lambda d: row_copy(d, col).start())

    def await_features(col_sem, row_sem, cedge_sem, redge_sem):
        await_bytes(coledge, cedge_sem)
        if n_row > 1:
            await_bytes(colbuf.at[0 : n_row - 1], col_sem)
        await_bytes(rowedge, redge_sem)
        if n_col > 1:
            await_bytes(rowbuf.at[0 : n_col - 1], row_sem)

    fetch.wait()
    for copy in inputs[4:]:
        copy.wait()

    def lay(i, _):
        for low in range(0, chan, 16):
            block = target_in[low : low + 16, pl.ds(pl.multiple_of(i * 16, 16), 16), :]
            block = jnp.swapaxes(block.astype(F32), 0, 1)
            for r in range(16):
                start = pl.multiple_of((i * 8 + r // 2) * chan + low, 16)
                lanes = slice(r % 2 * edge, (r % 2 + 1) * edge)
                aims[pl.ds(start, 16), lanes] = block[r].astype(BF16)
        return 0

    lax.fori_loop(0, edge // 16, lay, 0)
    for a in range(3):
        for b in range(3):
            weight_f[b * chan : (b + 1) * chan, a * chan : (a + 1) * chan] = conv_weight[
                a, b
            ].astype(F32)
    turned = weight_f[...].T
    eye = lax.broadcasted_iota(jnp.int32, (chan, chan), 0) == lax.broadcasted_iota(
        jnp.int32, (chan, chan), 1
    )
    none = jnp.zeros((chan, chan), F32)
    minus = jnp.concatenate([none, jnp.where(eye, -1.0, 0.0), none], axis=0)
    weight_t[...] = jnp.concatenate([turned, minus], axis=1).astype(BF16)
    out_t = pair_out[...].astype(F32).T
    out_t = jnp.concatenate([out_t, out_t], axis=1)
    pair_b = jnp.broadcast_to(pair_bias[...], (128, chan)).T
    conv_b = jnp.broadcast_to(conv_bias[...], (128, chan)).T
    term = lax.broadcasted_iota(jnp.int32, (chan, 128), 1)
    second = pair_b - rounded(pair_b)
    third = second - rounded(second)
    bias_terms = jnp.where(
        term == 0,
        pair_b,
        jnp.where(term == 1, second, jnp.where(term == 2, third, 0.0)),
    ).astype(BF16)
    bias_acc[...] = jnp.zeros_like(bias_acc)

    await_features(col_recv, row_recv, cedge_recv, redge_recv)

    def summed(terms):
        return sum(x.astype(F32) for x in terms)

    def unpack(target, values, low):
        for r in range(2):
            target[low + r : low + r + 1, :] = values[:, r * rank : (r + 1) * rank]

    for side, low in ((0, 6), (1, edge + 8)):
        edge_sum = rounded(summed(rowedge[side, c, 0:1, :] for c in range(n_col)))
        unpack(row_feat, edge_sum, low)
        unpack(col_wide, summed(coledge[side, r] for r in range(n_row)), low)
    row_feat[8 : edge + 8, :] = rounded(summed(rowbuf[c, 0:rank, :] for c in range(n_col))).T
    col_wide[8 : edge + 8, :] = summed(colbuf[r] for r in range(n_row)).T
    feat_pairs[0 : pairs + 2, :] = jnp.concatenate(
        [row_feat[pl.ds(6 + r, pairs + 2, stride=2), :] for r in range(2)], axis=1
    )

    lane = lax.broadcasted_iota(jnp.int32, (1, edge), 1)
    before, after = lax.rem(col + n_col - 1, n_col), lax.rem(col + 1, n_col)
    has_before = (col > 0).astype(F32)
    has_after = (col < n_col - 1).astype(F32)

    def masks(get, valid):
        here, left, right = (
            jnp.broadcast_to(get(c), (1, edge)) * scale
            for c, scale in ((col, valid), (before, valid * has_before), (after, valid * has_after))
        )
        return (jnp.where(lane < 2, left, here), here, jnp.where(lane >= edge - 2, right, here))

    top = masks(lambda c: rowedge[0, c, 1:2, 0:1], (line > 0).astype(F32))
    middle = masks(lambda c: rowbuf[c, rank:, 0:1].astype(F32)[0:1], jnp.float32(1))
    bottom = masks(lambda c: rowedge[1, c, 1:2, 0:1], (line < n_line - 1).astype(F32))

    shifted = [col_wide[6 + 2 * b : 6 + 2 * b + edge, :].T for b in range(3)]
    first_rows = lax.broadcasted_iota(jnp.int32, (2 * edge - 2 * rank, 2 * edge), 0) < 3

    def operand(b, mask):
        value = shifted[b] * mask
        blank = jnp.zeros_like(value)
        ones = jnp.where(first_rows, jnp.concatenate([mask, mask], axis=1), 0.0)
        return jnp.concatenate(
            [
                jnp.concatenate([value, blank], axis=1),
                jnp.concatenate([blank, value], axis=1),
                ones,
            ],
            axis=0,
        ).astype(BF16)

    for b in range(3):
        wide[b] = operand(b, middle[b])

    def scaled(p, count):
        low = (out_t * feat_pairs[pl.ds(p + 1 + r, 1), :] for r in range(count))
        low = jnp.concatenate([x.astype(BF16) for x in low], axis=0)
        return jnp.concatenate([low, jnp.concatenate([bias_terms] * count, axis=0)], axis=1)

    conv_b = jnp.concatenate([conv_b, conv_b], axis=1)
    blank = jnp.zeros((chan, 2 * edge), BF16)

    def slot(offset, first=0, count=1, of=1):
        low = (offset % 16 * of + first) * chan
        return slice(low, low + count * chan)

    def inside(p, offset):
        return not isinstance(p, int) or 0 <= p + offset < pairs

    def finish_pair(p, offset, conv):
        differ = (base[slot(offset), :] + conv) * keep
        grad_in[slot(offset), :] = differ.astype(BF16)
        bias_acc[...] += differ
        loss = 0.5 * jnp.sum(differ * differ, axis=0, keepdims=True)
        at = 2 * (p + offset)
        loss_out[pl.ds(at, 1), :] = loss[:, 0:edge]
        loss_out[pl.ds(at + 1, 1), :] = loss[:, edge : 2 * edge]

    def main(sum0, sum1, sum2, sum3, left0, left1, mid0, mid1, spare0, grad0, right0, right1, spare1, halo, grad1):
        sums, lefts, mids, rights = (
            (sum0, sum1, sum2, sum3),
            (left0, left1),
            (mid0, mid1),
            (right0, right1),
        )
        spares, grads = (spare0, spare1), (grad0, grad1)
        stage = [0, 0]

        def push_wide(unit, b):
            return lambda at: pltpu.matmul_push_rhs(wide[b], at, unit)

        def halo_item(p, offset, b, mask):
            def push(at):
                pltpu.matmul_push_rhs(operand(b, mask[b]), at, 1)

            def go(at):
                pltpu.matmul_acc_lhs(halo, scaled(p + offset, 1), load_staged_rhs=at)
                value = jnp.maximum(pltpu.matmul_pop(halo), 0.0)
                hid[slot(offset, b, 1, 3), :] = value.astype(BF16)

            return push, go, None, 4

        def feature_item(unit, b, p, offset, acc, memo):
            def go(at):
                if offset not in memo:
                    memo[offset] = scaled(p + offset, 2)
                pltpu.matmul_acc_lhs(acc, memo[offset], load_staged_rhs=at)

            def after():
                value = pltpu.matmul_pop(acc)
                for r in range(2):
                    own = value[r * chan : (r + 1) * chan]
                    hid[slot(offset + r, b, 1, 3), :] = jnp.maximum(own, 0.0).astype(BF16)
                    if b == 1:
                        base[slot(offset + r), :] = own + conv_b

            return push_wide(unit, b), go, after, 8

        def conv_item(p, offset):
            taps = [a for a in range(3) if inside(p, offset + 1 - a)]

            def push(at):
                aim = blank
                if inside(p, offset):
                    aim = aims[pl.ds(pl.multiple_of((p + offset) * chan, chan), chan), :]
                right = jnp.concatenate([hid[slot(offset, 0, 3, 3), :], aim], axis=0)
                pltpu.matmul_push_rhs(right, at, 0)

            def go(at):
                for a in taps:
                    pltpu.matmul_acc_lhs(
                        sums[(offset + 1 - a) % 4],
                        weight_t[a * chan : (a + 1) * chan, :],
                        load_staged_rhs=at,
                    )
                    at = None

            def after():
                if 2 in taps:
                    finish_pair(p, offset - 1, pltpu.matmul_pop(sums[(offset - 1) % 4]))

            return push, go, after, 4 * len(taps)

        def grad_item(unit, p, offset):
            def push(at):
                right = [
                    grad_in[slot(offset + k), :] if inside(p, offset + k) else blank
                    for k in range(-2, 2)
                ]
                right = jnp.concatenate(right, axis=0)
                pltpu.matmul_push_rhs(right, at, unit, transpose=True)

            def go(at):
                left = hid[slot(offset, 0, 3, 3), :]
                pltpu.matmul_acc_lhs(grads[unit], left, load_staged_rhs=at)

            return push, go, None, 12

        def spare_item(unit, b):
            def go(at):
                left = jnp.zeros((16, 2 * edge), BF16)
                pltpu.matmul_acc_lhs(spares[unit], left, load_staged_rhs=at)

            def after():
                spill[...] = pltpu.matmul_pop(spares[unit])[:, 0:128]

            return push_wide(unit, b), go, after, 1

        def run(queues, tails=(None, None), primed=True):
            spent, at, waiting = [0, 0], [0, 0], []
            for unit in range(2):
                if queues[unit] and not primed:
                    queues[unit][0][0](stage[unit])
            while any(at[u] < len(queues[u]) for u in range(2)):
                unit = min(
                    (u for u in range(2) if at[u] < len(queues[u])), key=lambda u: spent[u]
                )
                queue, index = queues[unit], at[unit]
                _, go, after, cost = queue[index]
                later = queue[index + 1][0] if index + 1 < len(queue) else tails[unit]
                while len(waiting) > 1:
                    waiting.pop(0)()
                go(stage[unit])
                stage[unit] = 1 - stage[unit]
                if later is not None:
                    later(stage[unit])
                at[unit] += 1
                spent[unit] += cost
                if after is not None:
                    waiting.append(after)
            for after in waiting:
                after()

        tails = (push_wide(0, 0), push_wide(1, 2))

        def features(p, low):
            memo = {}
            first, second = [], []
            for half in range(2):
                offset = low + 2 * half
                first.append(feature_item(0, 0, p, offset, lefts[half], memo))
                first.append(feature_item(0, 1, p, offset, mids[half], memo))
                second.append(feature_item(1, 2, p, offset, rights[half], memo))
            return first, second

        def merged(own, other):
            return own[0:2] + other[0:2] + own[2:4] + other[2:]

        def group(p, low):
            f0, f1 = features(p, low)
            convs = [conv_item(p, low - 4 + r) for r in range(4)]
            turns = [grad_item(1, p, low - 12 + r) for r in range(4)]
            run((merged(f0, convs), [f1[0], *turns[0:2], f1[1], *turns[2:4]]), tails)

        halos = [halo_item(0, -1, b, top) for b in range(3)]
        f0, f1 = features(0, 0)
        run((f0, halos + f1), tails, primed=False)
        f0, f1 = features(0, 4)
        convs = [conv_item(0, r) for r in range(-1, 4)]
        run((merged(f0, convs) + [spare_item(0, 0)], f1), tails)
        f0, f1 = features(0, 8)
        convs = [conv_item(0, r) for r in range(4, 8)]
        turns = [grad_item(1, 0, r) for r in (-1, 0, 1)]
        run((merged(f0, convs), [f1[0], *turns[0:2], f1[1], turns[2], spare_item(1, 2)]), tails)
        f0, f1 = features(0, 12)
        convs = [conv_item(0, r) for r in range(8, 12)]
        turns = [grad_item(1, 0, r) for r in (2, 3)]
        run((merged(f0, convs), [f1[0], turns[0], f1[1], turns[1]]), tails)

        def step(t, _):
            p = pl.multiple_of(t * 16, 16)
            for k in range(4):
                group(p, 4 * k)
            return 0

        lax.fori_loop(1, pairs // 16, step, 0)
        halos = [halo_item(pairs, 0, b, bottom) for b in range(3)]
        turns = [grad_item(1, pairs, r) for r in range(-12, -6)]
        convs = [conv_item(pairs, r) for r in range(-4, 1)]
        run(
            (
                [spare_item(0, 0)] + convs,
                [spare_item(1, 2)] + halos + turns,
            )
        )
        turns = [[grad_item(u, pairs, r) for r in range(-6 + u, 1, 2)] for u in range(2)]
        run(turns, primed=False)
        total[...] = pltpu.matmul_pop(grad0) + pltpu.matmul_pop(grad1)

    def accumulator(unit, rows_of):
        return pltpu.ACC(unit)((rows_of, 2 * edge), F32)

    pl.run_scoped(
        main,
        *[accumulator(0, chan)] * 4,
        *[accumulator(0, 2 * chan)] * 4,
        accumulator(0, 16),
        accumulator(0, 3 * chan),
        *[accumulator(1, 2 * chan)] * 2,
        accumulator(1, 16),
        accumulator(1, chan),
        accumulator(1, 3 * chan),
    )

    norm = 1.0 / (edge * edge)
    half = 3 * chan // 2
    rows = 3 * chan + half
    sums = total[...] * norm
    flat = jnp.concatenate(
        [
            sums[:, 2 * chan :],
            jnp.concatenate(
                [sums[0:half, chan : 2 * chan], sums[half:, chan : 2 * chan]], axis=1
            ),
        ],
        axis=0,
    )
    bias_sum = (bias_acc[:, 0:edge] + bias_acc[:, edge:]).T
    bias_sum = jnp.sum(bias_sum, axis=0, keepdims=True) * norm

    def coded(values, most):
        most = jnp.maximum(most, 1e-33)
        return jnp.round(values * (32767.0 / most)).astype(jnp.int32), most / 32767.0

    def largest(values):
        return jnp.max(jnp.max(jnp.abs(values), axis=0, keepdims=True), axis=1, keepdims=True)

    def side_row(bias, scale):
        return jnp.concatenate([bias, jnp.broadcast_to(scale, (1, 128 - chan))], axis=1)

    codes, scale = coded(flat, largest(flat))
    for index in range(n_own):
        have = min(max(rows - index * chunk, 0), chunk)
        values = [codes[index * chunk : index * chunk + have]] if have else []
        if have < chunk:
            values.append(jnp.zeros((chunk - have, 128), jnp.int32))
        values = jnp.concatenate(values, axis=0)
        part[index] = values.astype(jnp.int16)
    own_side[...] = side_row(bias_sum, scale)

    mine = me - first_own
    owner = (mine >= 0) & (mine < n_own)

    def remote(src, dst, send_sem, recv_sem, to):
        return pltpu.make_async_remote_copy(
            src_ref=src,
            dst_ref=dst,
            send_sem=send_sem,
            recv_sem=recv_sem,
            device_id=to,
            device_id_type=MESH,
        )

    def scatter(d):
        index = lax.rem(me + d, n_own)

        @pl.when(first_own + index != me)
        def _():
            to = device(first_own + index)
            remote(own_side, sides.at[me], side_send, side_recv, to).start()
            remote(part.at[index], reduced.at[me], rs_send, rs_recv, to).start()

    def gather(d):
        to = device(lax.rem(me + d, n_all))
        remote(full_side.at[mine], full_side.at[mine], full_send, full_recv, to).start()
        remote(full.at[mine], full.at[mine], ag_send, ag_recv, to).start()

    loop(0, n_own, scatter)

    @pl.when(owner)
    def _():
        reduced[me] = part[mine]
        sides[me] = own_side[...]
        await_bytes(sides.at[0 : n_all - 1], side_recv)
        await_bytes(reduced.at[0 : n_all - 1], rs_recv)

        def decoded(r):
            return reduced[r].astype(jnp.int32).astype(F32) * sides[r][:, 127:128]

        if n_all <= 16:
            own = sum(decoded(r) for r in range(n_all))
            bias = sum(sides[r] for r in range(n_all))
        else:
            own = lax.fori_loop(
                0, n_all, lambda r, x: x + decoded(r), jnp.zeros((chunk, 128), F32)
            )
            bias = lax.fori_loop(0, n_all, lambda r, x: x + sides[r], jnp.zeros((1, 128), F32))
        codes, scale = coded(own, largest(own))
        full[mine] = codes.astype(jnp.int16)
        full_side[mine] = side_row(bias[:, 0:chan], scale)
        loop(1, n_all, gather)
        if n_own > 1:
            await_bytes(full_side.at[0 : n_own - 1], full_recv)
            await_bytes(full.at[0 : n_own - 1], ag_recv)
            await_bytes(sides.at[0 : n_own - 1], side_send)
            await_bytes(part.at[0 : n_own - 1], rs_send)

    @pl.when(jnp.logical_not(owner))
    def _():
        await_bytes(full_side, full_recv)
        await_bytes(full, ag_recv)
        await_bytes(sides.at[0:n_own], side_send)
        await_bytes(part, rs_send)

    await_features(col_send, row_send, cedge_send, redge_send)

    @pl.when(owner)
    def _():
        await_bytes(sides.at[0 : n_all - 1], full_send)
        await_bytes(reduced.at[0 : n_all - 1], ag_send)


def finish(loss, gathered, side, loss_hbm, conv_grad_hbm, bias_hbm, full, conv_grad_out, bias_out, sem):
    n_all, chunk = gathered.shape[0:2]
    loss_copy = pltpu.make_async_copy(loss, loss_hbm, sem.at[0])
    loss_copy.start()

    def place(r):
        value = gathered[r].astype(jnp.int32).astype(F32) * side[r][:, 127:128]
        full[pl.ds(r * chunk, chunk), :] = value

    loop(0, n_all, place)
    chan = bias_out.shape[1]
    half = 3 * chan // 2
    rows = 3 * chan + half
    for b in range(3):
        low = b * chan
        conv_grad_out[1, b] = full[low : low + chan, 0:chan]
        conv_grad_out[0, b] = full[low : low + chan, chan : 2 * chan]
    low = 3 * chan
    conv_grad_out[2, 0] = full[low : low + chan, 0:chan]
    conv_grad_out[2, 1, 0 : half - chan] = full[low + chan : low + half, 0:chan]
    conv_grad_out[2, 1, half - chan :] = full[low : low + 2 * chan - half, chan : 2 * chan]
    conv_grad_out[2, 2] = full[low + 2 * chan - half : low + half, chan : 2 * chan]
    bias_out[...] = side[0][:, 0:chan]
    grad_copy = pltpu.make_async_copy(conv_grad_out, conv_grad_hbm, sem.at[1])
    bias_copy = pltpu.make_async_copy(bias_out, bias_hbm, sem.at[2])
    grad_copy.start()
    bias_copy.start()
    loss_copy.wait()
    grad_copy.wait()
    bias_copy.wait()


def solution(mesh):
    n_row, n_col, n_rep = (mesh.shape[axis] for axis in ("row", "col", "rep"))
    n_all = n_row * n_col * n_rep

    def per_device(
        emb_row,
        emb_col,
        proj_row,
        proj_col,
        pair_out,
        pair_bias,
        conv_weight,
        conv_bias,
        target,
        kept_tiles,
    ):
        chan, edge = target.shape[0], target.shape[1]
        rank = pair_out.shape[0]
        pairs = edge // 2
        used = 3 * chan + 3 * chan // 2
        inner = n_row // 2 if n_row >= 4 else n_row
        n_own = inner * n_col * n_rep
        first_own = (n_row - inner) // 2 * n_col * n_rep
        chunk = 8 * pl.cdiv(used, 8 * n_own)

        dma = pltpu.SemaphoreType.DMA
        vmem = pl.BlockSpec(memory_space=pltpu.VMEM)
        hbm = pl.BlockSpec(memory_space=pltpu.HBM)
        results = pl.pallas_call(
            functools.partial(
                kernel, (n_row, n_col, n_rep, edge, chan, n_own, first_own, chunk)
            ),
            out_shape=(
                pltpu.VMEM((edge, edge), F32),
                pltpu.VMEM((n_own, chunk, 128), jnp.int16),
                pltpu.VMEM((n_own, 1, 128), F32),
            ),
            in_specs=[hbm] * 9 + [pl.BlockSpec(memory_space=pltpu.SMEM)],
            out_specs=(vmem,) * 3,
            scratch_shapes=[
                pltpu.VMEM(emb_row.shape, BF16),
                pltpu.VMEM(emb_col.shape[::-1], BF16),
                pltpu.VMEM(proj_row.shape[::-1], BF16),
                pltpu.VMEM(proj_col.shape[::-1], BF16),
                pltpu.VMEM(conv_weight.shape, BF16),
                pltpu.VMEM(pair_out.shape, BF16),
                pltpu.VMEM((1, chan), F32),
                pltpu.VMEM((1, chan), F32),
                dma((8,)),
                pltpu.VMEM((2, 2, 2 * rank), F32),
                pltpu.VMEM((2, 1, 2 * rank), F32),
                pltpu.VMEM((n_col, rank + 16, edge), BF16),
                pltpu.VMEM((2, n_col, 2, 2 * rank), F32),
                pltpu.VMEM((n_row, rank, edge), BF16),
                pltpu.VMEM((2, n_row, 1, 2 * rank), F32),
                pltpu.VMEM((edge + 16, rank), F32),
                pltpu.VMEM((edge + 16, rank), F32),
                pltpu.VMEM((pairs + 8, 2 * rank), F32),
                pltpu.VMEM((256, 256), BF16),
                pltpu.VMEM((3, 2 * edge, 2 * edge), BF16),
                pltpu.VMEM((3 * chan, 4 * chan), BF16),
                pltpu.VMEM((chan, edge, edge), BF16),
                pltpu.VMEM((pairs * chan, 2 * edge), BF16),
                pltpu.VMEM((16 * 3 * chan, 2 * edge), BF16),
                pltpu.VMEM((16 * chan, 2 * edge), F32),
                pltpu.VMEM((16 * chan, 2 * edge), BF16),
                pltpu.VMEM((3 * chan, 3 * chan), F32),
                pltpu.VMEM((3 * chan, 4 * chan), F32),
                pltpu.VMEM((chan, 2 * edge), F32),
                pltpu.VMEM((16, 128), F32),
                pltpu.VMEM((n_own, chunk, 128), jnp.int16),
                pltpu.VMEM((n_all, chunk, 128), jnp.int16),
                pltpu.VMEM((1, 128), F32),
                pltpu.VMEM((n_all, 1, 128), F32),
                *[pltpu.SemaphoreType.DMA] * 17,
            ],
            compiler_params=pltpu.CompilerParams(collective_id=0, has_side_effects=True),
            name="pair_step",
        )(
            emb_row,
            emb_col.T,
            proj_row.T,
            proj_col.T,
            pair_out,
            pair_bias.reshape(1, chan),
            conv_weight,
            conv_bias.reshape(1, chan),
            target,
            kept_tiles,
        )
        loss, grads, bias = pl.pallas_call(
            finish,
            out_shape=(
                jax.ShapeDtypeStruct((edge, edge), F32),
                jax.ShapeDtypeStruct((3, 3, chan, chan), F32),
                jax.ShapeDtypeStruct((1, chan), F32),
            ),
            in_specs=[vmem] * 3,
            out_specs=(hbm,) * 3,
            scratch_shapes=[
                pltpu.VMEM((n_own * chunk, 128), F32),
                pltpu.VMEM((3, 3, chan, chan), F32),
                pltpu.VMEM((1, chan), F32),
                dma((3,)),
            ],
            name="finish",
        )(
            *(pltpu.with_memory_space_constraint(x, pltpu.VMEM) for x in results)
        )
        return loss, grads, bias.reshape(chan)

    in_specs = (
        P(("grp", "row", "rep"), "col"),
        P(("grp", "col"), "row"),
        P(),
        P(),
        P(),
        P(),
        P(),
        P(),
        P(None, ("grp", "row", "rep"), "col"),
        P(("grp", "row", "rep"), "col"),
    )
    out_specs = (P(("grp", "row", "rep"), "col"), P("grp", None, None, None), P("grp"))
    return jax.shard_map(
        per_device, mesh=mesh, in_specs=in_specs, out_specs=out_specs, check_vma=False
    )
```

```python
import functools

import jax
import jax.numpy as jnp
from jax import lax
from jax.experimental import pallas as pl
from jax.experimental.pallas import tpu as pltpu
from jax.sharding import PartitionSpec as P

MESH = pl.DeviceIdType.MESH
F32 = jnp.float32
BF16 = jnp.bfloat16
NT = (((1,), (1,)), ((), ()))


def loop(low, high, body):
    if high - low <= 16:
        for d in range(low, high):
            body(d)
    else:
        lax.fori_loop(low, high, lambda d, _: (body(d), 0)[1], 0)


def window_of(everything, width, index, count):
    if width % 128 == 0:
        return index * width, width, 0
    offset = max(i * width % 128 for i in range(count))
    window = min(-(-(offset + width) // 128) * 128, everything)
    tile = lax.div(index * width, 128)
    if any(i * width // 128 * 128 + window > everything for i in range(count)):
        tile = jnp.minimum(tile, (everything - window) // 128)
    return tile * 128, window, index * width - tile * 128


def columns(ref, width, shift):
    window = ref.shape[1]
    if width % 128 == 0:
        return ref[...]
    value = pltpu.roll(ref[...].astype(F32), lax.rem(window - shift, window), 1)
    lane = lax.broadcasted_iota(jnp.int32, value.shape, 1)
    return jnp.where(lane < width, value, 0.0).astype(BF16)


def padded(value, square):
    if all(have == 256 or have % 128 == 0 for have in value.shape):
        for axis in range(2):
            if value.shape[axis] < 256:
                blank = list(value.shape)
                blank[axis] = 256 - blank[axis]
                value = jnp.concatenate([value, jnp.zeros(blank, BF16)], axis=axis)
        return value
    square[...] = jnp.zeros_like(square)
    square[0 : value.shape[0], 0 : value.shape[1]] = value
    return square[...]


def wide_tile(value, low):
    value = value[:, low : low + 256]
    if value.shape[1] < 256:
        blank = jnp.zeros((value.shape[0], 256 - value.shape[1]), BF16)
        value = jnp.concatenate([value, blank], axis=1)
    return value


def kernel(
    sizes,
    emb_row_hbm,
    emb_col_hbm,
    proj_row_hbm,
    proj_col_hbm,
    pair_out_hbm,
    pair_bias_hbm,
    conv_weight_hbm,
    conv_bias_hbm,
    target,
    kept,
    loss_out,
    full,
    full_side,
    emb_row,
    emb_col,
    proj_row,
    proj_col,
    conv_weight,
    pair_out,
    pair_bias,
    conv_bias,
    in_sem,
    rowtail,
    coltail,
    rowbuf,
    rowedge,
    colbuf,
    coledge,
    row_feat,
    col_wide,
    feat_pairs,
    square,
    wide,
    weight_t,
    target_in,
    aims,
    hid,
    base,
    grad_in,
    weight_f,
    total,
    bias_acc,
    part,
    reduced,
    own_side,
    sides,
    target_sem,
    row_send,
    row_recv,
    redge_send,
    redge_recv,
    col_send,
    col_recv,
    cedge_send,
    cedge_recv,
    rs_send,
    rs_recv,
    ag_send,
    ag_recv,
    side_send,
    side_recv,
    full_send,
    full_recv,
):
    n_row, n_col, n_rep, edge, chan, n_own, first_own, chunk = sizes
    n_all = n_row * n_col * n_rep
    pairs = edge // 2
    row, col, rep = lax.axis_index("row"), lax.axis_index("col"), lax.axis_index("rep")
    line = row * n_rep + rep
    n_line = n_row * n_rep
    me = line * n_col + col

    def device(index):
        across = lax.rem(index, n_col)
        along = lax.div(index, n_col)
        return {"row": lax.div(along, n_rep), "rep": lax.rem(along, n_rep), "col": across}

    def wrapped(index, count):
        return jnp.where(index >= count, index - count, index)

    def far(k):
        down, up = n_row - 1 - k, k
        down = down - (down <= row).astype(jnp.int32)
        up = up + (up >= row).astype(jnp.int32)
        return jnp.where(2 * row < n_row, down, up)

    def await_bytes(ref, sem):
        pltpu.make_async_copy(ref, ref, sem).wait()

    col_width, row_width = emb_col.shape[0], emb_row.shape[1]
    everything = proj_col_hbm.shape[1]
    col_low, col_window, col_shift = window_of(everything, col_width, row, n_row)
    row_low, row_window, row_shift = window_of(everything, row_width, col, n_col)

    def lanes(low, window):
        return pl.ds(pl.multiple_of(low, 128), window)

    inputs = [
        pltpu.make_async_copy(src, dst, in_sem.at[i])
        for i, (src, dst) in enumerate(
            (
                (emb_col_hbm, emb_col),
                (proj_col_hbm.at[:, lanes(col_low, col_window)], proj_col),
                (emb_row_hbm, emb_row),
                (proj_row_hbm.at[:, lanes(row_low, row_window)], proj_row),
                (conv_weight_hbm, conv_weight),
                (pair_out_hbm, pair_out),
                (pair_bias_hbm, pair_bias),
                (conv_bias_hbm, conv_bias),
            )
        )
    ]
    for copy in inputs:
        copy.start()
    barrier = pltpu.get_barrier_semaphore()

    def greet(to):
        pl.semaphore_signal(barrier, inc=1, device_id=to, device_id_type=MESH)

    if n_all <= 16:
        for k in range(n_row):
            for c in range(n_col - 1, -1, -1):
                for r in range(n_rep - 1, -1, -1):
                    if k < n_row - 1 or c + r > 0:
                        greet(
                            {
                                "row": far(k) if k < n_row - 1 else row,
                                "col": wrapped(col + c, n_col),
                                "rep": wrapped(rep + r, n_rep),
                            }
                        )
    else:
        loop(1, n_all, lambda d: greet(device(lax.rem(me + d, n_all))))


    def rounded(x):
        return x.astype(BF16).astype(F32)

    rank = proj_row.shape[0]
    ends = ((edge - 2, edge - 1), (0, 1))
    fetch = pltpu.make_async_copy(target, target_in, target_sem)

    def pair_row(values, at):
        return jnp.concatenate([values[r : r + 1] for r in at], axis=1)

    def row_copy(d, src):
        return pltpu.make_async_remote_copy(
            src_ref=rowbuf.at[src],
            dst_ref=rowbuf.at[src],
            send_sem=row_send,
            recv_sem=row_recv,
            device_id={"col": lax.rem(col + d, n_col)},
            device_id_type=MESH,
        )

    def redge_copy(side, d, src):
        to = lax.rem(line + (1 if side == 0 else n_line - 1), n_line)
        return pltpu.make_async_remote_copy(
            src_ref=rowtail.at[side],
            dst_ref=rowedge.at[side, src],
            send_sem=redge_send,
            recv_sem=redge_recv,
            device_id={
                "row": lax.div(to, n_rep),
                "rep": lax.rem(to, n_rep),
                "col": lax.rem(col + d, n_col),
            },
            device_id_type=MESH,
        )

    def col_copy(k, src):
        return pltpu.make_async_remote_copy(
            src_ref=colbuf.at[src],
            dst_ref=colbuf.at[src],
            send_sem=col_send,
            recv_sem=col_recv,
            device_id={"row": far(k)},
            device_id_type=MESH,
        )

    def cedge_copy(side, d, src):
        to = lax.rem(col + (1 if side == 0 else n_col - 1), n_col)
        return pltpu.make_async_remote_copy(
            src_ref=coltail.at[side],
            dst_ref=coledge.at[side, src],
            send_sem=cedge_send,
            recv_sem=cedge_recv,
            device_id={"row": lax.rem(row + d, n_row), "col": to},
            device_id_type=MESH,
        )

    for copy in inputs[0:2]:
        copy.wait()
    fetch.start()

    def project_col(col_sum):
        left = columns(proj_col, col_width, col_shift)
        for low in range(0, col_width, 256):
            right = padded(emb_col[low : min(low + 256, col_width), :], square)
            pltpu.matmul_push_rhs(right, 0, 0)
            pltpu.matmul_acc_lhs(col_sum, wide_tile(left, low), load_staged_rhs=0)
        return pltpu.matmul_pop(col_sum)[:, 0:edge]

    def project_row(row_sum):
        left = columns(proj_row, row_width, row_shift)
        for low in range(0, row_width, 256):
            right = padded(emb_row[:, low : min(low + 256, row_width)], square)
            pltpu.matmul_push_rhs(right, 0, 1, transpose=True)
            pltpu.matmul_acc_lhs(row_sum, wide_tile(left, low), load_staged_rhs=0)
        return pltpu.matmul_pop(row_sum)[:, 0:edge]

    part_col = pl.run_scoped(project_col, pltpu.ACC(0)((rank, 256), F32))
    colbuf[row] = part_col.astype(BF16)
    pl.semaphore_wait(barrier, n_all - 1)
    loop(0, n_row - 1, lambda k: col_copy(k, row).start())
    turned = rounded(part_col).T
    for side in range(2):
        coltail[side] = pair_row(turned, ends[side])
    for side in range(2):
        loop(0, n_row, lambda d: cedge_copy(side, d, row).start())

    for copy in inputs[2:4]:
        copy.wait()
    part_row = pl.run_scoped(project_row, pltpu.ACC(1)((rank, 256), F32))
    keep = kept[0, 0].astype(F32)
    rowbuf[col, 0:rank, :] = part_row.astype(BF16)
    rowbuf[col, rank:, :] = jnp.full((16, edge), keep, F32).astype(BF16)
    loop(1, n_col, lambda d: row_copy(d, col).start())
    turned = rounded(part_row).T
    for side in range(2):
        rowtail[side, 0:1] = pair_row(turned, ends[side])
        rowtail[side, 1:2] = jnp.full((1, 2 * rank), keep, F32)
    for side in range(2):
        loop(0, n_col, lambda d: redge_copy(side, d, col).start())

    def await_features(col_sem, row_sem, cedge_sem, redge_sem):
        await_bytes(coledge, cedge_sem)
        if n_row > 1:
            await_bytes(colbuf.at[0 : n_row - 1], col_sem)
        await_bytes(rowedge, redge_sem)
        if n_col > 1:
            await_bytes(rowbuf.at[0 : n_col - 1], row_sem)

    fetch.wait()
    for copy in inputs[4:]:
        copy.wait()

    def lay(i, _):
        for low in range(0, chan, 16):
            block = target_in[low : low + 16, pl.ds(pl.multiple_of(i * 16, 16), 16), :]
            block = jnp.swapaxes(block.astype(F32), 0, 1)
            for r in range(16):
                start = pl.multiple_of((i * 8 + r // 2) * chan + low, 16)
                lanes = slice(r % 2 * edge, (r % 2 + 1) * edge)
                aims[pl.ds(start, 16), lanes] = block[r].astype(BF16)
        return 0

    lax.fori_loop(0, edge // 16, lay, 0)
    for a in range(3):
        for b in range(3):
            weight_f[b * chan : (b + 1) * chan, a * chan : (a + 1) * chan] = conv_weight[
                a, b
            ].astype(F32)
    turned = weight_f[...].T
    eye = lax.broadcasted_iota(jnp.int32, (chan, chan), 0) == lax.broadcasted_iota(
        jnp.int32, (chan, chan), 1
    )
    none = jnp.zeros((chan, chan), F32)
    minus = jnp.concatenate([none, jnp.where(eye, -1.0, 0.0), none], axis=0)
    weight_t[...] = jnp.concatenate([turned, minus], axis=1).astype(BF16)
    out_t = pair_out[...].astype(F32).T
    out_t = jnp.concatenate([out_t, out_t], axis=1)
    pair_b = jnp.broadcast_to(pair_bias[...], (128, chan)).T
    conv_b = jnp.broadcast_to(conv_bias[...], (128, chan)).T
    term = lax.broadcasted_iota(jnp.int32, (chan, 128), 1)
    second = pair_b - rounded(pair_b)
    third = second - rounded(second)
    bias_terms = jnp.where(
        term == 0,
        pair_b,
        jnp.where(term == 1, second, jnp.where(term == 2, third, 0.0)),
    ).astype(BF16)
    bias_acc[...] = jnp.zeros_like(bias_acc)

    await_features(col_recv, row_recv, cedge_recv, redge_recv)

    def summed(terms):
        return sum(x.astype(F32) for x in terms)

    def unpack(target, values, low):
        for r in range(2):
            target[low + r : low + r + 1, :] = values[:, r * rank : (r + 1) * rank]

    for side, low in ((0, 6), (1, edge + 8)):
        edge_sum = rounded(summed(rowedge[side, c, 0:1, :] for c in range(n_col)))
        unpack(row_feat, edge_sum, low)
        unpack(col_wide, summed(coledge[side, r] for r in range(n_row)), low)
    row_feat[8 : edge + 8, :] = rounded(summed(rowbuf[c, 0:rank, :] for c in range(n_col))).T
    col_wide[8 : edge + 8, :] = summed(colbuf[r] for r in range(n_row)).T
    feat_pairs[0 : pairs + 2, :] = jnp.concatenate(
        [row_feat[pl.ds(6 + r, pairs + 2, stride=2), :] for r in range(2)], axis=1
    )

    lane = lax.broadcasted_iota(jnp.int32, (1, edge), 1)
    before, after = lax.rem(col + n_col - 1, n_col), lax.rem(col + 1, n_col)
    has_before = (col > 0).astype(F32)
    has_after = (col < n_col - 1).astype(F32)

    def masks(get, valid):
        here, left, right = (
            jnp.broadcast_to(get(c), (1, edge)) * scale
            for c, scale in ((col, valid), (before, valid * has_before), (after, valid * has_after))
        )
        return (jnp.where(lane < 2, left, here), here, jnp.where(lane >= edge - 2, right, here))

    top = masks(lambda c: rowedge[0, c, 1:2, 0:1], (line > 0).astype(F32))
    middle = masks(lambda c: rowbuf[c, rank:, 0:1].astype(F32)[0:1], jnp.float32(1))
    bottom = masks(lambda c: rowedge[1, c, 1:2, 0:1], (line < n_line - 1).astype(F32))

    shifted = [col_wide[6 + 2 * b : 6 + 2 * b + edge, :].T for b in range(3)]
    first_rows = lax.broadcasted_iota(jnp.int32, (2 * edge - 2 * rank, 2 * edge), 0) < 3

    def operand(b, mask):
        value = shifted[b] * mask
        blank = jnp.zeros_like(value)
        ones = jnp.where(first_rows, jnp.concatenate([mask, mask], axis=1), 0.0)
        return jnp.concatenate(
            [
                jnp.concatenate([value, blank], axis=1),
                jnp.concatenate([blank, value], axis=1),
                ones,
            ],
            axis=0,
        ).astype(BF16)

    for b in range(3):
        wide[b] = operand(b, middle[b])

    def scaled(p, count):
        low = (out_t * feat_pairs[pl.ds(p + 1 + r, 1), :] for r in range(count))
        low = jnp.concatenate([x.astype(BF16) for x in low], axis=0)
        return jnp.concatenate([low, jnp.concatenate([bias_terms] * count, axis=0)], axis=1)

    conv_b = jnp.concatenate([conv_b, conv_b], axis=1)
    blank = jnp.zeros((chan, 2 * edge), BF16)

    def slot(offset, first=0, count=1, of=1):
        low = (offset % 16 * of + first) * chan
        return slice(low, low + count * chan)

    def inside(p, offset):
        return not isinstance(p, int) or 0 <= p + offset < pairs

    def finish_pair(p, offset, conv):
        differ = (base[slot(offset), :] + conv) * keep
        grad_in[slot(offset), :] = differ.astype(BF16)
        bias_acc[...] += differ
        loss = 0.5 * jnp.sum(differ * differ, axis=0, keepdims=True)
        at = 2 * (p + offset)
        loss_out[pl.ds(at, 1), :] = loss[:, 0:edge]
        loss_out[pl.ds(at + 1, 1), :] = loss[:, edge : 2 * edge]

    def main(*accs):
        sums, grads, halo, features_of = accs[0:4], accs[4:6], accs[6], (accs[7:10], accs[10:16])
        stage, primed = [0, 0], [False, False]

        def halo_item(p, offset, b, mask):
            def push(at):
                pltpu.matmul_push_rhs(operand(b, mask[b]), at, 1)

            def go(at):
                pltpu.matmul_acc_lhs(halo, scaled(p + offset, 1), load_staged_rhs=at)
                value = jnp.maximum(pltpu.matmul_pop(halo), 0.0)
                hid[slot(offset, b, 1, 3), :] = value.astype(BF16)

            return push, go, None, 4

        def feature_item(unit, b, p, offset, acc, memo):
            def push(at):
                pltpu.matmul_push_rhs(wide[b], at, unit)

            def go(at):
                if offset not in memo:
                    memo[offset] = scaled(p + offset, 2)
                pltpu.matmul_acc_lhs(acc, memo[offset], load_staged_rhs=at)

            def after():
                value = pltpu.matmul_pop(acc)
                for r in range(2):
                    own = value[r * chan : (r + 1) * chan]
                    hid[slot(offset + r, b, 1, 3), :] = jnp.maximum(own, 0.0).astype(BF16)
                    if b == 1:
                        base[slot(offset + r), :] = own + conv_b

            return push, go, after, 8

        def conv_item(p, offset):
            taps = [a for a in range(3) if inside(p, offset + 1 - a)]

            def push(at):
                aim = blank
                if inside(p, offset):
                    aim = aims[pl.ds(pl.multiple_of((p + offset) * chan, chan), chan), :]
                right = jnp.concatenate([hid[slot(offset, 0, 3, 3), :], aim], axis=0)
                pltpu.matmul_push_rhs(right, at, 0)

            def go(at):
                for a in taps:
                    pltpu.matmul_acc_lhs(
                        sums[(offset + 1 - a) % 4],
                        weight_t[a * chan : (a + 1) * chan, :],
                        load_staged_rhs=at,
                    )
                    at = None

            def after():
                if 2 in taps:
                    finish_pair(p, offset - 1, pltpu.matmul_pop(sums[(offset - 1) % 4]))

            return push, go, after, 4 * len(taps)

        def grad_item(unit, p, offset):
            def push(at):
                right = [
                    grad_in[slot(offset + k), :] if inside(p, offset + k) else blank
                    for k in range(-2, 2)
                ]
                right = jnp.concatenate(right, axis=0)
                pltpu.matmul_push_rhs(right, at, unit, transpose=True)

            def go(at):
                left = hid[slot(offset, 0, 3, 3), :]
                pltpu.matmul_acc_lhs(grads[unit], left, load_staged_rhs=at)

            return push, go, None, 12

        def run(queues, follow=(None, None)):
            spent, at, waiting = [0, 0], [0, 0], []
            for unit in range(2):
                if queues[unit] and not primed[unit]:
                    queues[unit][0][0](stage[unit])
                primed[unit] = False
            while any(at[u] < len(queues[u]) for u in range(2)):
                unit = min(
                    (u for u in range(2) if at[u] < len(queues[u])), key=lambda u: spent[u]
                )
                queue, index = queues[unit], at[unit]
                _, go, after, cost = queue[index]
                while len(waiting) > 1:
                    waiting.pop(0)()
                go(stage[unit])
                stage[unit] = 1 - stage[unit]
                if index + 1 < len(queue):
                    queue[index + 1][0](stage[unit])
                at[unit] += 1
                spent[unit] += cost
                if after is not None:
                    waiting.append(after)
            for after in waiting:
                after()
            for unit in range(2):
                if follow[unit] is not None:
                    follow[unit][0](stage[unit])
                    primed[unit] = True

        def features(p, low, units=(1, 1)):
            items = []
            for half, unit in enumerate(units):
                memo = {}
                held = features_of[unit][3 * half * unit : 3 * half * unit + 3]
                items.append(
                    [
                        feature_item(unit, b, p, low + 2 * half, held[b], memo)
                        for b in range(3)
                    ]
                )
            return items

        def convs(p, low, high):
            return [conv_item(p, r) for r in range(low, high)]

        def turns(unit, p, *offsets):
            return [grad_item(unit, p, r) for r in offsets]

        def group(p, low):
            early, late = features(p, low)
            conv = convs(p, low - 4, low)
            run(
                (
                    turns(0, p, low - 12) + conv[0:2] + turns(0, p, low - 10) + conv[2:4],
                    turns(1, p, low - 11) + early + turns(1, p, low - 9) + late,
                ),
                [turns(u, p, low - 8 + u)[0] for u in range(2)],
            )

        early, late = features(0, 0, (1, 0))
        first = convs(0, -1, 4)
        second = features(0, 4)
        run((late, [halo_item(0, -1, b, top) for b in range(3)] + early), (first[0], second[0][0]))
        third, fourth = convs(0, 4, 8), features(0, 8)
        run((first, second[0] + second[1]), (third[0], fourth[0][0]))
        fifth, sixth = convs(0, 8, 12), features(0, 12)
        run((third, fourth[0] + turns(1, 0, -1) + fourth[1]), (fifth[0], sixth[0][0]))
        run(
            (
                fifth[0:2] + turns(0, 0, 0) + fifth[2:4] + turns(0, 0, 2),
                sixth[0] + turns(1, 0, 1) + sixth[1] + turns(1, 0, 3),
            ),
            [turns(u, 0, 4 + u)[0] for u in range(2)],
        )

        def step(t, _):
            p = pl.multiple_of(t * 16, 16)
            for k in range(4):
                group(p, 4 * k)
            return 0

        lax.fori_loop(1, pairs // 16, step, 0)
        last = convs(pairs, -4, 1)
        run(
            (
                turns(0, pairs, -12) + last[0:2] + turns(0, pairs, -10) + last[2:4],
                turns(1, pairs, -11)
                + [halo_item(pairs, 0, b, bottom) for b in range(3)]
                + turns(1, pairs, -9, -8, -7),
            ),
            (last[4], turns(1, pairs, -6)[0]),
        )
        run((last[4:] + turns(0, pairs, -5, -4), turns(1, pairs, -6, -3)))
        run((turns(0, pairs, -2, 0), turns(1, pairs, -1)))
        total[...] = pltpu.matmul_pop(grads[0]) + pltpu.matmul_pop(grads[1])

    def accumulator(unit, rows_of):
        return pltpu.ACC(unit)((rows_of, 2 * edge), F32)

    pl.run_scoped(
        main,
        *[accumulator(0, chan)] * 4,
        *[accumulator(unit, 3 * chan) for unit in range(2)],
        accumulator(1, chan),
        *[accumulator(0, 2 * chan)] * 3,
        *[accumulator(1, 2 * chan)] * 6,
    )

    norm = 1.0 / (edge * edge)
    half = 3 * chan // 2
    rows = 3 * chan + half
    sums = total[...] * norm
    flat = jnp.concatenate(
        [
            sums[:, 2 * chan :],
            jnp.concatenate(
                [sums[0:half, chan : 2 * chan], sums[half:, chan : 2 * chan]], axis=1
            ),
        ],
        axis=0,
    )
    bias_sum = (bias_acc[:, 0:edge] + bias_acc[:, edge:]).T
    bias_sum = jnp.sum(bias_sum, axis=0, keepdims=True) * norm

    def coded(values, most):
        most = jnp.maximum(most, 1e-33)
        return jnp.round(values * (32767.0 / most)).astype(jnp.int32), most / 32767.0

    def largest(values):
        return jnp.max(jnp.max(jnp.abs(values), axis=0, keepdims=True), axis=1, keepdims=True)

    def side_row(bias, scale):
        return jnp.concatenate([bias, jnp.broadcast_to(scale, (1, 128 - chan))], axis=1)

    codes, scale = coded(flat, largest(flat))
    for index in range(n_own):
        have = min(max(rows - index * chunk, 0), chunk)
        values = [codes[index * chunk : index * chunk + have]] if have else []
        if have < chunk:
            values.append(jnp.zeros((chunk - have, 128), jnp.int32))
        values = jnp.concatenate(values, axis=0)
        part[index] = values.astype(jnp.int16)
    own_side[...] = side_row(bias_sum, scale)

    mine = me - first_own
    owner = (mine >= 0) & (mine < n_own)

    def remote(src, dst, send_sem, recv_sem, to):
        return pltpu.make_async_remote_copy(
            src_ref=src,
            dst_ref=dst,
            send_sem=send_sem,
            recv_sem=recv_sem,
            device_id=to,
            device_id_type=MESH,
        )

    def scatter(d):
        index = lax.rem(me + d, n_own)

        @pl.when(first_own + index != me)
        def _():
            to = device(first_own + index)
            remote(part.at[index], reduced.at[me], rs_send, rs_recv, to).start()
            remote(own_side, sides.at[me], side_send, side_recv, to).start()

    def gather(d):
        to = device(lax.rem(me + d, n_all))
        remote(full.at[mine], full.at[mine], ag_send, ag_recv, to).start()
        remote(full_side.at[mine], full_side.at[mine], full_send, full_recv, to).start()

    loop(0, n_own, scatter)

    @pl.when(owner)
    def _():
        reduced[me] = part[mine]
        sides[me] = own_side[...]
        await_bytes(sides.at[0 : n_all - 1], side_recv)
        await_bytes(reduced.at[0 : n_all - 1], rs_recv)

        def decoded(r):
            return reduced[r].astype(jnp.int32).astype(F32) * sides[r][:, 127:128]

        if n_all <= 16:
            own = sum(decoded(r) for r in range(n_all))
            bias = sum(sides[r] for r in range(n_all))
        else:
            own = lax.fori_loop(
                0, n_all, lambda r, x: x + decoded(r), jnp.zeros((chunk, 128), F32)
            )
            bias = lax.fori_loop(0, n_all, lambda r, x: x + sides[r], jnp.zeros((1, 128), F32))
        codes, scale = coded(own, largest(own))
        full[mine] = codes.astype(jnp.int16)
        full_side[mine] = side_row(bias[:, 0:chan], scale)
        loop(1, n_all, gather)
        if n_own > 1:
            await_bytes(full_side.at[0 : n_own - 1], full_recv)
            await_bytes(full.at[0 : n_own - 1], ag_recv)
            await_bytes(sides.at[0 : n_own - 1], side_send)
            await_bytes(part.at[0 : n_own - 1], rs_send)

    @pl.when(jnp.logical_not(owner))
    def _():
        await_bytes(full_side, full_recv)
        await_bytes(full, ag_recv)
        await_bytes(sides.at[0:n_own], side_send)
        await_bytes(part, rs_send)

    await_features(col_send, row_send, cedge_send, redge_send)

    @pl.when(owner)
    def _():
        await_bytes(sides.at[0 : n_all - 1], full_send)
        await_bytes(reduced.at[0 : n_all - 1], ag_send)


def finish(loss, gathered, side, loss_hbm, conv_grad_hbm, bias_hbm, full, conv_grad_out, bias_out, sem):
    n_all, chunk = gathered.shape[0:2]
    loss_copy = pltpu.make_async_copy(loss, loss_hbm, sem.at[0])
    loss_copy.start()

    def place(r):
        value = gathered[r].astype(jnp.int32).astype(F32) * side[r][:, 127:128]
        full[pl.ds(r * chunk, chunk), :] = value

    loop(0, n_all, place)
    chan = bias_out.shape[1]
    half = 3 * chan // 2
    rows = 3 * chan + half
    for b in range(3):
        low = b * chan
        conv_grad_out[1, b] = full[low : low + chan, 0:chan]
        conv_grad_out[0, b] = full[low : low + chan, chan : 2 * chan]
    low = 3 * chan
    conv_grad_out[2, 0] = full[low : low + chan, 0:chan]
    conv_grad_out[2, 1, 0 : half - chan] = full[low + chan : low + half, 0:chan]
    conv_grad_out[2, 1, half - chan :] = full[low : low + 2 * chan - half, chan : 2 * chan]
    conv_grad_out[2, 2] = full[low + 2 * chan - half : low + half, chan : 2 * chan]
    bias_out[...] = side[0][:, 0:chan]
    grad_copy = pltpu.make_async_copy(conv_grad_out, conv_grad_hbm, sem.at[1])
    bias_copy = pltpu.make_async_copy(bias_out, bias_hbm, sem.at[2])
    grad_copy.start()
    bias_copy.start()
    loss_copy.wait()
    grad_copy.wait()
    bias_copy.wait()


def solution(mesh):
    n_row, n_col, n_rep = (mesh.shape[axis] for axis in ("row", "col", "rep"))
    n_all = n_row * n_col * n_rep

    def per_device(
        emb_row,
        emb_col,
        proj_row,
        proj_col,
        pair_out,
        pair_bias,
        conv_weight,
        conv_bias,
        target,
        kept_tiles,
    ):
        chan, edge = target.shape[0], target.shape[1]
        rank = pair_out.shape[0]
        pairs = edge // 2
        used = 3 * chan + 3 * chan // 2
        inner = n_row // 2 if n_row >= 4 else n_row
        n_own = inner * n_col * n_rep
        first_own = (n_row - inner) // 2 * n_col * n_rep
        chunk = 8 * pl.cdiv(used, 8 * n_own)

        def window(width, count):
            return window_of(proj_row.shape[0], width, 0, count)[1]

        dma = pltpu.SemaphoreType.DMA
        vmem = pl.BlockSpec(memory_space=pltpu.VMEM)
        hbm = pl.BlockSpec(memory_space=pltpu.HBM)
        results = pl.pallas_call(
            functools.partial(
                kernel, (n_row, n_col, n_rep, edge, chan, n_own, first_own, chunk)
            ),
            out_shape=(
                pltpu.VMEM((edge, edge), F32),
                pltpu.VMEM((n_own, chunk, 128), jnp.int16),
                pltpu.VMEM((n_own, 1, 128), F32),
            ),
            in_specs=[hbm] * 9 + [pl.BlockSpec(memory_space=pltpu.SMEM)],
            out_specs=(vmem,) * 3,
            scratch_shapes=[
                pltpu.VMEM(emb_row.shape, BF16),
                pltpu.VMEM(emb_col.shape[::-1], BF16),
                pltpu.VMEM((rank, window(emb_row.shape[1], n_col)), BF16),
                pltpu.VMEM((rank, window(emb_col.shape[1], n_row)), BF16),
                pltpu.VMEM(conv_weight.shape, BF16),
                pltpu.VMEM(pair_out.shape, BF16),
                pltpu.VMEM((1, chan), F32),
                pltpu.VMEM((1, chan), F32),
                dma((8,)),
                pltpu.VMEM((2, 2, 2 * rank), F32),
                pltpu.VMEM((2, 1, 2 * rank), F32),
                pltpu.VMEM((n_col, rank + 16, edge), BF16),
                pltpu.VMEM((2, n_col, 2, 2 * rank), F32),
                pltpu.VMEM((n_row, rank, edge), BF16),
                pltpu.VMEM((2, n_row, 1, 2 * rank), F32),
                pltpu.VMEM((edge + 16, rank), F32),
                pltpu.VMEM((edge + 16, rank), F32),
                pltpu.VMEM((pairs + 8, 2 * rank), F32),
                pltpu.VMEM((256, 256), BF16),
                pltpu.VMEM((3, 2 * edge, 2 * edge), BF16),
                pltpu.VMEM((3 * chan, 4 * chan), BF16),
                pltpu.VMEM((chan, edge, edge), BF16),
                pltpu.VMEM((pairs * chan, 2 * edge), BF16),
                pltpu.VMEM((16 * 3 * chan, 2 * edge), BF16),
                pltpu.VMEM((16 * chan, 2 * edge), F32),
                pltpu.VMEM((16 * chan, 2 * edge), BF16),
                pltpu.VMEM((3 * chan, 3 * chan), F32),
                pltpu.VMEM((3 * chan, 4 * chan), F32),
                pltpu.VMEM((chan, 2 * edge), F32),
                pltpu.VMEM((n_own, chunk, 128), jnp.int16),
                pltpu.VMEM((n_all, chunk, 128), jnp.int16),
                pltpu.VMEM((1, 128), F32),
                pltpu.VMEM((n_all, 1, 128), F32),
                *[pltpu.SemaphoreType.DMA] * 17,
            ],
            compiler_params=pltpu.CompilerParams(collective_id=0, has_side_effects=True),
            name="pair_step",
        )(
            emb_row,
            emb_col.T,
            proj_row.T,
            proj_col.T,
            pair_out,
            pair_bias.reshape(1, chan),
            conv_weight,
            conv_bias.reshape(1, chan),
            target,
            kept_tiles,
        )
        loss, grads, bias = pl.pallas_call(
            finish,
            out_shape=(
                jax.ShapeDtypeStruct((edge, edge), F32),
                jax.ShapeDtypeStruct((3, 3, chan, chan), F32),
                jax.ShapeDtypeStruct((1, chan), F32),
            ),
            in_specs=[vmem] * 3,
            out_specs=(hbm,) * 3,
            scratch_shapes=[
                pltpu.VMEM((n_own * chunk, 128), F32),
                pltpu.VMEM((3, 3, chan, chan), F32),
                pltpu.VMEM((1, chan), F32),
                dma((3,)),
            ],
            name="finish",
        )(
            *(pltpu.with_memory_space_constraint(x, pltpu.VMEM) for x in results)
        )
        return loss, grads, bias.reshape(chan)

    in_specs = (
        P(("grp", "row", "rep"), "col"),
        P(("grp", "col"), "row"),
        P(),
        P(),
        P(),
        P(),
        P(),
        P(),
        P(None, ("grp", "row", "rep"), "col"),
        P(("grp", "row", "rep"), "col"),
    )
    out_specs = (P(("grp", "row", "rep"), "col"), P("grp", None, None, None), P("grp"))
    return jax.shard_map(
        per_device, mesh=mesh, in_specs=in_specs, out_specs=out_specs, check_vma=False
    )
```

```python
import functools

import jax
import jax.numpy as jnp
from jax import lax
from jax.experimental import pallas as pl
from jax.experimental.pallas import tpu as pltpu
from jax.sharding import PartitionSpec as P

MESH = pl.DeviceIdType.MESH
F32 = jnp.float32
BF16 = jnp.bfloat16
CODES = 32000.0
LOG2E = 1.4426950408889634


def loop(low, high, body):
    if high - low <= 16:
        for d in range(low, high):
            body(d)
    else:
        lax.fori_loop(low, high, lambda d, _: (body(d), 0)[1], 0)


def window_of(everything, width, index, count):
    if width % 128 == 0:
        return index * width, width, 0
    offset = max(i * width % 128 for i in range(count))
    window = min(-(-(offset + width) // 128) * 128, everything)
    tile = lax.div(index * width, 128)
    if any(i * width // 128 * 128 + window > everything for i in range(count)):
        tile = jnp.minimum(tile, (everything - window) // 128)
    return tile * 128, window, index * width - tile * 128


def columns(ref, width, shift):
    window = ref.shape[1]
    if width % 128 == 0:
        return ref[...]
    value = pltpu.roll(ref[...].astype(F32), lax.rem(window - shift, window), 1)
    lane = lax.broadcasted_iota(jnp.int32, value.shape, 1)
    return jnp.where(lane < width, value, 0.0).astype(BF16)


def padded(value, square):
    if all(have == 256 or have % 128 == 0 for have in value.shape):
        for axis in range(2):
            if value.shape[axis] < 256:
                blank = list(value.shape)
                blank[axis] = 256 - blank[axis]
                value = jnp.concatenate([value, jnp.zeros(blank, BF16)], axis=axis)
        return value
    square[...] = jnp.zeros_like(square)
    square[0 : value.shape[0], 0 : value.shape[1]] = value
    return square[...]


def wide_tile(value, low):
    value = value[:, low : low + 256]
    if value.shape[1] < 256:
        blank = jnp.zeros((value.shape[0], 256 - value.shape[1]), BF16)
        value = jnp.concatenate([value, blank], axis=1)
    return value


def kernel(
    sizes,
    emb_row_hbm,
    emb_col_hbm,
    proj_row_hbm,
    proj_col_hbm,
    pair_out_hbm,
    pair_bias_hbm,
    conv_weight_hbm,
    conv_bias_hbm,
    target,
    kept,
    loss_out,
    full,
    emb_row,
    emb_col,
    proj_row,
    proj_col,
    conv_weight,
    pair_out,
    pair_bias,
    conv_bias,
    in_sem,
    rowtail,
    coltail,
    rowbuf,
    rowedge,
    colbuf,
    coledge,
    row_feat,
    col_wide,
    feat_pairs,
    square,
    wide,
    weight_t,
    target_in,
    aims,
    hid,
    base,
    grad_in,
    weight_f,
    total,
    bias_acc,
    part,
    reduced,
    target_sem,
    row_send,
    row_recv,
    redge_send,
    redge_recv,
    col_send,
    col_recv,
    cedge_send,
    cedge_recv,
    rs_send,
    rs_recv,
    ag_send,
    ag_recv,
):
    n_row, n_col, n_rep, edge, chan, n_own, first_own, share, chunk = sizes
    n_all = n_row * n_col * n_rep
    pairs = edge // 2
    row, col, rep = lax.axis_index("row"), lax.axis_index("col"), lax.axis_index("rep")
    line = row * n_rep + rep
    n_line = n_row * n_rep
    me = line * n_col + col

    def device(index):
        across = lax.rem(index, n_col)
        along = lax.div(index, n_col)
        return {"row": lax.div(along, n_rep), "rep": lax.rem(along, n_rep), "col": across}

    def wrapped(index, count):
        return jnp.where(index >= count, index - count, index)

    def far(k):
        down, up = n_row - 1 - k, k
        down = down - (down <= row).astype(jnp.int32)
        up = up + (up >= row).astype(jnp.int32)
        return jnp.where(2 * row < n_row, down, up)

    def await_bytes(ref, sem):
        pltpu.make_async_copy(ref, ref, sem).wait()

    col_width, row_width = emb_col.shape[0], emb_row.shape[1]
    everything = proj_col_hbm.shape[1]
    col_low, col_window, col_shift = window_of(everything, col_width, row, n_row)
    row_low, row_window, row_shift = window_of(everything, row_width, col, n_col)

    def lanes(low, window):
        return pl.ds(pl.multiple_of(low, 128), window)

    inputs = [
        pltpu.make_async_copy(src, dst, in_sem.at[i])
        for i, (src, dst) in enumerate(
            (
                (emb_col_hbm, emb_col),
                (proj_col_hbm.at[:, lanes(col_low, col_window)], proj_col),
                (emb_row_hbm, emb_row),
                (proj_row_hbm.at[:, lanes(row_low, row_window)], proj_row),
                (conv_weight_hbm, conv_weight),
                (pair_out_hbm, pair_out),
                (pair_bias_hbm, pair_bias),
                (conv_bias_hbm, conv_bias),
            )
        )
    ]
    for copy in inputs:
        copy.start()
    barrier = pltpu.get_barrier_semaphore()

    def greet(to):
        pl.semaphore_signal(barrier, inc=1, device_id=to, device_id_type=MESH)

    if n_all <= 16:
        for k in range(n_row):
            for c in range(n_col - 1, -1, -1):
                for r in range(n_rep - 1, -1, -1):
                    if k < n_row - 1 or c + r > 0:
                        greet(
                            {
                                "row": far(k) if k < n_row - 1 else row,
                                "col": wrapped(col + c, n_col),
                                "rep": wrapped(rep + r, n_rep),
                            }
                        )
    else:
        loop(1, n_all, lambda d: greet(device(lax.rem(me + d, n_all))))


    def rounded(x):
        return x.astype(BF16).astype(F32)

    rank = proj_row.shape[0]
    ends = ((edge - 2, edge - 1), (0, 1))
    fetch = pltpu.make_async_copy(target, target_in, target_sem)

    def pair_row(values, at):
        return jnp.concatenate([values[r : r + 1] for r in at], axis=1)

    def row_copy(d, src):
        return pltpu.make_async_remote_copy(
            src_ref=rowbuf.at[src],
            dst_ref=rowbuf.at[src],
            send_sem=row_send,
            recv_sem=row_recv,
            device_id={"col": lax.rem(col + d, n_col)},
            device_id_type=MESH,
        )

    def redge_copy(side, d, src):
        to = lax.rem(line + (1 if side == 0 else n_line - 1), n_line)
        return pltpu.make_async_remote_copy(
            src_ref=rowtail.at[side],
            dst_ref=rowedge.at[side, src],
            send_sem=redge_send,
            recv_sem=redge_recv,
            device_id={
                "row": lax.div(to, n_rep),
                "rep": lax.rem(to, n_rep),
                "col": lax.rem(col + d, n_col),
            },
            device_id_type=MESH,
        )

    def col_copy(to, src):
        return pltpu.make_async_remote_copy(
            src_ref=colbuf.at[src],
            dst_ref=colbuf.at[src],
            send_sem=col_send,
            recv_sem=col_recv,
            device_id={"row": to},
            device_id_type=MESH,
        )

    def cedge_copy(side, at, src):
        to = lax.rem(col + (1 if side == 0 else n_col - 1), n_col)
        return pltpu.make_async_remote_copy(
            src_ref=coltail.at[side],
            dst_ref=coledge.at[side, src],
            send_sem=cedge_send,
            recv_sem=cedge_recv,
            device_id={"row": at, "col": to},
            device_id_type=MESH,
        )

    for copy in inputs[0:2]:
        copy.wait()
    fetch.start()

    def project_col(col_sum):
        left = columns(proj_col, col_width, col_shift)
        for low in range(0, col_width, 256):
            right = padded(emb_col[low : min(low + 256, col_width), :], square)
            pltpu.matmul_push_rhs(right, 0, 0)
            pltpu.matmul_acc_lhs(col_sum, wide_tile(left, low), load_staged_rhs=0)
        return pltpu.matmul_pop(col_sum)[:, 0:edge]

    def project_row(row_sum):
        left = columns(proj_row, row_width, row_shift)
        for low in range(0, row_width, 256):
            right = padded(emb_row[:, low : min(low + 256, row_width)], square)
            pltpu.matmul_push_rhs(right, 0, 1, transpose=True)
            pltpu.matmul_acc_lhs(row_sum, wide_tile(left, low), load_staged_rhs=0)
        return pltpu.matmul_pop(row_sum)[:, 0:edge]

    part_col = pl.run_scoped(project_col, pltpu.ACC(0)((rank, 256), F32))
    colbuf[row] = part_col.astype(BF16)
    turned = rounded(part_col).T
    for side in range(2):
        coltail[side] = pair_row(turned, ends[side])
    for copy in inputs[2:4]:
        copy.wait()
    part_row = pl.run_scoped(project_row, pltpu.ACC(1)((rank, 256), F32))
    keep = kept[0, 0].astype(F32)
    rowbuf[col, 0:rank, :] = part_row.astype(BF16)
    rowbuf[col, rank:, :] = jnp.full((16, edge), keep, F32).astype(BF16)
    turned = rounded(part_row).T
    for side in range(2):
        rowtail[side, 0:1] = pair_row(turned, ends[side])
        rowtail[side, 1:2] = jnp.full((1, 2 * rank), keep, F32)
    pl.semaphore_wait(barrier, n_all - 1)

    def send_col(k):
        to = far(k)
        col_copy(to, row).start()
        for side in range(2):
            cedge_copy(side, to, row).start()

    loop(0, n_row - 1, send_col)
    for side in range(2):
        cedge_copy(side, row, row).start()
    loop(1, n_col, lambda d: row_copy(d, col).start())
    for side in range(2):
        loop(0, n_col, lambda d: redge_copy(side, d, col).start())

    def await_features(col_sem, row_sem, cedge_sem, redge_sem):
        await_bytes(coledge, cedge_sem)
        if n_row > 1:
            await_bytes(colbuf.at[0 : n_row - 1], col_sem)
        await_bytes(rowedge, redge_sem)
        if n_col > 1:
            await_bytes(rowbuf.at[0 : n_col - 1], row_sem)

    fetch.wait()
    for copy in inputs[4:]:
        copy.wait()

    def lay(i, _):
        for low in range(0, chan, 16):
            block = target_in[low : low + 16, pl.ds(pl.multiple_of(i * 16, 16), 16), :]
            block = jnp.swapaxes(block.astype(F32), 0, 1)
            for r in range(16):
                start = pl.multiple_of((i * 8 + r // 2) * chan + low, 16)
                lanes = slice(r % 2 * edge, (r % 2 + 1) * edge)
                aims[pl.ds(start, 16), lanes] = block[r].astype(BF16)
        return 0

    lax.fori_loop(0, edge // 16, lay, 0)
    for a in range(3):
        for b in range(3):
            weight_f[b * chan : (b + 1) * chan, a * chan : (a + 1) * chan] = conv_weight[
                a, b
            ].astype(F32)
    turned = weight_f[...].T
    eye = lax.broadcasted_iota(jnp.int32, (chan, chan), 0) == lax.broadcasted_iota(
        jnp.int32, (chan, chan), 1
    )
    none = jnp.zeros((chan, chan), F32)
    minus = jnp.concatenate([none, jnp.where(eye, -1.0, 0.0), none], axis=0)
    weight_t[...] = jnp.concatenate([turned, minus], axis=1).astype(BF16)
    out_t = pair_out[...].astype(F32).T
    out_t = jnp.concatenate([out_t, out_t], axis=1)
    pair_b = jnp.broadcast_to(pair_bias[...], (128, chan)).T
    conv_b = jnp.broadcast_to(conv_bias[...], (128, chan)).T
    term = lax.broadcasted_iota(jnp.int32, (chan, 128), 1)
    second = pair_b - rounded(pair_b)
    third = second - rounded(second)
    bias_terms = jnp.where(
        term == 0,
        pair_b,
        jnp.where(term == 1, second, jnp.where(term == 2, third, 0.0)),
    ).astype(BF16)
    bias_acc[...] = jnp.zeros_like(bias_acc)

    await_features(col_recv, row_recv, cedge_recv, redge_recv)

    def summed(terms):
        return sum(x.astype(F32) for x in terms)

    def unpack(target, values, low):
        for r in range(2):
            target[low + r : low + r + 1, :] = values[:, r * rank : (r + 1) * rank]

    for side, low in ((0, 6), (1, edge + 8)):
        edge_sum = rounded(summed(rowedge[side, c, 0:1, :] for c in range(n_col)))
        unpack(row_feat, edge_sum, low)
        unpack(col_wide, summed(coledge[side, r] for r in range(n_row)), low)
    row_feat[8 : edge + 8, :] = rounded(summed(rowbuf[c, 0:rank, :] for c in range(n_col))).T
    col_wide[8 : edge + 8, :] = summed(colbuf[r] for r in range(n_row)).T
    feat_pairs[0 : pairs + 2, :] = jnp.concatenate(
        [row_feat[pl.ds(6 + r, pairs + 2, stride=2), :] for r in range(2)], axis=1
    )

    lane = lax.broadcasted_iota(jnp.int32, (1, edge), 1)
    before, after = lax.rem(col + n_col - 1, n_col), lax.rem(col + 1, n_col)
    has_before = (col > 0).astype(F32)
    has_after = (col < n_col - 1).astype(F32)

    def masks(get, valid):
        here, left, right = (
            jnp.broadcast_to(get(c), (1, edge)) * scale
            for c, scale in ((col, valid), (before, valid * has_before), (after, valid * has_after))
        )
        return (jnp.where(lane < 2, left, here), here, jnp.where(lane >= edge - 2, right, here))

    top = masks(lambda c: rowedge[0, c, 1:2, 0:1], (line > 0).astype(F32))
    middle = masks(lambda c: rowbuf[c, rank:, 0:1].astype(F32)[0:1], jnp.float32(1))
    bottom = masks(lambda c: rowedge[1, c, 1:2, 0:1], (line < n_line - 1).astype(F32))

    shifted = [col_wide[6 + 2 * b : 6 + 2 * b + edge, :].T for b in range(3)]
    first_rows = lax.broadcasted_iota(jnp.int32, (2 * edge - 2 * rank, 2 * edge), 0) < 3

    def operand(value, mask):
        value = value * mask
        blank = jnp.zeros_like(value)
        ones = jnp.where(first_rows, jnp.concatenate([mask, mask], axis=1), 0.0)
        return jnp.concatenate(
            [
                jnp.concatenate([value, blank], axis=1),
                jnp.concatenate([blank, value], axis=1),
                ones,
            ],
            axis=0,
        ).astype(BF16)

    def outer(left, right):
        return jnp.where(lane < 2, left, jnp.where(lane >= edge - 2, right, 0.0))

    wide[0] = operand(shifted[1], middle[1])
    wide[1] = operand(outer(shifted[0], shifted[2]), outer(middle[0], middle[2]))
    lane_wide = lax.broadcasted_iota(jnp.int32, (chan, edge), 1)

    def moved(value, halo, b):
        halves = []
        for r in range(2):
            lanes = slice(r * edge, (r + 1) * edge)
            turned = pltpu.roll(value[:, lanes], 2 if b == 0 else edge - 2, 1)
            at_end = lane_wide < 2 if b == 0 else lane_wide >= edge - 2
            halves.append(jnp.where(at_end, halo[:, lanes], turned))
        return jnp.concatenate(halves, axis=1)

    def scaled(p, count):
        low = (out_t * feat_pairs[pl.ds(p + 1 + r, 1), :] for r in range(count))
        low = jnp.concatenate([x.astype(BF16) for x in low], axis=0)
        return jnp.concatenate([low, jnp.concatenate([bias_terms] * count, axis=0)], axis=1)

    conv_b = jnp.concatenate([conv_b, conv_b], axis=1)
    blank = jnp.zeros((chan, 2 * edge), BF16)

    def slot(offset, first=0, count=1, of=1):
        low = (offset % 16 * of + first) * chan
        return slice(low, low + count * chan)

    def inside(p, offset):
        return not isinstance(p, int) or 0 <= p + offset < pairs

    def finish_pair(p, offset, conv):
        differ = (base[slot(offset), :] + conv) * keep
        grad_in[slot(offset), :] = differ.astype(BF16)
        bias_acc[...] += differ
        loss = 0.5 * jnp.sum(differ * differ, axis=0, keepdims=True)
        at = 2 * (p + offset)
        loss_out[pl.ds(at, 1), :] = loss[:, 0:edge]
        loss_out[pl.ds(at + 1, 1), :] = loss[:, edge : 2 * edge]

    def main(*accs):
        sums, grads, halo, features_of = accs[0:4], accs[4:6], accs[6], (accs[7:9], accs[9:13])
        stage, primed = [0, 0], [False, False]

        def halo_item(p, offset, b, mask):
            def push(at):
                pltpu.matmul_push_rhs(operand(shifted[b], mask[b]), at, 1)

            def go(at):
                pltpu.matmul_acc_lhs(halo, scaled(p + offset, 1), load_staged_rhs=at)
                value = jnp.maximum(pltpu.matmul_pop(halo), 0.0)
                hid[slot(offset, b, 1, 3), :] = value.astype(BF16)

            return push, go, None, 4

        def feature_item(unit, kind, p, offset, held, memo):
            def push(at):
                pltpu.matmul_push_rhs(wide[kind], at, unit)

            def go(at):
                if not memo:
                    memo.append(scaled(p + offset, 2))
                pltpu.matmul_acc_lhs(held[kind], memo[0], load_staged_rhs=at)

            def after():
                value, halo = (pltpu.matmul_pop(acc) for acc in held)
                for r in range(2):
                    own = value[r * chan : (r + 1) * chan]
                    base[slot(offset + r), :] = own + conv_b
                    own = jnp.maximum(own, 0.0)
                    ends_of = jnp.maximum(halo[r * chan : (r + 1) * chan], 0.0)
                    for b in range(3):
                        copy_of = own if b == 1 else moved(own, ends_of, b)
                        hid[slot(offset + r, b, 1, 3), :] = copy_of.astype(BF16)

            return push, go, after if kind == 1 else None, 8

        def conv_item(p, offset):
            taps = [a for a in range(3) if inside(p, offset + 1 - a)]

            def push(at):
                aim = blank
                if inside(p, offset):
                    aim = aims[pl.ds(pl.multiple_of((p + offset) * chan, chan), chan), :]
                right = jnp.concatenate([hid[slot(offset, 0, 3, 3), :], aim], axis=0)
                pltpu.matmul_push_rhs(right, at, 0)

            def go(at):
                for a in taps:
                    pltpu.matmul_acc_lhs(
                        sums[(offset + 1 - a) % 4],
                        weight_t[a * chan : (a + 1) * chan, :],
                        load_staged_rhs=at,
                    )
                    at = None

            def after():
                if 2 in taps:
                    finish_pair(p, offset - 1, pltpu.matmul_pop(sums[(offset - 1) % 4]))

            return push, go, after, 4 * len(taps)

        def grad_item(unit, p, offset):
            def push(at):
                right = [
                    grad_in[slot(offset + k), :] if inside(p, offset + k) else blank
                    for k in range(-2, 2)
                ]
                right = jnp.concatenate(right, axis=0)
                pltpu.matmul_push_rhs(right, at, unit, transpose=True)

            def go(at):
                left = hid[slot(offset, 0, 3, 3), :]
                pltpu.matmul_acc_lhs(grads[unit], left, load_staged_rhs=at)

            return push, go, None, 12

        def run(queues, follow=(None, None)):
            spent, at, waiting = [0, 0], [0, 0], []
            for unit in range(2):
                if queues[unit] and not primed[unit]:
                    queues[unit][0][0](stage[unit])
                primed[unit] = False
            while any(at[u] < len(queues[u]) for u in range(2)):
                unit = min(
                    (u for u in range(2) if at[u] < len(queues[u])), key=lambda u: spent[u]
                )
                queue, index = queues[unit], at[unit]
                _, go, after, cost = queue[index]
                while len(waiting) > 1:
                    waiting.pop(0)()
                go(stage[unit])
                stage[unit] = 1 - stage[unit]
                if index + 1 < len(queue):
                    queue[index + 1][0](stage[unit])
                at[unit] += 1
                spent[unit] += cost
                if after is not None:
                    waiting.append(after)
            for after in waiting:
                after()
            for unit in range(2):
                if follow[unit] is not None:
                    follow[unit][0](stage[unit])
                    primed[unit] = True

        def features(p, low, units=(1, 1)):
            items = []
            for half, unit in enumerate(units):
                memo, held = [], features_of[unit][2 * half * unit : 2 * half * unit + 2]
                items.append(
                    [feature_item(unit, k, p, low + 2 * half, held, memo) for k in range(2)]
                )
            return items

        def convs(p, low, high):
            return [conv_item(p, r) for r in range(low, high)]

        def turns(unit, p, *offsets):
            return [grad_item(unit, p, r) for r in offsets]

        def group(p, low):
            early, late = features(p, low)
            conv = convs(p, low - 4, low)
            shared = [turns(0, p, low - 10), turns(1, p, low - 10)]
            shared[1 if low % 8 == 0 else 0] = []
            run(
                (
                    turns(0, p, low - 12) + conv[0:2] + shared[0] + conv[2:4],
                    turns(1, p, low - 11) + early + shared[1] + turns(1, p, low - 9) + late,
                ),
                [turns(u, p, low - 8 + u)[0] for u in range(2)],
            )

        early, late = features(0, 0, (1, 0))
        first = convs(0, -1, 4)
        second = features(0, 4)
        run((late, [halo_item(0, -1, b, top) for b in range(3)] + early), (first[0], second[0][0]))
        third, fourth = convs(0, 4, 8), features(0, 8)
        run((first, second[0] + second[1]), (third[0], fourth[0][0]))
        fifth, sixth = convs(0, 8, 12), features(0, 12)
        run((third, fourth[0] + turns(1, 0, -1) + fourth[1]), (fifth[0], sixth[0][0]))
        run(
            (
                fifth[0:2] + turns(0, 0, 0) + fifth[2:4] + turns(0, 0, 2),
                sixth[0] + turns(1, 0, 1) + sixth[1] + turns(1, 0, 3),
            ),
            [turns(u, 0, 4 + u)[0] for u in range(2)],
        )

        def step(t, _):
            p = pl.multiple_of(t * 16, 16)
            for k in range(4):
                group(p, 4 * k)
            return 0

        lax.fori_loop(1, pairs // 16, step, 0)
        last = convs(pairs, -4, 1)
        run(
            (
                turns(0, pairs, -12) + last[0:2] + turns(0, pairs, -10) + last[2:4],
                turns(1, pairs, -11)
                + [halo_item(pairs, 0, b, bottom) for b in range(3)]
                + turns(1, pairs, -9, -8, -7),
            ),
            (last[4], turns(1, pairs, -6)[0]),
        )
        run((last[4:] + turns(0, pairs, -5, -4), turns(1, pairs, -6, -3)))
        run((turns(0, pairs, -2, 0), turns(1, pairs, -1)))
        total[...] = pltpu.matmul_pop(grads[0]) + pltpu.matmul_pop(grads[1])

    def accumulator(unit, rows_of):
        return pltpu.ACC(unit)((rows_of, 2 * edge), F32)

    pl.run_scoped(
        main,
        *[accumulator(0, chan)] * 4,
        *[accumulator(unit, 3 * chan) for unit in range(2)],
        accumulator(1, chan),
        *[accumulator(0, 2 * chan)] * 2,
        *[accumulator(1, 2 * chan)] * 4,
    )

    norm = 1.0 / (edge * edge)
    half = 3 * chan // 2
    rows = 3 * chan + half
    sums = total[...] * norm
    flat = jnp.concatenate(
        [
            sums[:, 2 * chan :],
            jnp.concatenate(
                [sums[0:half, chan : 2 * chan], sums[half:, chan : 2 * chan]], axis=1
            ),
        ],
        axis=0,
    )
    bias_sum = (bias_acc[:, 0:edge] + bias_acc[:, edge:]).T
    bias_sum = jnp.sum(bias_sum, axis=0, keepdims=True) * norm

    def largest(values):
        return jnp.max(jnp.max(jnp.abs(values), axis=0, keepdims=True), axis=1, keepdims=True)

    def exponent(values):
        return jnp.ceil(jnp.log(jnp.maximum(largest(values), 1e-30)) * LOG2E + 0.01)

    def coded(values, power):
        return values * (jnp.exp2(-power) * CODES)

    def side_rows(power, bias):
        bias_power = exponent(bias)
        high = jnp.round(coded(bias, bias_power))
        low = (coded(bias, bias_power) - high) * CODES
        return [
            jnp.concatenate([high, low], axis=1),
            jnp.broadcast_to(power, (1, 128)),
            jnp.broadcast_to(bias_power, (1, 128)),
        ]

    def packed(values, sides):
        blank = chunk - values.shape[0] - len(sides)
        values = jnp.concatenate([values, *sides, jnp.zeros((blank, 128), F32)], axis=0)
        return jnp.round(values).astype(jnp.int32).astype(jnp.int16)

    power = exponent(flat)
    codes = coded(flat, power)
    sides = side_rows(power, bias_sum)
    for index in range(n_own):
        have = min(max(rows - index * share, 0), share)
        values = [codes[index * share : index * share + have]] if have else []
        if have < share:
            values.append(jnp.zeros((share - have, 128), F32))
        part[index] = packed(jnp.concatenate(values, axis=0), sides)

    mine = me - first_own
    owner = (mine >= 0) & (mine < n_own)

    def remote(src, dst, send_sem, recv_sem, to):
        return pltpu.make_async_remote_copy(
            src_ref=src,
            dst_ref=dst,
            send_sem=send_sem,
            recv_sem=recv_sem,
            device_id=to,
            device_id_type=MESH,
        )

    square_of = n_col * n_rep
    owner_rows = n_own // square_of

    def scatter(d):
        level = d // square_of if isinstance(d, int) else lax.div(d, square_of)
        level = jnp.where(2 * row < n_row, owner_rows - 1 - level, level)
        index = level * square_of + lax.rem(me + d, square_of)

        @pl.when(first_own + index != me)
        def _():
            to = device(first_own + index)
            remote(part.at[index], reduced.at[me], rs_send, rs_recv, to).start()

    def give(to):
        remote(full.at[mine], full.at[mine], ag_send, ag_recv, to).start()

    def around(at):
        for c in range(n_col - 1, -1, -1):
            for r in range(n_rep - 1, -1, -1):
                yield {"row": at, "col": wrapped(col + c, n_col), "rep": wrapped(rep + r, n_rep)}

    def gather(k):
        for to in around(far(k)):
            give(to)

    loop(0, n_own, scatter)

    @pl.when(owner)
    def _():
        reduced[me] = part[mine]
        await_bytes(reduced.at[0 : n_all - 1], rs_recv)

        def decoded(r):
            value = reduced[r].astype(jnp.int32).astype(F32)
            return (
                value[0:share] * (jnp.exp2(value[share + 1 : share + 2]) / CODES),
                value[share : share + 1] * (jnp.exp2(value[share + 2 : share + 3]) / CODES),
            )

        if n_all <= 16:
            terms = [decoded(r) for r in range(n_all)]
            own, bias = (sum(x[k] for x in terms) for k in range(2))
        else:
            own, bias = lax.fori_loop(
                0,
                n_all,
                lambda r, x: tuple(a + b for a, b in zip(x, decoded(r))),
                (jnp.zeros((share, 128), F32), jnp.zeros((1, 128), F32)),
            )
        bias = bias[:, 0:chan] + bias[:, chan : 2 * chan] * (1.0 / CODES)
        power = exponent(own)
        full[mine] = packed(coded(own, power), side_rows(power, bias))
        loop(0, n_row - 1, gather)
        for to in list(around(row))[:-1]:
            give(to)
        if n_own > 1:
            await_bytes(full.at[0 : n_own - 1], ag_recv)
            await_bytes(part.at[0 : n_own - 1], rs_send)

    @pl.when(jnp.logical_not(owner))
    def _():
        await_bytes(full, ag_recv)
        await_bytes(part, rs_send)

    await_features(col_send, row_send, cedge_send, redge_send)

    @pl.when(owner)
    def _():
        await_bytes(reduced.at[0 : n_all - 1], ag_send)


def finish(share, loss, gathered, loss_hbm, conv_grad_hbm, bias_hbm, full, conv_grad_out, bias_out, sem):
    n_own = gathered.shape[0]
    loss_copy = pltpu.make_async_copy(loss, loss_hbm, sem.at[0])
    loss_copy.start()

    def decoded(r, low, high, power):
        value = gathered[r].astype(jnp.int32).astype(F32)
        return value[low:high] * (jnp.exp2(value[power : power + 1]) / CODES)

    for r in range(min(n_own, pl.cdiv(full.shape[0], share))):
        high = min(share, full.shape[0] - r * share)
        full[r * share : r * share + high, :] = decoded(r, 0, high, share + 1)

    chan = bias_out.shape[1]
    half = 3 * chan // 2
    rows = 3 * chan + half
    for b in range(3):
        low = b * chan
        conv_grad_out[1, b] = full[low : low + chan, 0:chan]
        conv_grad_out[0, b] = full[low : low + chan, chan : 2 * chan]
    low = 3 * chan
    conv_grad_out[2, 0] = full[low : low + chan, 0:chan]
    conv_grad_out[2, 1, 0 : half - chan] = full[low + chan : low + half, 0:chan]
    conv_grad_out[2, 1, half - chan :] = full[low : low + 2 * chan - half, chan : 2 * chan]
    conv_grad_out[2, 2] = full[low + 2 * chan - half : low + half, chan : 2 * chan]
    terms = decoded(0, share, share + 1, share + 2)
    bias_out[...] = terms[:, 0:chan] + terms[:, chan : 2 * chan] * (1.0 / CODES)
    grad_copy = pltpu.make_async_copy(conv_grad_out, conv_grad_hbm, sem.at[1])
    bias_copy = pltpu.make_async_copy(bias_out, bias_hbm, sem.at[2])
    grad_copy.start()
    bias_copy.start()
    loss_copy.wait()
    grad_copy.wait()
    bias_copy.wait()


def solution(mesh):
    n_row, n_col, n_rep = (mesh.shape[axis] for axis in ("row", "col", "rep"))
    n_all = n_row * n_col * n_rep

    def per_device(
        emb_row,
        emb_col,
        proj_row,
        proj_col,
        pair_out,
        pair_bias,
        conv_weight,
        conv_bias,
        target,
        kept_tiles,
    ):
        chan, edge = target.shape[0], target.shape[1]
        rank = pair_out.shape[0]
        pairs = edge // 2
        used = 3 * chan + 3 * chan // 2
        inner = n_row // 2 if n_row >= 4 else n_row
        n_own = inner * n_col * n_rep
        first_own = (n_row - inner) // 2 * n_col * n_rep
        share = pl.cdiv(used, n_own)
        chunk = 8 * pl.cdiv(share + 3, 8)

        def window(width, count):
            return window_of(proj_row.shape[0], width, 0, count)[1]

        dma = pltpu.SemaphoreType.DMA
        vmem = pl.BlockSpec(memory_space=pltpu.VMEM)
        hbm = pl.BlockSpec(memory_space=pltpu.HBM)
        results = pl.pallas_call(
            functools.partial(
                kernel, (n_row, n_col, n_rep, edge, chan, n_own, first_own, share, chunk)
            ),
            out_shape=(
                pltpu.VMEM((edge, edge), F32),
                pltpu.VMEM((n_own, chunk, 128), jnp.int16),
            ),
            in_specs=[hbm] * 9 + [pl.BlockSpec(memory_space=pltpu.SMEM)],
            out_specs=(vmem,) * 2,
            scratch_shapes=[
                pltpu.VMEM(emb_row.shape, BF16),
                pltpu.VMEM(emb_col.shape[::-1], BF16),
                pltpu.VMEM((rank, window(emb_row.shape[1], n_col)), BF16),
                pltpu.VMEM((rank, window(emb_col.shape[1], n_row)), BF16),
                pltpu.VMEM(conv_weight.shape, BF16),
                pltpu.VMEM(pair_out.shape, BF16),
                pltpu.VMEM((1, chan), F32),
                pltpu.VMEM((1, chan), F32),
                dma((8,)),
                pltpu.VMEM((2, 2, 2 * rank), F32),
                pltpu.VMEM((2, 1, 2 * rank), F32),
                pltpu.VMEM((n_col, rank + 16, edge), BF16),
                pltpu.VMEM((2, n_col, 2, 2 * rank), F32),
                pltpu.VMEM((n_row, rank, edge), BF16),
                pltpu.VMEM((2, n_row, 1, 2 * rank), F32),
                pltpu.VMEM((edge + 16, rank), F32),
                pltpu.VMEM((edge + 16, rank), F32),
                pltpu.VMEM((pairs + 8, 2 * rank), F32),
                pltpu.VMEM((256, 256), BF16),
                pltpu.VMEM((2, 2 * edge, 2 * edge), BF16),
                pltpu.VMEM((3 * chan, 4 * chan), BF16),
                pltpu.VMEM((chan, edge, edge), BF16),
                pltpu.VMEM((pairs * chan, 2 * edge), BF16),
                pltpu.VMEM((16 * 3 * chan, 2 * edge), BF16),
                pltpu.VMEM((16 * chan, 2 * edge), F32),
                pltpu.VMEM((16 * chan, 2 * edge), BF16),
                pltpu.VMEM((3 * chan, 3 * chan), F32),
                pltpu.VMEM((3 * chan, 4 * chan), F32),
                pltpu.VMEM((chan, 2 * edge), F32),
                pltpu.VMEM((n_own, chunk, 128), jnp.int16),
                pltpu.VMEM((n_all, chunk, 128), jnp.int16),
                *[pltpu.SemaphoreType.DMA] * 13,
            ],
            compiler_params=pltpu.CompilerParams(collective_id=0, has_side_effects=True),
            name="pair_step",
        )(
            emb_row,
            emb_col.T,
            proj_row.T,
            proj_col.T,
            pair_out,
            pair_bias.reshape(1, chan),
            conv_weight,
            conv_bias.reshape(1, chan),
            target,
            kept_tiles,
        )
        loss, grads, bias = pl.pallas_call(
            functools.partial(finish, share),
            out_shape=(
                jax.ShapeDtypeStruct((edge, edge), F32),
                jax.ShapeDtypeStruct((3, 3, chan, chan), F32),
                jax.ShapeDtypeStruct((1, chan), F32),
            ),
            in_specs=[vmem] * 2,
            out_specs=(hbm,) * 3,
            scratch_shapes=[
                pltpu.VMEM((used, 128), F32),
                pltpu.VMEM((3, 3, chan, chan), F32),
                pltpu.VMEM((1, chan), F32),
                dma((3,)),
            ],
            name="finish",
        )(
            *(pltpu.with_memory_space_constraint(x, pltpu.VMEM) for x in results)
        )
        return loss, grads, bias.reshape(chan)

    in_specs = (
        P(("grp", "row", "rep"), "col"),
        P(("grp", "col"), "row"),
        P(),
        P(),
        P(),
        P(),
        P(),
        P(),
        P(None, ("grp", "row", "rep"), "col"),
        P(("grp", "row", "rep"), "col"),
    )
    out_specs = (P(("grp", "row", "rep"), "col"), P("grp", None, None, None), P("grp"))
    return jax.shard_map(
        per_device, mesh=mesh, in_specs=in_specs, out_specs=out_specs, check_vma=False
    )
```

```python
import functools

import jax
import jax.numpy as jnp
from jax import lax
from jax.experimental import pallas as pl
from jax.experimental.pallas import tpu as pltpu
from jax.sharding import PartitionSpec as P

MESH = pl.DeviceIdType.MESH
F32 = jnp.float32
BF16 = jnp.bfloat16
CODES = 32000.0
LOG2E = 1.4426950408889634


def loop(low, high, body):
    if high - low <= 16:
        for d in range(low, high):
            body(d)
    else:
        lax.fori_loop(low, high, lambda d, _: (body(d), 0)[1], 0)


def window_of(everything, width, index, count):
    if width % 128 == 0:
        return index * width, width, 0
    offset = max(i * width % 128 for i in range(count))
    window = min(-(-(offset + width) // 128) * 128, everything)
    tile = lax.div(index * width, 128)
    if any(i * width // 128 * 128 + window > everything for i in range(count)):
        tile = jnp.minimum(tile, (everything - window) // 128)
    return tile * 128, window, index * width - tile * 128


def columns(ref, width, shift):
    window = ref.shape[1]
    if width % 128 == 0:
        return ref[...]
    value = pltpu.roll(ref[...].astype(F32), lax.rem(window - shift, window), 1)
    lane = lax.broadcasted_iota(jnp.int32, value.shape, 1)
    return jnp.where(lane < width, value, 0.0).astype(BF16)


def padded(value, square):
    if all(have == 256 or have % 128 == 0 for have in value.shape):
        for axis in range(2):
            if value.shape[axis] < 256:
                blank = list(value.shape)
                blank[axis] = 256 - blank[axis]
                value = jnp.concatenate([value, jnp.zeros(blank, BF16)], axis=axis)
        return value
    square[...] = jnp.zeros_like(square)
    square[0 : value.shape[0], 0 : value.shape[1]] = value
    return square[...]


def wide_tile(value, low):
    value = value[:, low : low + 256]
    if value.shape[1] < 256:
        blank = jnp.zeros((value.shape[0], 256 - value.shape[1]), BF16)
        value = jnp.concatenate([value, blank], axis=1)
    return value


def kernel(
    sizes,
    emb_row_hbm,
    emb_col_hbm,
    proj_row_hbm,
    proj_col_hbm,
    pair_out_hbm,
    pair_bias_hbm,
    conv_weight_hbm,
    conv_bias_hbm,
    target,
    kept,
    loss_out,
    full,
    emb_row,
    emb_col,
    proj_row,
    proj_col,
    conv_weight,
    pair_out,
    pair_bias,
    conv_bias,
    in_sem,
    rowtail,
    coltail,
    rowbuf,
    rowedge,
    colbuf,
    coledge,
    row_feat,
    col_wide,
    feat_pairs,
    square,
    wide,
    weight_t,
    target_in,
    aims,
    hid,
    base,
    grad_in,
    weight_f,
    total,
    bias_acc,
    part,
    reduced,
    target_sem,
    row_send,
    row_recv,
    redge_send,
    redge_recv,
    col_send,
    col_recv,
    cedge_send,
    cedge_recv,
    rs_send,
    rs_recv,
    ag_send,
    ag_recv,
):
    n_row, n_col, n_rep, edge, chan, n_own, first_own, share, chunk = sizes
    n_all = n_row * n_col * n_rep
    pairs = edge // 2
    row, col, rep = lax.axis_index("row"), lax.axis_index("col"), lax.axis_index("rep")
    line = row * n_rep + rep
    n_line = n_row * n_rep
    me = line * n_col + col

    def device(index):
        across = lax.rem(index, n_col)
        along = lax.div(index, n_col)
        return {"row": lax.div(along, n_rep), "rep": lax.rem(along, n_rep), "col": across}

    def wrapped(index, count):
        return jnp.where(index >= count, index - count, index)

    def far(k):
        down, up = n_row - 1 - k, k
        down = down - (down <= row).astype(jnp.int32)
        up = up + (up >= row).astype(jnp.int32)
        return jnp.where(2 * row < n_row, down, up)

    def await_bytes(ref, sem):
        pltpu.make_async_copy(ref, ref, sem).wait()

    col_width, row_width = emb_col.shape[0], emb_row.shape[1]
    everything = proj_col_hbm.shape[1]
    col_low, col_window, col_shift = window_of(everything, col_width, row, n_row)
    row_low, row_window, row_shift = window_of(everything, row_width, col, n_col)

    def lanes(low, window):
        return pl.ds(pl.multiple_of(low, 128), window)

    inputs = [
        pltpu.make_async_copy(src, dst, in_sem.at[i])
        for i, (src, dst) in enumerate(
            (
                (emb_col_hbm, emb_col),
                (proj_col_hbm.at[:, lanes(col_low, col_window)], proj_col),
                (emb_row_hbm, emb_row),
                (proj_row_hbm.at[:, lanes(row_low, row_window)], proj_row),
                (conv_weight_hbm, conv_weight),
                (pair_out_hbm, pair_out),
                (pair_bias_hbm, pair_bias),
                (conv_bias_hbm, conv_bias),
            )
        )
    ]
    for copy in inputs:
        copy.start()
    barrier = pltpu.get_barrier_semaphore()

    def greet(to):
        pl.semaphore_signal(barrier, inc=1, device_id=to, device_id_type=MESH)

    if n_all <= 16:
        for k in range(n_row):
            for c in range(n_col - 1, -1, -1):
                for r in range(n_rep - 1, -1, -1):
                    if k < n_row - 1 or c + r > 0:
                        greet(
                            {
                                "row": far(k) if k < n_row - 1 else row,
                                "col": wrapped(col + c, n_col),
                                "rep": wrapped(rep + r, n_rep),
                            }
                        )
    else:
        loop(1, n_all, lambda d: greet(device(lax.rem(me + d, n_all))))


    def rounded(x):
        return x.astype(BF16).astype(F32)

    rank = proj_row.shape[0]
    ends = ((edge - 2, edge - 1), (0, 1))
    fetch = pltpu.make_async_copy(target, target_in, target_sem)

    def pair_row(values, at):
        return jnp.concatenate([values[r : r + 1] for r in at], axis=1)

    def row_copy(d, src):
        return pltpu.make_async_remote_copy(
            src_ref=rowbuf.at[src],
            dst_ref=rowbuf.at[src],
            send_sem=row_send,
            recv_sem=row_recv,
            device_id={"col": lax.rem(col + d, n_col)},
            device_id_type=MESH,
        )

    def redge_copy(side, d, src):
        to = lax.rem(line + (1 if side == 0 else n_line - 1), n_line)
        return pltpu.make_async_remote_copy(
            src_ref=rowtail.at[side],
            dst_ref=rowedge.at[side, src],
            send_sem=redge_send,
            recv_sem=redge_recv,
            device_id={
                "row": lax.div(to, n_rep),
                "rep": lax.rem(to, n_rep),
                "col": lax.rem(col + d, n_col),
            },
            device_id_type=MESH,
        )

    def col_copy(to, src):
        return pltpu.make_async_remote_copy(
            src_ref=colbuf.at[src],
            dst_ref=colbuf.at[src],
            send_sem=col_send,
            recv_sem=col_recv,
            device_id={"row": to},
            device_id_type=MESH,
        )

    def cedge_copy(side, at, src):
        to = lax.rem(col + (1 if side == 0 else n_col - 1), n_col)
        return pltpu.make_async_remote_copy(
            src_ref=coltail.at[side],
            dst_ref=coledge.at[side, src],
            send_sem=cedge_send,
            recv_sem=cedge_recv,
            device_id={"row": at, "col": to},
            device_id_type=MESH,
        )

    for copy in inputs[0:2]:
        copy.wait()
    fetch.start()

    def project_col(col_sum):
        left = columns(proj_col, col_width, col_shift)
        for low in range(0, col_width, 256):
            right = padded(emb_col[low : min(low + 256, col_width), :], square)
            pltpu.matmul_push_rhs(right, 0, 0)
            pltpu.matmul_acc_lhs(col_sum, wide_tile(left, low), load_staged_rhs=0)
        return pltpu.matmul_pop(col_sum)[:, 0:edge]

    def project_row(row_sum):
        left = columns(proj_row, row_width, row_shift)
        for low in range(0, row_width, 256):
            right = padded(emb_row[:, low : min(low + 256, row_width)], square)
            pltpu.matmul_push_rhs(right, 0, 1, transpose=True)
            pltpu.matmul_acc_lhs(row_sum, wide_tile(left, low), load_staged_rhs=0)
        return pltpu.matmul_pop(row_sum)[:, 0:edge]

    part_col = pl.run_scoped(project_col, pltpu.ACC(0)((rank, 256), F32))
    colbuf[row] = part_col.astype(BF16)
    turned = rounded(part_col).T
    for side in range(2):
        coltail[side] = pair_row(turned, ends[side])
    for copy in inputs[2:4]:
        copy.wait()
    part_row = pl.run_scoped(project_row, pltpu.ACC(1)((rank, 256), F32))
    keep = kept[0, 0].astype(F32)
    rowbuf[col, 0:rank, :] = part_row.astype(BF16)
    rowbuf[col, rank:, :] = jnp.full((16, edge), keep, F32).astype(BF16)
    turned = rounded(part_row).T
    for side in range(2):
        rowtail[side, 0:1] = pair_row(turned, ends[side])
        rowtail[side, 1:2] = jnp.full((1, 2 * rank), keep, F32)
    pl.semaphore_wait(barrier, n_all - 1)

    def send_col(k):
        to = far(k)
        col_copy(to, row).start()
        for side in range(2):
            cedge_copy(side, to, row).start()

    loop(0, n_row - 1, send_col)
    for side in range(2):
        cedge_copy(side, row, row).start()
    loop(1, n_col, lambda d: row_copy(d, col).start())
    for side in range(2):
        loop(0, n_col, lambda d: redge_copy(side, d, col).start())

    def await_features(col_sem, row_sem, cedge_sem, redge_sem):
        await_bytes(coledge, cedge_sem)
        if n_row > 1:
            await_bytes(colbuf.at[0 : n_row - 1], col_sem)
        await_bytes(rowedge, redge_sem)
        if n_col > 1:
            await_bytes(rowbuf.at[0 : n_col - 1], row_sem)

    fetch.wait()
    for copy in inputs[4:]:
        copy.wait()

    def lay(i, _):
        for low in range(0, chan, 16):
            block = target_in[low : low + 16, pl.ds(pl.multiple_of(i * 16, 16), 16), :]
            block = jnp.swapaxes(block.astype(F32), 0, 1)
            for r in range(16):
                start = pl.multiple_of((i * 8 + r // 2) * chan + low, 16)
                lanes = slice(r % 2 * edge, (r % 2 + 1) * edge)
                aims[pl.ds(start, 16), lanes] = block[r].astype(BF16)
        return 0

    lax.fori_loop(0, edge // 16, lay, 0)
    for a in range(3):
        for b in range(3):
            weight_f[b * chan : (b + 1) * chan, a * chan : (a + 1) * chan] = conv_weight[
                a, b
            ].astype(F32)
    turned = weight_f[...].T
    eye = lax.broadcasted_iota(jnp.int32, (chan, chan), 0) == lax.broadcasted_iota(
        jnp.int32, (chan, chan), 1
    )
    none = jnp.zeros((chan, chan), F32)
    minus = jnp.concatenate([none, jnp.where(eye, -1.0, 0.0), none], axis=0)
    weight_t[...] = jnp.concatenate([turned, minus], axis=1).astype(BF16)
    out_t = pair_out[...].astype(F32).T
    out_t = jnp.concatenate([out_t, out_t], axis=1)
    pair_b = jnp.broadcast_to(pair_bias[...], (128, chan)).T
    conv_b = jnp.broadcast_to(conv_bias[...], (128, chan)).T
    term = lax.broadcasted_iota(jnp.int32, (chan, 128), 1)
    second = pair_b - rounded(pair_b)
    third = second - rounded(second)
    bias_terms = jnp.where(
        term == 0,
        pair_b,
        jnp.where(term == 1, second, jnp.where(term == 2, third, 0.0)),
    ).astype(BF16)
    bias_acc[...] = jnp.zeros_like(bias_acc)

    await_features(col_recv, row_recv, cedge_recv, redge_recv)

    def summed(terms):
        return sum(x.astype(F32) for x in terms)

    def unpack(target, values, low):
        for r in range(2):
            target[low + r : low + r + 1, :] = values[:, r * rank : (r + 1) * rank]

    for side, low in ((0, 6), (1, edge + 8)):
        edge_sum = rounded(summed(rowedge[side, c, 0:1, :] for c in range(n_col)))
        unpack(row_feat, edge_sum, low)
        unpack(col_wide, summed(coledge[side, r] for r in range(n_row)), low)
    row_feat[8 : edge + 8, :] = rounded(summed(rowbuf[c, 0:rank, :] for c in range(n_col))).T
    col_wide[8 : edge + 8, :] = summed(colbuf[r] for r in range(n_row)).T
    feat_pairs[0 : pairs + 2, :] = jnp.concatenate(
        [row_feat[pl.ds(6 + r, pairs + 2, stride=2), :] for r in range(2)], axis=1
    )

    lane = lax.broadcasted_iota(jnp.int32, (1, edge), 1)
    before, after = lax.rem(col + n_col - 1, n_col), lax.rem(col + 1, n_col)
    has_before = (col > 0).astype(F32)
    has_after = (col < n_col - 1).astype(F32)

    def masks(get, valid):
        here, left, right = (
            jnp.broadcast_to(get(c), (1, edge)) * scale
            for c, scale in ((col, valid), (before, valid * has_before), (after, valid * has_after))
        )
        return (jnp.where(lane < 2, left, here), here, jnp.where(lane >= edge - 2, right, here))

    top = masks(lambda c: rowedge[0, c, 1:2, 0:1], (line > 0).astype(F32))
    middle = masks(lambda c: rowbuf[c, rank:, 0:1].astype(F32)[0:1], jnp.float32(1))
    bottom = masks(lambda c: rowedge[1, c, 1:2, 0:1], (line < n_line - 1).astype(F32))

    shifted = [col_wide[6 + 2 * b : 6 + 2 * b + edge, :].T for b in range(3)]
    first_rows = lax.broadcasted_iota(jnp.int32, (2 * edge - 2 * rank, 2 * edge), 0) < 3

    def operand(value, mask):
        value = value * mask
        blank = jnp.zeros_like(value)
        ones = jnp.where(first_rows, jnp.concatenate([mask, mask], axis=1), 0.0)
        return jnp.concatenate(
            [
                jnp.concatenate([value, blank], axis=1),
                jnp.concatenate([blank, value], axis=1),
                ones,
            ],
            axis=0,
        ).astype(BF16)

    def outer(left, right):
        return jnp.where(lane < 2, left, jnp.where(lane >= edge - 2, right, 0.0))

    wide[0] = operand(shifted[1], middle[1])
    wide[1] = operand(outer(shifted[0], shifted[2]), outer(middle[0], middle[2]))
    lane_wide = lax.broadcasted_iota(jnp.int32, (chan, edge), 1)

    def moved(value, halo, b):
        halves = []
        for r in range(2):
            lanes = slice(r * edge, (r + 1) * edge)
            turned = pltpu.roll(value[:, lanes], 2 if b == 0 else edge - 2, 1)
            at_end = lane_wide < 2 if b == 0 else lane_wide >= edge - 2
            halves.append(jnp.where(at_end, halo[:, lanes], turned))
        return jnp.concatenate(halves, axis=1)

    def scaled(p, count):
        low = (out_t * feat_pairs[pl.ds(p + 1 + r, 1), :] for r in range(count))
        low = jnp.concatenate([x.astype(BF16) for x in low], axis=0)
        return jnp.concatenate([low, jnp.concatenate([bias_terms] * count, axis=0)], axis=1)

    conv_b = jnp.concatenate([conv_b, conv_b], axis=1)
    blank = jnp.zeros((chan, 2 * edge), BF16)

    def slot(offset, first=0, count=1, of=1):
        low = (offset % 16 * of + first) * chan
        return slice(low, low + count * chan)

    def inside(p, offset):
        return not isinstance(p, int) or 0 <= p + offset < pairs

    def finish_pair(p, offset, conv):
        differ = (base[slot(offset), :] + conv) * keep
        grad_in[slot(offset), :] = differ.astype(BF16)
        bias_acc[...] += differ
        loss = 0.5 * jnp.sum(differ * differ, axis=0, keepdims=True)
        at = 2 * (p + offset)
        loss_out[pl.ds(at, 1), :] = loss[:, 0:edge]
        loss_out[pl.ds(at + 1, 1), :] = loss[:, edge : 2 * edge]

    def main(*accs):
        sums, grads, halos = accs[0:4], accs[4:6], accs[6:8]
        features_of = (accs[8:10], accs[10:14])
        stage, primed = [0, 0], [False, False]

        def halo_item(unit, p, offset, b, mask):
            halo = halos[unit]

            def push(at):
                pltpu.matmul_push_rhs(operand(shifted[b], mask[b]), at, unit)

            def go(at):
                pltpu.matmul_acc_lhs(halo, scaled(p + offset, 1), load_staged_rhs=at)
                value = jnp.maximum(pltpu.matmul_pop(halo), 0.0)
                hid[slot(offset, b, 1, 3), :] = value.astype(BF16)

            return push, go, None, 4

        def feature_item(unit, kind, p, offset, held, memo):
            def push(at):
                pltpu.matmul_push_rhs(wide[kind], at, unit)

            def go(at):
                if not memo:
                    memo.append(scaled(p + offset, 2))
                pltpu.matmul_acc_lhs(held[kind], memo[0], load_staged_rhs=at)

            def after():
                value, halo = (pltpu.matmul_pop(acc) for acc in held)
                for r in range(2):
                    own = value[r * chan : (r + 1) * chan]
                    base[slot(offset + r), :] = own + conv_b
                    own = jnp.maximum(own, 0.0)
                    ends_of = jnp.maximum(halo[r * chan : (r + 1) * chan], 0.0)
                    for b in range(3):
                        copy_of = own if b == 1 else moved(own, ends_of, b)
                        hid[slot(offset + r, b, 1, 3), :] = copy_of.astype(BF16)

            return push, go, after if kind == 1 else None, 8

        def conv_item(p, offset):
            taps = [a for a in range(3) if inside(p, offset + 1 - a)]

            def push(at):
                aim = blank
                if inside(p, offset):
                    aim = aims[pl.ds(pl.multiple_of((p + offset) * chan, chan), chan), :]
                right = jnp.concatenate([hid[slot(offset, 0, 3, 3), :], aim], axis=0)
                pltpu.matmul_push_rhs(right, at, 0)

            def go(at):
                for a in taps:
                    pltpu.matmul_acc_lhs(
                        sums[(offset + 1 - a) % 4],
                        weight_t[a * chan : (a + 1) * chan, :],
                        load_staged_rhs=at,
                    )
                    at = None

            def after():
                if 2 in taps:
                    finish_pair(p, offset - 1, pltpu.matmul_pop(sums[(offset - 1) % 4]))

            return push, go, after, 4 * len(taps)

        def grad_item(unit, p, offset):
            def push(at):
                right = [
                    grad_in[slot(offset + k), :] if inside(p, offset + k) else blank
                    for k in range(-2, 2)
                ]
                right = jnp.concatenate(right, axis=0)
                pltpu.matmul_push_rhs(right, at, unit, transpose=True)

            def go(at):
                left = hid[slot(offset, 0, 3, 3), :]
                pltpu.matmul_acc_lhs(grads[unit], left, load_staged_rhs=at)

            return push, go, None, 12

        def run(queues, follow=(None, None)):
            spent, at, waiting = [0, 0], [0, 0], []
            for unit in range(2):
                if queues[unit] and not primed[unit]:
                    queues[unit][0][0](stage[unit])
                primed[unit] = False
            while any(at[u] < len(queues[u]) for u in range(2)):
                unit = min(
                    (u for u in range(2) if at[u] < len(queues[u])), key=lambda u: spent[u]
                )
                queue, index = queues[unit], at[unit]
                _, go, after, cost = queue[index]
                while len(waiting) > 1:
                    waiting.pop(0)()
                go(stage[unit])
                stage[unit] = 1 - stage[unit]
                if index + 1 < len(queue):
                    queue[index + 1][0](stage[unit])
                at[unit] += 1
                spent[unit] += cost
                if after is not None:
                    waiting.append(after)
            for after in waiting:
                after()
            for unit in range(2):
                if follow[unit] is not None:
                    follow[unit][0](stage[unit])
                    primed[unit] = True

        def features(p, low, units=(1, 1)):
            items = []
            for half, unit in enumerate(units):
                memo, held = [], features_of[unit][2 * half * unit : 2 * half * unit + 2]
                items.append(
                    [feature_item(unit, k, p, low + 2 * half, held, memo) for k in range(2)]
                )
            return items

        def convs(p, low, high):
            return [conv_item(p, r) for r in range(low, high)]

        def turns(unit, p, *offsets):
            return [grad_item(unit, p, r) for r in offsets]

        def group(p, low):
            early, late = features(p, low)
            conv = convs(p, low - 4, low)
            shared = [turns(0, p, low - 10), turns(1, p, low - 10)]
            shared[1 if low % 8 == 0 else 0] = []
            run(
                (
                    turns(0, p, low - 12) + conv[0:2] + shared[0] + conv[2:4],
                    turns(1, p, low - 11) + early + shared[1] + turns(1, p, low - 9) + late,
                ),
                [turns(u, p, low - 8 + u)[0] for u in range(2)],
            )

        early, late = features(0, 0)
        first = convs(0, -1, 4)
        second = features(0, 4)
        tops = [halo_item(0, 0, -1, b, top) for b in range(3)]
        run((tops, early + late), (first[0], second[0][0]))
        third, fourth = convs(0, 4, 8), features(0, 8)
        run((first, second[0] + second[1]), (third[0], fourth[0][0]))
        fifth, sixth = convs(0, 8, 12), features(0, 12)
        run((third, fourth[0] + turns(1, 0, -1) + fourth[1]), (fifth[0], sixth[0][0]))
        run(
            (
                fifth[0:2] + turns(0, 0, 0) + fifth[2:4] + turns(0, 0, 2),
                sixth[0] + turns(1, 0, 1) + sixth[1] + turns(1, 0, 3),
            ),
            [turns(u, 0, 4 + u)[0] for u in range(2)],
        )

        def step(t, _):
            p = pl.multiple_of(t * 16, 16)
            for k in range(4):
                group(p, 4 * k)
            return 0

        lax.fori_loop(1, pairs // 16, step, 0)
        last = convs(pairs, -4, 1)
        run(
            (
                turns(0, pairs, -12) + last[0:2] + turns(0, pairs, -10) + last[2:4],
                turns(1, pairs, -11)
                + [halo_item(1, pairs, 0, b, bottom) for b in range(3)]
                + turns(1, pairs, -9, -8, -7),
            ),
            (last[4], turns(1, pairs, -6)[0]),
        )
        run((last[4:] + turns(0, pairs, -5, -4), turns(1, pairs, -6, -3)))
        run((turns(0, pairs, -2, 0), turns(1, pairs, -1)))
        total[...] = pltpu.matmul_pop(grads[0]) + pltpu.matmul_pop(grads[1])

    def accumulator(unit, rows_of):
        return pltpu.ACC(unit)((rows_of, 2 * edge), F32)

    pl.run_scoped(
        main,
        *[accumulator(0, chan)] * 4,
        *[accumulator(unit, 3 * chan) for unit in range(2)],
        *[accumulator(unit, chan) for unit in range(2)],
        *[accumulator(0, 2 * chan)] * 2,
        *[accumulator(1, 2 * chan)] * 4,
    )

    norm = 1.0 / (edge * edge)
    half = 3 * chan // 2
    rows = 3 * chan + half
    sums = total[...] * norm
    flat = jnp.concatenate(
        [
            sums[:, 2 * chan :],
            jnp.concatenate(
                [sums[0:half, chan : 2 * chan], sums[half:, chan : 2 * chan]], axis=1
            ),
        ],
        axis=0,
    )
    bias_sum = (bias_acc[:, 0:edge] + bias_acc[:, edge:]).T
    bias_sum = jnp.sum(bias_sum, axis=0, keepdims=True) * norm

    def largest(values):
        return jnp.max(jnp.max(jnp.abs(values), axis=0, keepdims=True), axis=1, keepdims=True)

    def exponent(values):
        return jnp.ceil(jnp.log(jnp.maximum(largest(values), 1e-30)) * LOG2E + 0.01)

    def coded(values, power):
        return values * (jnp.exp2(-power) * CODES)

    def side_rows(power, bias):
        bias_power = exponent(bias)
        high = jnp.round(coded(bias, bias_power))
        low = (coded(bias, bias_power) - high) * CODES
        return [
            jnp.concatenate([high, low], axis=1),
            jnp.broadcast_to(power, (1, 128)),
            jnp.broadcast_to(bias_power, (1, 128)),
        ]

    def packed(values, sides):
        blank = chunk - values.shape[0] - len(sides)
        values = jnp.concatenate([values, *sides, jnp.zeros((blank, 128), F32)], axis=0)
        return jnp.round(values).astype(jnp.int32).astype(jnp.int16)

    power = exponent(flat)
    codes = coded(flat, power)
    sides = side_rows(power, bias_sum)
    for index in range(n_own):
        have = min(max(rows - index * share, 0), share)
        values = [codes[index * share : index * share + have]] if have else []
        if have < share:
            values.append(jnp.zeros((share - have, 128), F32))
        part[index] = packed(jnp.concatenate(values, axis=0), sides)

    mine = me - first_own
    owner = (mine >= 0) & (mine < n_own)

    def remote(src, dst, send_sem, recv_sem, to):
        return pltpu.make_async_remote_copy(
            src_ref=src,
            dst_ref=dst,
            send_sem=send_sem,
            recv_sem=recv_sem,
            device_id=to,
            device_id_type=MESH,
        )

    square_of = n_col * n_rep
    owner_rows = n_own // square_of

    def scatter(d):
        level = d // square_of if isinstance(d, int) else lax.div(d, square_of)
        level = jnp.where(2 * row < n_row, owner_rows - 1 - level, level)
        index = level * square_of + lax.rem(me + d, square_of)

        @pl.when(first_own + index != me)
        def _():
            to = device(first_own + index)
            remote(part.at[index], reduced.at[me], rs_send, rs_recv, to).start()

    def give(to):
        remote(full.at[mine], full.at[mine], ag_send, ag_recv, to).start()

    def around(at):
        for c in range(n_col - 1, -1, -1):
            for r in range(n_rep - 1, -1, -1):
                yield {"row": at, "col": wrapped(col + c, n_col), "rep": wrapped(rep + r, n_rep)}

    def gather(k):
        for to in around(far(k)):
            give(to)

    loop(0, n_own, scatter)

    @pl.when(owner)
    def _():
        reduced[me] = part[mine]
        await_bytes(reduced.at[0 : n_all - 1], rs_recv)

        def decoded(r):
            value = reduced[r].astype(jnp.int32).astype(F32)
            return (
                value[0:share] * (jnp.exp2(value[share + 1 : share + 2]) / CODES),
                value[share : share + 1] * (jnp.exp2(value[share + 2 : share + 3]) / CODES),
            )

        if n_all <= 16:
            terms = [decoded(r) for r in range(n_all)]
            own, bias = (sum(x[k] for x in terms) for k in range(2))
        else:
            own, bias = lax.fori_loop(
                0,
                n_all,
                lambda r, x: tuple(a + b for a, b in zip(x, decoded(r))),
                (jnp.zeros((share, 128), F32), jnp.zeros((1, 128), F32)),
            )
        bias = bias[:, 0:chan] + bias[:, chan : 2 * chan] * (1.0 / CODES)
        power = exponent(own)
        full[mine] = packed(coded(own, power), side_rows(power, bias))
        loop(0, n_row - 1, gather)
        for to in list(around(row))[:-1]:
            give(to)
        if n_own > 1:
            await_bytes(full.at[0 : n_own - 1], ag_recv)
            await_bytes(part.at[0 : n_own - 1], rs_send)

    @pl.when(jnp.logical_not(owner))
    def _():
        await_bytes(full, ag_recv)
        await_bytes(part, rs_send)

    await_features(col_send, row_send, cedge_send, redge_send)

    @pl.when(owner)
    def _():
        await_bytes(reduced.at[0 : n_all - 1], ag_send)


def finish(share, loss, gathered, loss_hbm, conv_grad_hbm, bias_hbm, full, conv_grad_out, bias_out, sem):
    n_own = gathered.shape[0]
    loss_copy = pltpu.make_async_copy(loss, loss_hbm, sem.at[0])
    loss_copy.start()

    def decoded(r, low, high, power):
        value = gathered[r].astype(jnp.int32).astype(F32)
        return value[low:high] * (jnp.exp2(value[power : power + 1]) / CODES)

    for r in range(min(n_own, pl.cdiv(full.shape[0], share))):
        high = min(share, full.shape[0] - r * share)
        full[r * share : r * share + high, :] = decoded(r, 0, high, share + 1)

    chan = bias_out.shape[1]
    half = 3 * chan // 2
    rows = 3 * chan + half
    for b in range(3):
        low = b * chan
        conv_grad_out[1, b] = full[low : low + chan, 0:chan]
        conv_grad_out[0, b] = full[low : low + chan, chan : 2 * chan]
    low = 3 * chan
    conv_grad_out[2, 0] = full[low : low + chan, 0:chan]
    conv_grad_out[2, 1, 0 : half - chan] = full[low + chan : low + half, 0:chan]
    conv_grad_out[2, 1, half - chan :] = full[low : low + 2 * chan - half, chan : 2 * chan]
    conv_grad_out[2, 2] = full[low + 2 * chan - half : low + half, chan : 2 * chan]
    terms = decoded(0, share, share + 1, share + 2)
    bias_out[...] = terms[:, 0:chan] + terms[:, chan : 2 * chan] * (1.0 / CODES)
    grad_copy = pltpu.make_async_copy(conv_grad_out, conv_grad_hbm, sem.at[1])
    bias_copy = pltpu.make_async_copy(bias_out, bias_hbm, sem.at[2])
    grad_copy.start()
    bias_copy.start()
    loss_copy.wait()
    grad_copy.wait()
    bias_copy.wait()


def solution(mesh):
    n_row, n_col, n_rep = (mesh.shape[axis] for axis in ("row", "col", "rep"))
    n_all = n_row * n_col * n_rep

    def per_device(
        emb_row,
        emb_col,
        proj_row,
        proj_col,
        pair_out,
        pair_bias,
        conv_weight,
        conv_bias,
        target,
        kept_tiles,
    ):
        chan, edge = target.shape[0], target.shape[1]
        rank = pair_out.shape[0]
        pairs = edge // 2
        used = 3 * chan + 3 * chan // 2
        inner = n_row // 2 if n_row >= 4 else n_row
        n_own = inner * n_col * n_rep
        first_own = (n_row - inner) // 2 * n_col * n_rep
        share = pl.cdiv(used, n_own)
        chunk = 8 * pl.cdiv(share + 3, 8)

        def window(width, count):
            return window_of(proj_row.shape[0], width, 0, count)[1]

        dma = pltpu.SemaphoreType.DMA
        vmem = pl.BlockSpec(memory_space=pltpu.VMEM)
        hbm = pl.BlockSpec(memory_space=pltpu.HBM)
        results = pl.pallas_call(
            functools.partial(
                kernel, (n_row, n_col, n_rep, edge, chan, n_own, first_own, share, chunk)
            ),
            out_shape=(
                pltpu.VMEM((edge, edge), F32),
                pltpu.VMEM((n_own, chunk, 128), jnp.int16),
            ),
            in_specs=[hbm] * 9 + [pl.BlockSpec(memory_space=pltpu.SMEM)],
            out_specs=(vmem,) * 2,
            scratch_shapes=[
                pltpu.VMEM(emb_row.shape, BF16),
                pltpu.VMEM(emb_col.shape[::-1], BF16),
                pltpu.VMEM((rank, window(emb_row.shape[1], n_col)), BF16),
                pltpu.VMEM((rank, window(emb_col.shape[1], n_row)), BF16),
                pltpu.VMEM(conv_weight.shape, BF16),
                pltpu.VMEM(pair_out.shape, BF16),
                pltpu.VMEM((1, chan), F32),
                pltpu.VMEM((1, chan), F32),
                dma((8,)),
                pltpu.VMEM((2, 2, 2 * rank), F32),
                pltpu.VMEM((2, 1, 2 * rank), F32),
                pltpu.VMEM((n_col, rank + 16, edge), BF16),
                pltpu.VMEM((2, n_col, 2, 2 * rank), F32),
                pltpu.VMEM((n_row, rank, edge), BF16),
                pltpu.VMEM((2, n_row, 1, 2 * rank), F32),
                pltpu.VMEM((edge + 16, rank), F32),
                pltpu.VMEM((edge + 16, rank), F32),
                pltpu.VMEM((pairs + 8, 2 * rank), F32),
                pltpu.VMEM((256, 256), BF16),
                pltpu.VMEM((2, 2 * edge, 2 * edge), BF16),
                pltpu.VMEM((3 * chan, 4 * chan), BF16),
                pltpu.VMEM((chan, edge, edge), BF16),
                pltpu.VMEM((pairs * chan, 2 * edge), BF16),
                pltpu.VMEM((16 * 3 * chan, 2 * edge), BF16),
                pltpu.VMEM((16 * chan, 2 * edge), F32),
                pltpu.VMEM((16 * chan, 2 * edge), BF16),
                pltpu.VMEM((3 * chan, 3 * chan), F32),
                pltpu.VMEM((3 * chan, 4 * chan), F32),
                pltpu.VMEM((chan, 2 * edge), F32),
                pltpu.VMEM((n_own, chunk, 128), jnp.int16),
                pltpu.VMEM((n_all, chunk, 128), jnp.int16),
                *[pltpu.SemaphoreType.DMA] * 13,
            ],
            compiler_params=pltpu.CompilerParams(collective_id=0, has_side_effects=True),
            name="pair_step",
        )(
            emb_row,
            emb_col.T,
            proj_row.T,
            proj_col.T,
            pair_out,
            pair_bias.reshape(1, chan),
            conv_weight,
            conv_bias.reshape(1, chan),
            target,
            kept_tiles,
        )
        loss, grads, bias = pl.pallas_call(
            functools.partial(finish, share),
            out_shape=(
                jax.ShapeDtypeStruct((edge, edge), F32),
                jax.ShapeDtypeStruct((3, 3, chan, chan), F32),
                jax.ShapeDtypeStruct((1, chan), F32),
            ),
            in_specs=[vmem] * 2,
            out_specs=(hbm,) * 3,
            scratch_shapes=[
                pltpu.VMEM((used, 128), F32),
                pltpu.VMEM((3, 3, chan, chan), F32),
                pltpu.VMEM((1, chan), F32),
                dma((3,)),
            ],
            name="finish",
        )(
            *(pltpu.with_memory_space_constraint(x, pltpu.VMEM) for x in results)
        )
        return loss, grads, bias.reshape(chan)

    in_specs = (
        P(("grp", "row", "rep"), "col"),
        P(("grp", "col"), "row"),
        P(),
        P(),
        P(),
        P(),
        P(),
        P(),
        P(None, ("grp", "row", "rep"), "col"),
        P(("grp", "row", "rep"), "col"),
    )
    out_specs = (P(("grp", "row", "rep"), "col"), P("grp", None, None, None), P("grp"))
    return jax.shard_map(
        per_device, mesh=mesh, in_specs=in_specs, out_specs=out_specs, check_vma=False
    )
```

```python
import functools

import jax
import jax.numpy as jnp
from jax import lax
from jax.experimental import pallas as pl
from jax.experimental.pallas import tpu as pltpu
from jax.sharding import PartitionSpec as P

MESH = pl.DeviceIdType.MESH
F32 = jnp.float32
BF16 = jnp.bfloat16
CODES = 32000.0
LOG2E = 1.4426950408889634


def loop(low, high, body):
    if high - low <= 16:
        for d in range(low, high):
            body(d)
    else:
        lax.fori_loop(low, high, lambda d, _: (body(d), 0)[1], 0)


def window_of(everything, width, index, count):
    if width % 128 == 0:
        return index * width, width, 0
    offset = max(i * width % 128 for i in range(count))
    window = min(-(-(offset + width) // 128) * 128, everything)
    tile = lax.div(index * width, 128)
    if any(i * width // 128 * 128 + window > everything for i in range(count)):
        tile = jnp.minimum(tile, (everything - window) // 128)
    return tile * 128, window, index * width - tile * 128


def columns(ref, width, shift):
    window = ref.shape[1]
    if width % 128 == 0:
        return ref[...]
    value = pltpu.roll(ref[...].astype(F32), lax.rem(window - shift, window), 1)
    lane = lax.broadcasted_iota(jnp.int32, value.shape, 1)
    return jnp.where(lane < width, value, 0.0).astype(BF16)


def padded(value, square):
    if all(have == 256 or have % 128 == 0 for have in value.shape):
        for axis in range(2):
            if value.shape[axis] < 256:
                blank = list(value.shape)
                blank[axis] = 256 - blank[axis]
                value = jnp.concatenate([value, jnp.zeros(blank, BF16)], axis=axis)
        return value
    square[...] = jnp.zeros_like(square)
    square[0 : value.shape[0], 0 : value.shape[1]] = value
    return square[...]


def wide_tile(value, low):
    value = value[:, low : low + 256]
    if value.shape[1] < 256:
        blank = jnp.zeros((value.shape[0], 256 - value.shape[1]), BF16)
        value = jnp.concatenate([value, blank], axis=1)
    return value


def kernel(
    sizes,
    emb_row_hbm,
    emb_col_hbm,
    proj_row_hbm,
    proj_col_hbm,
    pair_out_hbm,
    pair_bias_hbm,
    conv_weight_hbm,
    conv_bias_hbm,
    target,
    kept,
    loss_out,
    full,
    emb_row,
    emb_col,
    proj_row,
    proj_col,
    conv_weight,
    pair_out,
    pair_bias,
    conv_bias,
    in_sem,
    rowtail,
    coltail,
    rowbuf,
    rowedge,
    colbuf,
    coledge,
    row_feat,
    col_wide,
    feat_pairs,
    square,
    wide,
    weight_t,
    target_in,
    aims,
    hid,
    base,
    grad_in,
    weight_f,
    total,
    bias_acc,
    part,
    reduced,
    target_sem,
    row_send,
    row_recv,
    redge_send,
    redge_recv,
    col_send,
    col_recv,
    cedge_send,
    cedge_recv,
    rs_send,
    rs_recv,
    ag_send,
    ag_recv,
):
    n_row, n_col, n_rep, edge, chan, n_own, first_own, share, chunk = sizes
    n_all = n_row * n_col * n_rep
    pairs = edge // 2
    row, col, rep = lax.axis_index("row"), lax.axis_index("col"), lax.axis_index("rep")
    line = row * n_rep + rep
    n_line = n_row * n_rep
    me = line * n_col + col

    def device(index):
        across = lax.rem(index, n_col)
        along = lax.div(index, n_col)
        return {"row": lax.div(along, n_rep), "rep": lax.rem(along, n_rep), "col": across}

    def wrapped(index, count):
        return jnp.where(index >= count, index - count, index)

    def far(k):
        down, up = n_row - 1 - k, k
        down = down - (down <= row).astype(jnp.int32)
        up = up + (up >= row).astype(jnp.int32)
        return jnp.where(2 * row < n_row, down, up)

    def await_bytes(ref, sem):
        pltpu.make_async_copy(ref, ref, sem).wait()

    col_width, row_width = emb_col.shape[0], emb_row.shape[1]
    everything = proj_col_hbm.shape[1]
    col_low, col_window, col_shift = window_of(everything, col_width, row, n_row)
    row_low, row_window, row_shift = window_of(everything, row_width, col, n_col)

    def lanes(low, window):
        return pl.ds(pl.multiple_of(low, 128), window)

    inputs = [
        pltpu.make_async_copy(src, dst, in_sem.at[i])
        for i, (src, dst) in enumerate(
            (
                (emb_col_hbm, emb_col),
                (proj_col_hbm.at[:, lanes(col_low, col_window)], proj_col),
                (emb_row_hbm, emb_row),
                (proj_row_hbm.at[:, lanes(row_low, row_window)], proj_row),
                (conv_weight_hbm, conv_weight),
                (pair_out_hbm, pair_out),
                (pair_bias_hbm, pair_bias),
                (conv_bias_hbm, conv_bias),
            )
        )
    ]
    for copy in inputs:
        copy.start()
    barrier = pltpu.get_barrier_semaphore()

    def greet(to):
        pl.semaphore_signal(barrier, inc=1, device_id=to, device_id_type=MESH)

    if n_all <= 16:
        for k in range(n_row):
            for c in range(n_col - 1, -1, -1):
                for r in range(n_rep - 1, -1, -1):
                    if k < n_row - 1 or c + r > 0:
                        greet(
                            {
                                "row": far(k) if k < n_row - 1 else row,
                                "col": wrapped(col + c, n_col),
                                "rep": wrapped(rep + r, n_rep),
                            }
                        )
    else:
        loop(1, n_all, lambda d: greet(device(lax.rem(me + d, n_all))))


    def rounded(x):
        return x.astype(BF16).astype(F32)

    rank = proj_row.shape[0]
    ends = ((edge - 2, edge - 1), (0, 1))
    fetch = pltpu.make_async_copy(target, target_in, target_sem)

    def pair_row(values, at):
        return jnp.concatenate([values[r : r + 1] for r in at], axis=1)

    def row_copy(d, src):
        return pltpu.make_async_remote_copy(
            src_ref=rowbuf.at[src],
            dst_ref=rowbuf.at[src],
            send_sem=row_send,
            recv_sem=row_recv,
            device_id={"col": lax.rem(col + d, n_col)},
            device_id_type=MESH,
        )

    def redge_copy(side, d, src):
        to = lax.rem(line + (1 if side == 0 else n_line - 1), n_line)
        return pltpu.make_async_remote_copy(
            src_ref=rowtail.at[side],
            dst_ref=rowedge.at[side, src],
            send_sem=redge_send,
            recv_sem=redge_recv,
            device_id={
                "row": lax.div(to, n_rep),
                "rep": lax.rem(to, n_rep),
                "col": lax.rem(col + d, n_col),
            },
            device_id_type=MESH,
        )

    def col_copy(to, src):
        return pltpu.make_async_remote_copy(
            src_ref=colbuf.at[src],
            dst_ref=colbuf.at[src],
            send_sem=col_send,
            recv_sem=col_recv,
            device_id={"row": to},
            device_id_type=MESH,
        )

    def cedge_copy(side, at, src):
        to = lax.rem(col + (1 if side == 0 else n_col - 1), n_col)
        return pltpu.make_async_remote_copy(
            src_ref=coltail.at[side],
            dst_ref=coledge.at[side, src],
            send_sem=cedge_send,
            recv_sem=cedge_recv,
            device_id={"row": at, "col": to},
            device_id_type=MESH,
        )

    for copy in inputs[0:2]:
        copy.wait()
    fetch.start()

    def project_col(col_sum):
        left = columns(proj_col, col_width, col_shift)
        for low in range(0, col_width, 256):
            right = padded(emb_col[low : min(low + 256, col_width), :], square)
            pltpu.matmul_push_rhs(right, 0, 0)
            pltpu.matmul_acc_lhs(col_sum, wide_tile(left, low), load_staged_rhs=0)
        return pltpu.matmul_pop(col_sum)[:, 0:edge]

    def project_row(row_sum):
        left = columns(proj_row, row_width, row_shift)
        for low in range(0, row_width, 256):
            right = padded(emb_row[:, low : min(low + 256, row_width)], square)
            pltpu.matmul_push_rhs(right, 0, 1, transpose=True)
            pltpu.matmul_acc_lhs(row_sum, wide_tile(left, low), load_staged_rhs=0)
        return pltpu.matmul_pop(row_sum)[:, 0:edge]

    part_col = pl.run_scoped(project_col, pltpu.ACC(0)((rank, 256), F32))
    colbuf[row] = part_col.astype(BF16)
    turned = rounded(part_col).T
    for side in range(2):
        coltail[side] = pair_row(turned, ends[side])
    for copy in inputs[2:4]:
        copy.wait()
    part_row = pl.run_scoped(project_row, pltpu.ACC(1)((rank, 256), F32))
    keep = kept[0, 0].astype(F32)
    rowbuf[col, 0:rank, :] = part_row.astype(BF16)
    rowbuf[col, rank:, :] = jnp.full((16, edge), keep, F32).astype(BF16)
    turned = rounded(part_row).T
    for side in range(2):
        rowtail[side, 0:1] = pair_row(turned, ends[side])
        rowtail[side, 1:2] = jnp.full((1, 2 * rank), keep, F32)
    pl.semaphore_wait(barrier, n_all - 1)

    def send_col(k):
        to = far(k)
        col_copy(to, row).start()
        for side in range(2):
            cedge_copy(side, to, row).start()

    loop(0, n_row - 1, send_col)
    for side in range(2):
        cedge_copy(side, row, row).start()
    loop(1, n_col, lambda d: row_copy(d, col).start())
    for side in range(2):
        loop(0, n_col, lambda d: redge_copy(side, d, col).start())

    def await_features(col_sem, row_sem, cedge_sem, redge_sem):
        await_bytes(coledge, cedge_sem)
        if n_row > 1:
            await_bytes(colbuf.at[0 : n_row - 1], col_sem)
        await_bytes(rowedge, redge_sem)
        if n_col > 1:
            await_bytes(rowbuf.at[0 : n_col - 1], row_sem)

    fetch.wait()
    for copy in inputs[4:]:
        copy.wait()

    def lay(i, _):
        for low in range(0, chan, 16):
            block = target_in[low : low + 16, pl.ds(pl.multiple_of(i * 16, 16), 16), :]
            block = jnp.swapaxes(block.astype(F32), 0, 1)
            for r in range(16):
                start = pl.multiple_of((i * 8 + r // 2) * chan + low, 16)
                lanes = slice(r % 2 * edge, (r % 2 + 1) * edge)
                aims[pl.ds(start, 16), lanes] = block[r].astype(BF16)
        return 0

    lax.fori_loop(0, edge // 16, lay, 0)
    for a in range(3):
        for b in range(3):
            weight_f[b * chan : (b + 1) * chan, a * chan : (a + 1) * chan] = conv_weight[
                a, b
            ].astype(F32)
    turned = weight_f[...].T
    eye = lax.broadcasted_iota(jnp.int32, (chan, chan), 0) == lax.broadcasted_iota(
        jnp.int32, (chan, chan), 1
    )
    none = jnp.zeros((chan, chan), F32)
    minus = jnp.concatenate([none, jnp.where(eye, -1.0, 0.0), none], axis=0)
    weight_t[...] = jnp.concatenate([turned, minus], axis=1).astype(BF16)
    out_t = pair_out[...].astype(F32).T
    out_t = jnp.concatenate([out_t, out_t], axis=1)
    pair_b = jnp.broadcast_to(pair_bias[...], (128, chan)).T
    conv_b = jnp.broadcast_to(conv_bias[...], (128, chan)).T
    term = lax.broadcasted_iota(jnp.int32, (chan, 128), 1)
    second = pair_b - rounded(pair_b)
    third = second - rounded(second)
    bias_terms = jnp.where(
        term == 0,
        pair_b,
        jnp.where(term == 1, second, jnp.where(term == 2, third, 0.0)),
    ).astype(BF16)
    bias_acc[...] = jnp.zeros_like(bias_acc)

    await_features(col_recv, row_recv, cedge_recv, redge_recv)

    def summed(terms):
        return sum(x.astype(F32) for x in terms)

    def unpack(target, values, low):
        for r in range(2):
            target[low + r : low + r + 1, :] = values[:, r * rank : (r + 1) * rank]

    for side, low in ((0, 6), (1, edge + 8)):
        edge_sum = rounded(summed(rowedge[side, c, 0:1, :] for c in range(n_col)))
        unpack(row_feat, edge_sum, low)
        unpack(col_wide, summed(coledge[side, r] for r in range(n_row)), low)
    row_feat[8 : edge + 8, :] = rounded(summed(rowbuf[c, 0:rank, :] for c in range(n_col))).T
    col_wide[8 : edge + 8, :] = summed(colbuf[r] for r in range(n_row)).T
    feat_pairs[0 : pairs + 2, :] = jnp.concatenate(
        [row_feat[pl.ds(6 + r, pairs + 2, stride=2), :] for r in range(2)], axis=1
    )

    lane = lax.broadcasted_iota(jnp.int32, (1, edge), 1)
    before, after = lax.rem(col + n_col - 1, n_col), lax.rem(col + 1, n_col)
    has_before = (col > 0).astype(F32)
    has_after = (col < n_col - 1).astype(F32)

    def masks(get, valid):
        here, left, right = (
            jnp.broadcast_to(get(c), (1, edge)) * scale
            for c, scale in ((col, valid), (before, valid * has_before), (after, valid * has_after))
        )
        return (jnp.where(lane < 2, left, here), here, jnp.where(lane >= edge - 2, right, here))

    top = masks(lambda c: rowedge[0, c, 1:2, 0:1], (line > 0).astype(F32))
    middle = masks(lambda c: rowbuf[c, rank:, 0:1].astype(F32)[0:1], jnp.float32(1))
    bottom = masks(lambda c: rowedge[1, c, 1:2, 0:1], (line < n_line - 1).astype(F32))

    shifted = [col_wide[6 + 2 * b : 6 + 2 * b + edge, :].T for b in range(3)]
    first_rows = lax.broadcasted_iota(jnp.int32, (2 * edge - 2 * rank, 2 * edge), 0) < 3

    def operand(value, mask):
        value = value * mask
        blank = jnp.zeros_like(value)
        ones = jnp.where(first_rows, jnp.concatenate([mask, mask], axis=1), 0.0)
        return jnp.concatenate(
            [
                jnp.concatenate([value, blank], axis=1),
                jnp.concatenate([blank, value], axis=1),
                ones,
            ],
            axis=0,
        ).astype(BF16)

    def outer(left, right):
        return jnp.where(lane < 2, left, jnp.where(lane >= edge - 2, right, 0.0))

    wide[0] = operand(shifted[1], middle[1])
    wide[1] = operand(outer(shifted[0], shifted[2]), outer(middle[0], middle[2]))
    lane_wide = lax.broadcasted_iota(jnp.int32, (chan, edge), 1)

    def moved(value, halo, b):
        halves = []
        for r in range(2):
            lanes = slice(r * edge, (r + 1) * edge)
            turned = pltpu.roll(value[:, lanes], 2 if b == 0 else edge - 2, 1)
            at_end = lane_wide < 2 if b == 0 else lane_wide >= edge - 2
            halves.append(jnp.where(at_end, halo[:, lanes], turned))
        return jnp.concatenate(halves, axis=1)

    def scaled(p, count):
        low = (out_t * feat_pairs[pl.ds(p + 1 + r, 1), :] for r in range(count))
        low = jnp.concatenate([x.astype(BF16) for x in low], axis=0)
        return jnp.concatenate([low, jnp.concatenate([bias_terms] * count, axis=0)], axis=1)

    conv_b = jnp.concatenate([conv_b, conv_b], axis=1)
    blank = jnp.zeros((chan, 2 * edge), BF16)

    def slot(offset, first=0, count=1, of=1):
        low = (offset % 16 * of + first) * chan
        return slice(low, low + count * chan)

    def inside(p, offset):
        return not isinstance(p, int) or 0 <= p + offset < pairs

    def finish_pair(p, offset, conv):
        differ = (base[slot(offset), :] + conv) * keep
        grad_in[slot(offset), :] = differ.astype(BF16)
        bias_acc[...] += differ
        loss = 0.5 * jnp.sum(differ * differ, axis=0, keepdims=True)
        at = 2 * (p + offset)
        loss_out[pl.ds(at, 1), :] = loss[:, 0:edge]
        loss_out[pl.ds(at + 1, 1), :] = loss[:, edge : 2 * edge]

    def main(*accs):
        sums, grads, halos = accs[0:4], accs[4:6], accs[6:8]
        features_of = (accs[8:10], accs[10:14])
        stage, primed = [0, 0], [False, False]

        def halo_item(unit, p, offset, b, mask):
            halo = halos[unit]

            def push(at):
                pltpu.matmul_push_rhs(operand(shifted[b], mask[b]), at, unit)

            def go(at):
                pltpu.matmul_acc_lhs(halo, scaled(p + offset, 1), load_staged_rhs=at)
                value = jnp.maximum(pltpu.matmul_pop(halo), 0.0)
                hid[slot(offset, b, 1, 3), :] = value.astype(BF16)

            return push, go, None, 4

        def feature_item(unit, kind, p, offset, held, memo):
            def push(at):
                pltpu.matmul_push_rhs(wide[kind], at, unit)

            def go(at):
                if not memo:
                    memo.append(scaled(p + offset, 2))
                pltpu.matmul_acc_lhs(held[kind], memo[0], load_staged_rhs=at)

            def after():
                value, halo = (pltpu.matmul_pop(acc) for acc in held)
                for r in range(2):
                    own = value[r * chan : (r + 1) * chan]
                    base[slot(offset + r), :] = own + conv_b
                    own = jnp.maximum(own, 0.0)
                    ends_of = jnp.maximum(halo[r * chan : (r + 1) * chan], 0.0)
                    for b in range(3):
                        copy_of = own if b == 1 else moved(own, ends_of, b)
                        hid[slot(offset + r, b, 1, 3), :] = copy_of.astype(BF16)

            return push, go, after if kind == 1 else None, 8

        def conv_item(p, offset):
            taps = [a for a in range(3) if inside(p, offset + 1 - a)]

            def push(at):
                aim = blank
                if inside(p, offset):
                    aim = aims[pl.ds(pl.multiple_of((p + offset) * chan, chan), chan), :]
                right = jnp.concatenate([hid[slot(offset, 0, 3, 3), :], aim], axis=0)
                pltpu.matmul_push_rhs(right, at, 0)

            def go(at):
                for a in taps:
                    pltpu.matmul_acc_lhs(
                        sums[(offset + 1 - a) % 4],
                        weight_t[a * chan : (a + 1) * chan, :],
                        load_staged_rhs=at,
                    )
                    at = None

            def after():
                if 2 in taps:
                    finish_pair(p, offset - 1, pltpu.matmul_pop(sums[(offset - 1) % 4]))

            return push, go, after, 4 * len(taps)

        def grad_item(unit, p, offset):
            def push(at):
                right = [
                    grad_in[slot(offset + k), :] if inside(p, offset + k) else blank
                    for k in range(-2, 2)
                ]
                right = jnp.concatenate(right, axis=0)
                pltpu.matmul_push_rhs(right, at, unit, transpose=True)

            def go(at):
                left = hid[slot(offset, 0, 3, 3), :]
                pltpu.matmul_acc_lhs(grads[unit], left, load_staged_rhs=at)

            return push, go, None, 12

        def run(queues, follow=(None, None)):
            spent, at, waiting = [0, 0], [0, 0], []
            for unit in range(2):
                if queues[unit] and not primed[unit]:
                    queues[unit][0][0](stage[unit])
                primed[unit] = False
            while any(at[u] < len(queues[u]) for u in range(2)):
                unit = min(
                    (u for u in range(2) if at[u] < len(queues[u])), key=lambda u: spent[u]
                )
                queue, index = queues[unit], at[unit]
                _, go, after, cost = queue[index]
                while len(waiting) > 1:
                    waiting.pop(0)()
                go(stage[unit])
                stage[unit] = 1 - stage[unit]
                if index + 1 < len(queue):
                    queue[index + 1][0](stage[unit])
                at[unit] += 1
                spent[unit] += cost
                if after is not None:
                    waiting.append(after)
            for after in waiting:
                after()
            for unit in range(2):
                if follow[unit] is not None:
                    follow[unit][0](stage[unit])
                    primed[unit] = True

        def features(p, low, units=(1, 1)):
            items = []
            for half, unit in enumerate(units):
                memo, held = [], features_of[unit][2 * half * unit : 2 * half * unit + 2]
                items.append(
                    [feature_item(unit, k, p, low + 2 * half, held, memo) for k in range(2)]
                )
            return items

        def convs(p, low, high):
            return [conv_item(p, r) for r in range(low, high)]

        def turns(unit, p, *offsets):
            return [grad_item(unit, p, r) for r in offsets]

        def group(p, low):
            early, late = features(p, low)
            conv = convs(p, low - 4, low)
            shared = [turns(0, p, low - 10), turns(1, p, low - 10)]
            shared[1 if low % 8 == 0 else 0] = []
            run(
                (
                    turns(0, p, low - 12) + conv[0:2] + shared[0] + conv[2:4],
                    turns(1, p, low - 11) + early + shared[1] + turns(1, p, low - 9) + late,
                ),
                [turns(u, p, low - 8 + u)[0] for u in range(2)],
            )

        early, late = features(0, 0)
        first = convs(0, -1, 4)
        second = features(0, 4)
        tops = [halo_item(0, 0, -1, b, top) for b in range(3)]
        run((tops, early + late), (first[0], second[0][0]))
        third, fourth = convs(0, 4, 8), features(0, 8)
        run((first, second[0] + second[1]), (third[0], fourth[0][0]))
        fifth, sixth = convs(0, 8, 12), features(0, 12)
        run((third, fourth[0] + turns(1, 0, -1) + fourth[1]), (fifth[0], sixth[0][0]))
        run(
            (
                fifth[0:2] + turns(0, 0, 0) + fifth[2:4] + turns(0, 0, 2),
                sixth[0] + turns(1, 0, 1) + sixth[1] + turns(1, 0, 3),
            ),
            [turns(u, 0, 4 + u)[0] for u in range(2)],
        )

        def step(t, _):
            p = pl.multiple_of(t * 16, 16)
            for k in range(4):
                group(p, 4 * k)
            return 0

        lax.fori_loop(1, pairs // 16, step, 0)
        last = convs(pairs, -4, 1)
        run(
            (
                turns(0, pairs, -12) + last[0:2] + turns(0, pairs, -10) + last[2:4],
                turns(1, pairs, -11)
                + [halo_item(1, pairs, 0, b, bottom) for b in range(3)]
                + turns(1, pairs, -9, -8, -7),
            ),
            (last[4], turns(1, pairs, -6)[0]),
        )
        run((last[4:] + turns(0, pairs, -5, -4), turns(1, pairs, -6, -3)))
        run((turns(0, pairs, -2, 0), turns(1, pairs, -1)))
        total[...] = pltpu.matmul_pop(grads[0]) + pltpu.matmul_pop(grads[1])

    def accumulator(unit, rows_of):
        return pltpu.ACC(unit)((rows_of, 2 * edge), F32)

    pl.run_scoped(
        main,
        *[accumulator(0, chan)] * 4,
        *[accumulator(unit, 3 * chan) for unit in range(2)],
        *[accumulator(unit, chan) for unit in range(2)],
        *[accumulator(0, 2 * chan)] * 2,
        *[accumulator(1, 2 * chan)] * 4,
    )

    norm = 1.0 / (edge * edge)
    half = 3 * chan // 2
    rows = 3 * chan + half
    sums = total[...] * norm
    flat = jnp.concatenate(
        [
            sums[:, 2 * chan :],
            jnp.concatenate(
                [sums[0:half, chan : 2 * chan], sums[half:, chan : 2 * chan]], axis=1
            ),
        ],
        axis=0,
    )
    bias_sum = (bias_acc[:, 0:edge] + bias_acc[:, edge:]).T
    bias_sum = jnp.sum(bias_sum, axis=0, keepdims=True) * norm

    def largest(values):
        return jnp.max(jnp.max(jnp.abs(values), axis=0, keepdims=True), axis=1, keepdims=True)

    def exponent(values):
        return jnp.ceil(jnp.log(jnp.maximum(largest(values), 1e-30)) * LOG2E + 0.01)

    def coded(values, power):
        return values * (jnp.exp2(-power) * CODES)

    def side_rows(power, bias):
        bias_power = exponent(bias)
        high = jnp.round(coded(bias, bias_power))
        low = (coded(bias, bias_power) - high) * CODES
        return [
            jnp.concatenate([high, low], axis=1),
            jnp.broadcast_to(power, (1, 128)),
            jnp.broadcast_to(bias_power, (1, 128)),
        ]

    def packed(values, sides):
        blank = chunk - values.shape[0] - len(sides)
        values = jnp.concatenate([values, *sides, jnp.zeros((blank, 128), F32)], axis=0)
        return jnp.round(values).astype(jnp.int32).astype(jnp.int16)

    power = exponent(flat)
    codes = coded(flat, power)
    sides = side_rows(power, bias_sum)
    for index in range(n_own):
        have = min(max(rows - index * share, 0), share)
        values = [codes[index * share : index * share + have]] if have else []
        if have < share:
            values.append(jnp.zeros((share - have, 128), F32))
        part[index] = packed(jnp.concatenate(values, axis=0), sides)

    mine = me - first_own
    owner = (mine >= 0) & (mine < n_own)

    def remote(src, dst, send_sem, recv_sem, to):
        return pltpu.make_async_remote_copy(
            src_ref=src,
            dst_ref=dst,
            send_sem=send_sem,
            recv_sem=recv_sem,
            device_id=to,
            device_id_type=MESH,
        )

    square_of = n_col * n_rep
    owner_rows = n_own // square_of

    def scatter(d):
        level = d // square_of if isinstance(d, int) else lax.div(d, square_of)
        level = jnp.where(2 * row < n_row, owner_rows - 1 - level, level)
        index = level * square_of + lax.rem(me + d, square_of)

        @pl.when(first_own + index != me)
        def _():
            to = device(first_own + index)
            remote(part.at[index], reduced.at[me], rs_send, rs_recv, to).start()

    def give(to):
        remote(full.at[mine], full.at[mine], ag_send, ag_recv, to).start()

    def around(at):
        for c in range(n_col - 1, -1, -1):
            for r in range(n_rep - 1, -1, -1):
                yield {"row": at, "col": wrapped(col + c, n_col), "rep": wrapped(rep + r, n_rep)}

    def gather(k):
        for to in around(far(k)):
            give(to)

    loop(0, n_own, scatter)

    @pl.when(owner)
    def _():
        reduced[me] = part[mine]
        await_bytes(reduced.at[0 : n_all - 1], rs_recv)

        def decoded(r):
            value = reduced[r].astype(jnp.int32).astype(F32)
            return (
                value[0:share] * (jnp.exp2(value[share + 1 : share + 2]) / CODES),
                value[share : share + 1] * (jnp.exp2(value[share + 2 : share + 3]) / CODES),
            )

        if n_all <= 16:
            terms = [decoded(r) for r in range(n_all)]
            own, bias = (sum(x[k] for x in terms) for k in range(2))
        else:
            own, bias = lax.fori_loop(
                0,
                n_all,
                lambda r, x: tuple(a + b for a, b in zip(x, decoded(r))),
                (jnp.zeros((share, 128), F32), jnp.zeros((1, 128), F32)),
            )
        bias = bias[:, 0:chan] + bias[:, chan : 2 * chan] * (1.0 / CODES)
        power = exponent(own)
        full[mine] = packed(coded(own, power), side_rows(power, bias))
        loop(0, n_row - 1, gather)
        for to in list(around(row))[:-1]:
            give(to)
        if n_own > 1:
            await_bytes(full.at[0 : n_own - 1], ag_recv)
            await_bytes(part.at[0 : n_own - 1], rs_send)

    @pl.when(jnp.logical_not(owner))
    def _():
        await_bytes(full, ag_recv)
        await_bytes(part, rs_send)

    await_features(col_send, row_send, cedge_send, redge_send)

    @pl.when(owner)
    def _():
        await_bytes(reduced.at[0 : n_all - 1], ag_send)


def finish(share, loss, gathered, loss_hbm, conv_grad_hbm, bias_hbm, full, conv_grad_out, bias_out, sem):
    n_own = gathered.shape[0]
    loss_copy = pltpu.make_async_copy(loss, loss_hbm, sem.at[0])
    loss_copy.start()
    grad_copies = [
        pltpu.make_async_copy(conv_grad_out.at[a], conv_grad_hbm.at[a], sem.at[2 + a])
        for a in range(3)
    ]

    def decoded(r, low, high, power):
        value = gathered[r].astype(jnp.int32).astype(F32)
        return value[low:high] * (jnp.exp2(value[power : power + 1]) / CODES)

    for r in range(min(n_own, pl.cdiv(full.shape[0], share))):
        high = min(share, full.shape[0] - r * share)
        full[r * share : r * share + high, :] = decoded(r, 0, high, share + 1)

    chan = bias_out.shape[1]
    half = 3 * chan // 2
    rows = 3 * chan + half
    for b in range(3):
        low = b * chan
        conv_grad_out[1, b] = full[low : low + chan, 0:chan]
    grad_copies[1].start()
    for b in range(3):
        low = b * chan
        conv_grad_out[0, b] = full[low : low + chan, chan : 2 * chan]
    grad_copies[0].start()
    low = 3 * chan
    conv_grad_out[2, 0] = full[low : low + chan, 0:chan]
    conv_grad_out[2, 1, 0 : half - chan] = full[low + chan : low + half, 0:chan]
    conv_grad_out[2, 1, half - chan :] = full[low : low + 2 * chan - half, chan : 2 * chan]
    conv_grad_out[2, 2] = full[low + 2 * chan - half : low + half, chan : 2 * chan]
    terms = decoded(0, share, share + 1, share + 2)
    bias_out[...] = terms[:, 0:chan] + terms[:, chan : 2 * chan] * (1.0 / CODES)
    bias_copy = pltpu.make_async_copy(bias_out, bias_hbm, sem.at[1])
    grad_copies[2].start()
    bias_copy.start()
    loss_copy.wait()
    for copy in grad_copies:
        copy.wait()
    bias_copy.wait()


def solution(mesh):
    n_row, n_col, n_rep = (mesh.shape[axis] for axis in ("row", "col", "rep"))
    n_all = n_row * n_col * n_rep

    def per_device(
        emb_row,
        emb_col,
        proj_row,
        proj_col,
        pair_out,
        pair_bias,
        conv_weight,
        conv_bias,
        target,
        kept_tiles,
    ):
        chan, edge = target.shape[0], target.shape[1]
        rank = pair_out.shape[0]
        pairs = edge // 2
        used = 3 * chan + 3 * chan // 2
        inner = n_row // 2 if n_row >= 4 else n_row
        n_own = inner * n_col * n_rep
        first_own = (n_row - inner) // 2 * n_col * n_rep
        share = pl.cdiv(used, n_own)
        chunk = 8 * pl.cdiv(share + 3, 8)

        def window(width, count):
            return window_of(proj_row.shape[0], width, 0, count)[1]

        dma = pltpu.SemaphoreType.DMA
        vmem = pl.BlockSpec(memory_space=pltpu.VMEM)
        hbm = pl.BlockSpec(memory_space=pltpu.HBM)
        results = pl.pallas_call(
            functools.partial(
                kernel, (n_row, n_col, n_rep, edge, chan, n_own, first_own, share, chunk)
            ),
            out_shape=(
                pltpu.VMEM((edge, edge), F32),
                pltpu.VMEM((n_own, chunk, 128), jnp.int16),
            ),
            in_specs=[hbm] * 9 + [pl.BlockSpec(memory_space=pltpu.SMEM)],
            out_specs=(vmem,) * 2,
            scratch_shapes=[
                pltpu.VMEM(emb_row.shape, BF16),
                pltpu.VMEM(emb_col.shape[::-1], BF16),
                pltpu.VMEM((rank, window(emb_row.shape[1], n_col)), BF16),
                pltpu.VMEM((rank, window(emb_col.shape[1], n_row)), BF16),
                pltpu.VMEM(conv_weight.shape, BF16),
                pltpu.VMEM(pair_out.shape, BF16),
                pltpu.VMEM((1, chan), F32),
                pltpu.VMEM((1, chan), F32),
                dma((8,)),
                pltpu.VMEM((2, 2, 2 * rank), F32),
                pltpu.VMEM((2, 1, 2 * rank), F32),
                pltpu.VMEM((n_col, rank + 16, edge), BF16),
                pltpu.VMEM((2, n_col, 2, 2 * rank), F32),
                pltpu.VMEM((n_row, rank, edge), BF16),
                pltpu.VMEM((2, n_row, 1, 2 * rank), F32),
                pltpu.VMEM((edge + 16, rank), F32),
                pltpu.VMEM((edge + 16, rank), F32),
                pltpu.VMEM((pairs + 8, 2 * rank), F32),
                pltpu.VMEM((256, 256), BF16),
                pltpu.VMEM((2, 2 * edge, 2 * edge), BF16),
                pltpu.VMEM((3 * chan, 4 * chan), BF16),
                pltpu.VMEM((chan, edge, edge), BF16),
                pltpu.VMEM((pairs * chan, 2 * edge), BF16),
                pltpu.VMEM((16 * 3 * chan, 2 * edge), BF16),
                pltpu.VMEM((16 * chan, 2 * edge), F32),
                pltpu.VMEM((16 * chan, 2 * edge), BF16),
                pltpu.VMEM((3 * chan, 3 * chan), F32),
                pltpu.VMEM((3 * chan, 4 * chan), F32),
                pltpu.VMEM((chan, 2 * edge), F32),
                pltpu.VMEM((n_own, chunk, 128), jnp.int16),
                pltpu.VMEM((n_all, chunk, 128), jnp.int16),
                *[pltpu.SemaphoreType.DMA] * 13,
            ],
            compiler_params=pltpu.CompilerParams(collective_id=0, has_side_effects=True),
            name="pair_step",
        )(
            emb_row,
            emb_col.T,
            proj_row.T,
            proj_col.T,
            pair_out,
            pair_bias.reshape(1, chan),
            conv_weight,
            conv_bias.reshape(1, chan),
            target,
            kept_tiles,
        )
        loss, grads, bias = pl.pallas_call(
            functools.partial(finish, share),
            out_shape=(
                jax.ShapeDtypeStruct((edge, edge), F32),
                jax.ShapeDtypeStruct((3, 3, chan, chan), F32),
                jax.ShapeDtypeStruct((1, chan), F32),
            ),
            in_specs=[vmem] * 2,
            out_specs=(hbm,) * 3,
            scratch_shapes=[
                pltpu.VMEM((used, 128), F32),
                pltpu.VMEM((3, 3, chan, chan), F32),
                pltpu.VMEM((1, chan), F32),
                dma((5,)),
            ],
            name="finish",
        )(
            *(pltpu.with_memory_space_constraint(x, pltpu.VMEM) for x in results)
        )
        return loss, grads, bias.reshape(chan)

    in_specs = (
        P(("grp", "row", "rep"), "col"),
        P(("grp", "col"), "row"),
        P(),
        P(),
        P(),
        P(),
        P(),
        P(),
        P(None, ("grp", "row", "rep"), "col"),
        P(("grp", "row", "rep"), "col"),
    )
    out_specs = (P(("grp", "row", "rep"), "col"), P("grp", None, None, None), P("grp"))
    return jax.shard_map(
        per_device, mesh=mesh, in_specs=in_specs, out_specs=out_specs, check_vma=False
    )
```
